256 devices in a mesh: ctx: 32 (over y, x, core), head: 8 (over z).
Axes of the slice: x: 4, y: 4, z: 8, core: 2. Of those that a mesh axis runs over, the one named last changes fastest.
Arguments:
- x_raw: bfloat16 [8192, 8192], P('ctx', 'head'), may hold values from -6 to 6
- bc_raw: bfloat16 [8192, 256], P('ctx'), may hold values from -6 to 6
- dt_raw: float32 [8192, 128], P('ctx', 'head')
- conv_x: float32 [4, 8192], P(None, 'head'), may hold values from -3 to 3
- conv_bc: float32 [4, 256], replicated, may hold values from -1.5 to 1.5
- a_log: float32 [128], P('head')
- dt_bias: float32 [128], P('head'), may hold values from -5 to -3
- skip_weight: float32 [128], P('head'), may hold values from 0.5 to 1.5
- segment: int32 [8192], replicated, may hold values from 0 to 7, as said below
- grad_y: bfloat16 [8192, 8192], P('ctx', 'head'), may hold values from -6 to 6
Outputs:
- ssd_out: bfloat16 [8192, 8192], P('ctx', 'head')
- grad_x: bfloat16 [8192, 8192], P('ctx', 'head')
- grad_bc: float32 [8192, 256], P(('ctx', 'head'))
- grad_dt: float32 [8192, 128], P('ctx', 'head')
- grad_conv_x: float32 [4, 8192], P(None, 'head')
- grad_conv_bc: float32 [4, 256], replicated
- grad_heads: float32 [3, 128], P(None, 'head')
The draws below stay inside these ranges and needn't reach their ends.
Inputs may be any that keep to these rules, and one draw needn't show every extreme that they name: `segment`: ids of 8 packed documents: 0 at the first token, never falling, rising by at most one from a token to the next.
All inputs are finite; a program needn't handle non-finite values.
Results may differ from the reference program's by a relative error of at most 0.008.
Values may be sent and summed in bfloat16 or wider, within the bound.
No kernel may reach another device: no remote copies, remote signals or barrier semaphores. Data moves between devices by JAX's collectives and lax.ppermute only.
A program may use at most 192 MiB of HBM per device.

```python
import jax
import jax.numpy as jnp
from jax import lax

HEADS = 128
HEAD_DIM = 64
STATE = 128
CONV = 4
TOK_DEV = 256
WIDTH = 8192
TOKENS = 8192
DOCS = 8


def draw_a_log(key, part):
    pick_key, level_key = jax.random.split(key)
    slow_share = 0.5
    slow = jax.random.uniform(pick_key, (HEADS,), jnp.float32) < slow_share
    level = jax.random.uniform(level_key, (HEADS,), jnp.float32)
    slow_level = jnp.log(5.0 / TOKENS) + level * jnp.log(10.0)
    fast_level = jnp.log(0.5) + level * jnp.log(4.0)
    return jnp.where(slow, slow_level, fast_level).astype(jnp.float32)


def draw_dt_raw(key, part):
    windows = TOKENS // TOK_DEV
    noise_key, offset_key = jax.random.split(key)
    noise = 0.5 * jax.random.normal(noise_key, (windows, TOK_DEV, HEADS), jnp.float32)
    offset = jax.random.uniform(offset_key, (windows, 1, HEADS), jnp.float32, -0.7, 0.7)
    return (noise + offset).reshape(TOKENS, HEADS).astype(jnp.float32)


def draw_segment(key, part):
    order = jax.random.permutation(key, TOKENS - 1).astype(jnp.int32)
    positions = order[:DOCS - 1] + 1
    starts = jnp.zeros((TOKENS,), jnp.int32).at[positions].set(1)
    return jnp.cumsum(starts).astype(jnp.int32)


def levels(rng, extent, cuts, least, high):
    def one(position, parts):
        draws = jax.random.uniform(jax.random.fold_in(jax.random.fold_in(rng, 6), position), (parts,), jnp.float32, least / len(cuts), high / len(cuts))
        return jnp.repeat(jnp.exp(draws), extent[position] // parts).reshape((-1,) + (1,) * (len(extent) - position - 1))

    factor_of = one(*cuts[0])
    for cut in cuts[1:]:
        factor_of = factor_of * one(*cut)
    return factor_of


def normal_values(key, shape, scale, bound, pieces=(), dtype=jnp.bfloat16):
    entries = jax.random.normal(key, shape, jnp.float32) * scale
    if len(pieces) > 0:
        entries = levels(key, shape, pieces, -0.22, 0.18) * entries
    return jnp.clip(entries, min=-bound, max=bound).astype(dtype)


def setup_inputs(seed: int = 0) -> dict:
    splits = jax.random.split(jax.random.key(seed), 11)
    x_raw = normal_values(splits[0], (TOKENS, WIDTH), 1.0, 6.0, ((0, 32), (1, 8)))
    bc_raw = normal_values(splits[1], (TOKENS, 2 * STATE), 1.0, 6.0, ((0, 32),))
    dt_raw = draw_dt_raw(jax.random.fold_in(splits[10], 71), 0)
    conv_x = normal_values(splits[3], (CONV, WIDTH), CONV ** -0.5, 3.0, ((1, 8),), jnp.float32)
    conv_bc = normal_values(splits[4], (CONV, 2 * STATE), (4 * CONV) ** -0.5, 1.5, (), jnp.float32)
    a_log = draw_a_log(jax.random.fold_in(splits[10], 71), 0)
    dt_bias = jnp.clip(-5.0 + 2.0 * jax.random.uniform(splits[6], (HEADS,), jnp.float32) ** levels(splits[6], (HEADS,), ((0, 8),), -0.2, 0.2), -5.0, -3.0)
    skip_weight = jnp.clip(1.0 + 0.1 * jax.random.normal(splits[7], (HEADS,), jnp.float32), 0.5, 1.5)
    segment = draw_segment(jax.random.fold_in(splits[10], 71), 0)
    grad_y = normal_values(splits[9], (TOKENS, WIDTH), 1.0, 6.0, ((0, 32), (1, 8)))
    return {"x_raw": x_raw, "bc_raw": bc_raw, "dt_raw": dt_raw, "conv_x": conv_x, "conv_bc": conv_bc, "a_log": a_log, "dt_bias": dt_bias, "skip_weight": skip_weight, "segment": segment, "grad_y": grad_y}


def round_values(values):
    low = lax.optimization_barrier(lax.stop_gradient(values).astype(jnp.bfloat16))
    return values + (low.astype(jnp.float32) - lax.stop_gradient(values))

def conv_activate(extended, weight, seg_ext):
    tap_count = weight.shape[0]
    row_count = extended.shape[0] - tap_count + 1
    target = seg_ext[tap_count - 1:]
    total = jnp.zeros((row_count, extended.shape[1]), jnp.float32)
    for tap_index in range(tap_count):
        match = (seg_ext[tap_index:tap_index + row_count] == target)[:, None]
        total = total + jnp.where(match, extended[tap_index:tap_index + row_count] * weight[tap_index][None, :], 0.0)
    return jax.nn.silu(total)

def window_parts(x_head, dt_head, rate, scores, b_vals, c_vals, seg_rows, continues):
    block_count = scores.shape[0]
    block_rows = scores.shape[1]
    head_dim = x_head.shape[1]
    state_width = b_vals.shape[1]
    log_decay = (-rate * dt_head).reshape(block_count, block_rows)
    cumul = jnp.cumsum(log_decay, axis=1)
    seg_blocks = seg_rows.reshape(block_count, block_rows)
    joins = jnp.concatenate([jnp.reshape(continues, (1,)), (seg_blocks[1:, 0] == seg_blocks[:-1, -1]).astype(jnp.float32)])
    lower = jnp.tril(jnp.ones((block_rows, block_rows), jnp.bool_))
    linked = lower[None] & (seg_blocks[:, :, None] == seg_blocks[:, None, :])
    spread = jnp.where(linked, cumul[:, :, None] - cumul[:, None, :], 0.0)
    decay_mat = jnp.where(linked, jnp.exp(spread), 0.0)
    inputs = (dt_head[:, None] * x_head).reshape(block_count, block_rows, head_dim)
    y_diag = jnp.einsum('bts,bsp->btp', decay_mat * scores, inputs)
    same_end = seg_blocks == seg_blocks[:, -1:]
    end_weight = jnp.where(same_end, jnp.exp(jnp.where(same_end, cumul[:, -1:] - cumul, 0.0)), 0.0)
    b_blocks = b_vals.reshape(block_count, block_rows, state_width)
    block_states = jnp.einsum('bsp,bsn->bpn', end_weight[:, :, None] * inputs, b_blocks)
    keep = joins[:, None] * (seg_blocks == seg_blocks[:, :1]).astype(jnp.float32)
    in_weight = keep * jnp.exp(cumul)
    passes = in_weight[:, -1]

    def advance(carry, item):
        state_now, through = carry
        pass_now, block_state = item
        return ((pass_now * state_now + block_state, through * pass_now), (state_now, through))
    start_carry = (jnp.zeros((head_dim, state_width), jnp.float32), jnp.ones((), jnp.float32))
    (last_state, through), (incoming, before) = lax.scan(advance, start_carry, (passes, block_states))
    c_blocks = c_vals.reshape(block_count, block_rows, state_width)
    y_inter = in_weight[:, :, None] * jnp.einsum('btn,bpn->btp', c_blocks, incoming)
    carry_weight = (in_weight * before[:, None]).reshape(-1)
    return ((y_diag + y_inter).reshape(-1, head_dim), last_state, carry_weight, through)

def full_head(x_head, dt_head, rate, skip_value, scores, b_vals, c_vals, seg_rows, continues, state_in):
    y_local, state_local, carry_weight, through = window_parts(x_head, dt_head, rate, scores, b_vals, c_vals, seg_rows, continues)
    y_head = y_local + carry_weight[:, None] * jnp.dot(c_vals, state_in.T, preferred_element_type=jnp.float32) + skip_value * x_head
    return (y_head, state_local + through * state_in)

def reference(x_raw, bc_raw, dt_raw, conv_x, conv_bc, a_log, dt_bias, skip_weight, segment, grad_y):
    margin = CONV - 1
    seg_ext = jnp.concatenate([jnp.full((margin,), -1, jnp.int32), segment.astype(jnp.int32)])
    block_rows = min(256, TOKENS)
    block_count = TOKENS // block_rows

    def forward(x_full, bc_full, dt_pre, weight_x, weight_bc, log_rate, bias, skip_vals):
        x_ext = jnp.concatenate([jnp.zeros((margin, WIDTH), jnp.float32), x_full], axis=0)
        x_act = round_values(conv_activate(x_ext, weight_x, seg_ext))
        bc_ext = jnp.concatenate([jnp.zeros((margin, 2 * STATE), jnp.float32), bc_full], axis=0)
        bc_act = round_values(conv_activate(bc_ext, weight_bc, seg_ext))
        b_vals = bc_act[:, :STATE]
        c_vals = bc_act[:, STATE:]
        scores = jnp.einsum('btn,bsn->bts', c_vals.reshape(block_count, block_rows, STATE), b_vals.reshape(block_count, block_rows, STATE))
        step_size = jax.nn.softplus(dt_pre + bias[None, :])
        rates = jnp.exp(log_rate)
        x_heads = x_act.reshape(TOKENS, HEADS, HEAD_DIM).transpose(1, 0, 2)
        zero_state = jnp.zeros((HEAD_DIM, STATE), jnp.float32)
        continues = jnp.zeros((), jnp.float32)

        def one_head(item):
            x_head, dt_head, rate, skip_value = item
            y_head, _ = full_head(x_head, dt_head, rate, skip_value, scores, b_vals, c_vals, segment, continues, zero_state)
            return y_head
        y_heads = lax.map(jax.checkpoint(one_head), (x_heads, step_size.T, rates, skip_vals))
        return y_heads.transpose(1, 0, 2).reshape(TOKENS, WIDTH)
    y_full, pull = jax.vjp(forward, x_raw.astype(jnp.float32), bc_raw.astype(jnp.float32), dt_raw, conv_x, conv_bc, a_log, dt_bias, skip_weight)
    grad_xr, grad_bcr, grad_dtr, grad_wx, grad_wbc, grad_alog, grad_bias, grad_skip = pull(grad_y.astype(jnp.float32))
    grad_heads = jnp.stack([grad_alog, grad_bias, grad_skip])
    return (y_full.astype(jnp.bfloat16), grad_xr.astype(jnp.bfloat16), grad_bcr, grad_dtr, grad_wx, grad_wbc, grad_heads)
```

```python
import jax
import jax.numpy as jnp
from jax import lax
from jax.experimental import pallas as pl
from jax.experimental.pallas import tpu as pltpu
from jax.sharding import PartitionSpec as P

F32 = jnp.float32
BF16 = jnp.bfloat16
HIGH = lax.Precision.HIGHEST

BLK = 256
HD = 64
NS = 128
RIM = 16
VMEM = 48 * 1024 * 1024


def mm(a, b, precision=None):
    return lax.dot_general(
        a, b, (((1,), (0,)), ((), ())), precision=precision, preferred_element_type=F32
    )


def mm_nt(a, b, precision=None):
    return lax.dot_general(
        a, b, (((1,), (1,)), ((), ())), precision=precision, preferred_element_type=F32
    )


def iota(shape, dim):
    return lax.broadcasted_iota(jnp.int32, shape, dim)


def eye(n, dtype):
    return (iota((n, n), 0) == iota((n, n), 1)).astype(dtype)


def silu_and_slope(pre):
    sig = 1.0 / (1.0 + jnp.exp(-pre))
    return pre * sig, sig * (1.0 + pre * (1.0 - sig))


def tap_masks(seg_ref):
    target = seg_ref[3:4, :]
    return [(seg_ref[k : k + 1, :] == target).astype(F32) for k in range(4)]


def conv_rows(raw, rim, taps, masks):
    lane = iota((raw.shape[0], 128), 1)
    total = taps[:, 3:4] * raw
    for j in range(1, 4):
        rolled = pltpu.roll(raw, j, 1)
        before = pltpu.roll(rim, j, 1)
        shifted = jnp.concatenate(
            [jnp.where(lane < j, before, rolled[:, :128]), rolled[:, 128:]], axis=1
        )
        total = total + shifted * (taps[:, 3 - j : 4 - j] * masks[3 - j])
    return total


def conv_back(g, raw, rim, taps, masks):
    lane = iota((g.shape[0], 128), 1)
    grad = taps[:, 3:4] * g
    spill = jnp.zeros((g.shape[0], 128), F32)
    width = g.shape[1]
    row = iota((8, width), 0)
    weights = mm_nt((row == 3).astype(F32), g * raw, HIGH)
    for j in range(1, 4):
        masked = g * masks[3 - j]
        rolled = pltpu.roll(masked, width - j, 1)
        inner = jnp.concatenate(
            [rolled[:, :128], jnp.where(lane >= 128 - j, 0.0, rolled[:, 128:])], axis=1
        )
        outer = jnp.where(lane >= 128 - j, rolled[:, 128:], 0.0)
        tap = taps[:, 3 - j : 4 - j]
        grad = grad + tap * inner
        spill = spill + tap * outer
        weights = weights + mm_nt((row == 3 - j).astype(F32), inner * raw, HIGH)
        weights = weights + mm_nt((row[:, :128] == 3 - j).astype(F32), outer * rim, HIGH)
    return grad, spill, weights


def wide_rim(rim):
    return jnp.concatenate([jnp.zeros((128 - RIM, rim.shape[1]), BF16), rim], axis=0)


def local_kernel(
    x_ref, rim_ref, gy_ref, wx_ref, bc_ref, rimbc_ref, wbc_ref, dt_ref, hv_ref, seg_ref,
    pay_ref, xa_ref, slope_ref, y_ref, du_ref, rows_ref, dbc_ref, bcslope_ref, bctok_ref,
    scores_ref, link_ref, bct_ref, acol_ref, dg_ref,
):
    step = pl.program_id(0)
    ident = eye(BLK, BF16)

    @pl.when(step == 0)
    def _():
        masks = tap_masks(seg_ref)
        raw = mm_nt(ident, bc_ref[...])
        rim = mm_nt(ident, wide_rim(rimbc_ref[...]))
        taps = mm_nt(eye(BLK, F32), wbc_ref[...], HIGH)
        act, slope = silu_and_slope(conv_rows(raw, rim, taps, masks))
        bcslope_ref[...] = slope
        act = act.astype(BF16)
        bct_ref[...] = act
        token = mm_nt(ident, act).astype(BF16)
        bctok_ref[...] = token
        scores_ref[...] = mm_nt(token[:, NS:], token[:, :NS])
        seg_row = seg_ref[3:4, :]
        seg_col = mm_nt(ident, seg_ref[...].astype(BF16))[:, 3:4]
        later = iota((BLK, BLK), 0) >= iota((BLK, BLK), 1)
        linked = jnp.logical_and(later, seg_col == seg_row)
        link_ref[...] = jnp.where(linked, 0.0, -jnp.inf)
        heads = dt_ref.shape[1]
        head_eye = eye(heads, F32)
        per_head = mm_nt(head_eye, hv_ref[...], HIGH)
        rate = jnp.exp(per_head[:, 0:1])
        pre = mm_nt(head_eye, dt_ref[...], HIGH) + per_head[:, 1:2]
        dt = jnp.maximum(pre, 0.0) + jnp.log1p(jnp.exp(-jnp.abs(pre)))
        log_decay = -rate * dt
        upto = (iota((BLK, BLK), 0) <= iota((BLK, BLK), 1)).astype(F32)
        cumul = mm(log_decay, upto, HIGH)
        keep = (seg_row == seg_ref[2:3, 0:1]).astype(F32)
        same_end = seg_row == seg_row[:, BLK - 1 :]
        rows_ref[0] = dt
        rows_ref[1] = cumul
        rows_ref[2] = keep * jnp.exp(cumul)
        rows_ref[3] = jnp.exp(jnp.where(same_end, cumul[:, BLK - 1 :] - cumul, -jnp.inf))
        rows_ref[4] = 1.0 / (1.0 + jnp.exp(-pre))
        dg_ref[...] = jnp.zeros_like(dg_ref)

    masks = tap_masks(seg_ref)
    raw = mm_nt(ident, x_ref[...])
    rim = mm_nt(ident, wide_rim(rim_ref[...]))
    taps = mm_nt(eye(BLK, F32), wx_ref[...], HIGH)
    act, slope = silu_and_slope(conv_rows(raw, rim, taps, masks))
    slope_ref[...] = slope
    act = act.astype(BF16)
    xa_ref[...] = act
    act = act.astype(F32)
    gy = gy_ref[...]
    dy = mm_nt(ident, gy)
    dy_low = dy.astype(BF16)
    b_tok = bctok_ref[:, :NS]
    c_tok = bctok_ref[:, NS:]
    per_step = BLK // HD
    cumul_all = rows_ref[1]
    acol_ref[...] = mm_nt(eye(BLK, F32), cumul_all, HIGH)
    step_heads = step * per_step
    pick = (iota((cumul_all.shape[0], per_step), 0) == step_heads + iota(
        (cumul_all.shape[0], per_step), 1)).astype(F32)
    acols = mm(acol_ref[...], pick, HIGH)
    for k in range(per_step):
        head = step_heads + k
        lo, hi = k * HD, (k + 1) * HD
        dt = rows_ref[0, pl.ds(head, 1), :]
        arow = rows_ref[1, pl.ds(head, 1), :]
        carry = rows_ref[2, pl.ds(head, 1), :]
        end = rows_ref[3, pl.ds(head, 1), :]
        u = dt * act[lo:hi]
        u_low = u.astype(BF16)
        state = mm((end * u).astype(BF16), b_tok)
        back = mm((carry * dy[lo:hi]).astype(BF16), c_tok)
        through = carry[:, BLK - 1 :]
        t_hi = through.astype(BF16)
        t_rest = through - t_hi.astype(F32)
        t_mid = t_rest.astype(BF16)
        t_low = (t_rest - t_mid.astype(F32)).astype(BF16)
        which = iota((16, NS), 0)
        thr = jnp.where(
            which == 0, t_hi.astype(F32), jnp.where(which == 1, t_mid.astype(F32), t_low.astype(F32))
        ).astype(BF16)
        for half in range(2):
            j = 2 * k + half
            pay_ref[j, 0:32, :] = state[half * 32 : half * 32 + 32].astype(BF16)
            pay_ref[j, 32:64, :] = back[half * 32 : half * 32 + 32].astype(BF16)
            pay_ref[j, 64:80, :] = thr
        du_first = None
        for tb in range(2):
            t0, t1 = tb * 128, tb * 128 + 128
            decay = jnp.exp(acols[t0:t1, k : k + 1] - arow[:, :t1] + link_ref[t0:t1, :t1])
            mixed = (decay * scores_ref[t0:t1, :t1]).astype(BF16)
            y_ref[lo:hi, t0:t1] = mm_nt(u_low[:, :t1], mixed)
            du = mm(dy_low[lo:hi, t0:t1], mixed)
            if tb == 0:
                du_first = du
            else:
                du_ref[lo:hi, :128] = du_first + du[:, :128]
                du_ref[lo:hi, 128:] = du[:, 128:]
            dmix = mm(gy[t0:t1, lo:hi], u_low[:, :t1])
            dg_ref[t0:t1, :t1] += decay * dmix

    @pl.when(step == pl.num_programs(0) - 1)
    def _():
        dg = dg_ref[...].astype(BF16)
        dbc_ref[:NS, :] = mm(bct_ref[NS:, :], dg)
        dbc_ref[NS:, :] = mm_nt(bct_ref[:NS, :], dg)


def scan_kernel(peers, in_ref, out_ref):
    ahead = jnp.zeros((32, NS), F32)
    behind = jnp.zeros((32, NS), F32)
    for i in range(peers):
        def through(at):
            parts = in_ref[at, 64:80, :].astype(F32)
            return parts[0:1] + parts[1:2] + parts[2:3]

        out_ref[i, 0:32, :] = ahead.astype(BF16)
        ahead = through(i) * ahead + in_ref[i, 0:32, :].astype(F32)
        at = peers - 1 - i
        out_ref[at, 32:64, :] = behind.astype(BF16)
        behind = through(at) * behind + in_ref[at, 32:64, :].astype(F32)


def final_kernel(
    x_ref, rim_ref, gy_ref, wx_ref, bc_ref, rimbc_ref, wbc_ref, hv_ref, seg_ref,
    state_ref, xa_ref, slope_ref, y_ref, du_ref, rows_ref, dbc_ref, bcslope_ref, bctok_ref,
    out_ref, gx_ref, last_ref, spill_ref, gw_ref, gdt_ref, gh_ref, pay_ref,
    red_ref, acc_ref,
):
    step = pl.program_id(0)
    ident = eye(BLK, BF16)
    per_step = BLK // HD
    step_heads = step * per_step
    masks = tap_masks(seg_ref)
    heads = rows_ref.shape[1]

    @pl.when(step == 0)
    def _():
        acc_ref[...] = dbc_ref[...]

    state_in = state_ref[:, 0:32, :].reshape(BLK, NS)
    state_back = state_ref[:, 32:64, :].reshape(BLK, NS)
    b_tok = bctok_ref[:, :NS]
    c_tok = bctok_ref[:, NS:]
    dy = mm_nt(ident, gy_ref[...])
    carried = mm_nt(state_in, c_tok)
    from_end = mm_nt(state_back, b_tok)
    act = xa_ref[...].astype(F32)
    skips = mm_nt(eye(heads, F32), hv_ref[...], HIGH)[:, 2:3]
    skip_wide = jnp.broadcast_to(skips, (heads, BLK))
    both = state_in.astype(F32) * state_back.astype(F32)
    y_parts, g_parts, cdy_parts, eu_parts = [], [], [], []
    for k in range(per_step):
        head = step_heads + k
        lo, hi = k * HD, (k + 1) * HD
        dt = rows_ref[0, pl.ds(head, 1), :]
        carry = rows_ref[2, pl.ds(head, 1), :]
        end = rows_ref[3, pl.ds(head, 1), :]
        is_head = iota((heads, BLK), 0) == head
        skip = jnp.sum(jnp.where(is_head, skip_wide, 0.0), axis=0, keepdims=True)
        x_h = act[lo:hi]
        dy_h = dy[lo:hi]
        y_h = y_ref[lo:hi, :] + carry * carried[lo:hi]
        ext = end * from_end[lo:hi]
        du = du_ref[lo:hi, :] + ext
        u = dt * x_h
        u_low = u.astype(BF16).astype(F32)
        last_lane = iota((1, BLK), 1) == BLK - 1
        at_end = jnp.sum(jnp.sum(u_low * ext, axis=0, keepdims=True), axis=1, keepdims=True)
        joint = jnp.sum(jnp.sum(both[lo:hi], axis=0, keepdims=True), axis=1, keepdims=True)
        at_end = at_end + carry[:, BLK - 1 :] * joint
        ga = jnp.sum(dy_h * y_h - u_low * du, axis=0, keepdims=True)
        red_ref[0, pl.ds(head, 1), :] = ga + jnp.where(last_lane, at_end, 0.0)
        red_ref[1, pl.ds(head, 1), :] = jnp.sum(x_h * du, axis=0, keepdims=True)
        red_ref[2, pl.ds(head, 1), :] = jnp.sum(x_h * dy_h, axis=0, keepdims=True)
        y_parts.append((y_h + skip * x_h).astype(BF16))
        g_parts.append(dt * du + skip * dy_h)
        cdy_parts.append((carry * dy_h).astype(BF16))
        eu_parts.append((end * u).astype(BF16))
    out_ref[...] = mm_nt(ident, jnp.concatenate(y_parts, axis=0)).astype(BF16)
    small = eye(NS, BF16)
    acc_ref[:NS, :] += mm(mm_nt(small, state_back).astype(BF16), jnp.concatenate(eu_parts, axis=0))
    acc_ref[NS:, :] += mm(mm_nt(small, state_in).astype(BF16), jnp.concatenate(cdy_parts, axis=0))
    g = jnp.concatenate(g_parts, axis=0) * slope_ref[...]
    raw = mm_nt(ident, x_ref[...])
    rim = mm_nt(ident, wide_rim(rim_ref[...]))
    taps = mm_nt(eye(BLK, F32), wx_ref[...], HIGH)
    grad, spill, weights = conv_back(g, raw, rim, taps, masks)
    gx_ref[...] = mm_nt(ident, grad.astype(BF16)).astype(BF16)
    tail = (iota((RIM, BLK), 0) + (BLK - RIM) == iota((RIM, BLK), 1)).astype(F32)
    last_ref[...] = mm_nt(tail, grad, HIGH)
    rim_pick = (iota((RIM, 128), 0) + (128 - RIM) == iota((RIM, 128), 1)).astype(F32)
    spill_ref[...] = mm_nt(rim_pick, spill, HIGH)
    gw_ref[...] = weights

    @pl.when(step == pl.num_programs(0) - 1)
    def _():
        per_head = mm_nt(eye(heads, F32), hv_ref[...], HIGH)
        rate = jnp.exp(per_head[:, 0:1])
        later = (iota((BLK, BLK), 0) >= iota((BLK, BLK), 1)).astype(F32)
        grad_log = mm(red_ref[0], later, HIGH)
        grad_step = (red_ref[1] - rate * grad_log) * rows_ref[4]
        gdt_ref[...] = mm_nt(eye(BLK, F32), grad_step, HIGH)
        which = iota((8, BLK), 0)
        gh = mm_nt((which == 0).astype(F32), -rate * rows_ref[0] * grad_log, HIGH)
        gh = gh + mm_nt((which == 1).astype(F32), grad_step, HIGH)
        gh_ref[...] = gh + mm_nt((which == 2).astype(F32), red_ref[2], HIGH)
        g_bc = acc_ref[...] * bcslope_ref[...]
        raw_bc = mm_nt(ident, bc_ref[...])
        rim_bc = mm_nt(ident, wide_rim(rimbc_ref[...]))
        taps_bc = mm_nt(eye(BLK, F32), wbc_ref[...], HIGH)
        grad_bc, spill_bc, weights_bc = conv_back(g_bc, raw_bc, rim_bc, taps_bc, masks)
        token = mm_nt(eye(BLK, F32), grad_bc, HIGH)
        shares = pay_ref.shape[0]
        share = BLK // shares
        last8 = (iota((8, 128), 0) + 120 == iota((8, 128), 1)).astype(F32)
        spill8 = mm_nt(last8, spill_bc, HIGH)
        for j in range(shares):
            pay_ref[j, 0:share, :] = token[j * share : (j + 1) * share]
            pay_ref[j, share : share + 8, :] = weights_bc
            pay_ref[j, share + 8 : share + 16, :] = spill8


def patch_kernel(gx_ref, last_ref, spill_ref, out_ref):
    del gx_ref
    out_ref[...] = (last_ref[...] + spill_ref[...]).astype(BF16)


def whole(shape):
    zeros = (0,) * len(shape)
    return pl.BlockSpec(shape, lambda *_: zeros)


def columns(rows):
    return pl.BlockSpec((rows, BLK), lambda i: (0, i))


def channel_rows(width):
    return pl.BlockSpec((BLK, width), lambda i: (i, 0))


def shaped(shape, dtype):
    return jax.ShapeDtypeStruct(shape, dtype)


def passed_along(value, by):
    peers = lax.axis_size("ctx")
    pairs = [(i, i + by) for i in range(peers) if 0 <= i + by < peers]
    return lax.ppermute(value, "ctx", pairs)


def summed_over_ctx(value):
    peers = lax.axis_size("ctx")
    value = value + lax.ppermute(value, "ctx", [(i, i ^ 1) for i in range(peers)])
    for stride in (2, 8):
        def turned(i, by):
            at = i // stride % 4
            return i + ((at + by) % 4 - at) * stride

        got = [
            lax.ppermute(value, "ctx", [(i, turned(i, by)) for i in range(peers)])
            for by in (1, 2, 3)
        ]
        value = (value + got[0]) + (got[1] + got[2])
    return value


def local(x_raw, bc_raw, dt_raw, conv_x, conv_bc, a_log, dt_bias, skip_weight, segment, grad_y):
    rows, channels = x_raw.shape
    heads = dt_raw.shape[1]
    steps = channels // BLK
    peers = lax.axis_size("ctx")
    shares = lax.axis_size("head")
    share = rows // shares
    rim = passed_along(jnp.concatenate([x_raw[rows - RIM :], bc_raw[rows - RIM :]], axis=1), 1)
    rim_x = rim[:, :channels]
    rim_bc = rim[:, channels:]
    padded = jnp.concatenate([jnp.full((3,), -1, jnp.int32), segment])
    seg_ext = lax.dynamic_slice_in_dim(padded, lax.axis_index("ctx") * rows, rows + 3)
    seg = jnp.stack([seg_ext[min(k, 3) : min(k, 3) + rows] for k in range(8)]).astype(F32)
    hv = jnp.stack([a_log, dt_bias, skip_weight, skip_weight])

    pay, xa, slope, y_loc, du_loc, head_rows, dbc, bcslope, bctok = pl.pallas_call(
        local_kernel,
        grid=(steps,),
        in_specs=[
            columns(rows), columns(RIM), columns(rows), columns(4),
            whole((rows, 256)), whole((RIM, 256)), whole((4, 256)),
            whole((rows, heads)), whole((4, heads)), whole((8, rows)),
        ],
        out_specs=[
            pl.BlockSpec((8, 80, NS), lambda i: (i, 0, 0)),
            channel_rows(rows), channel_rows(rows), channel_rows(rows), channel_rows(rows),
            whole((5, heads, rows)), whole((256, rows)), whole((256, rows)), whole((rows, 256)),
        ],
        out_shape=[
            shaped((peers, 80, NS), BF16),
            shaped((channels, rows), BF16), shaped((channels, rows), F32),
            shaped((channels, rows), F32), shaped((channels, rows), F32),
            shaped((5, heads, rows), F32), shaped((256, rows), F32),
            shaped((256, rows), F32), shaped((rows, 256), BF16),
        ],
        scratch_shapes=[
            pltpu.VMEM((rows, rows), F32), pltpu.VMEM((rows, rows), F32),
            pltpu.VMEM((256, rows), BF16), pltpu.VMEM((rows, heads), F32),
            pltpu.VMEM((rows, rows), F32),
        ],
        compiler_params=pltpu.CompilerParams(vmem_limit_bytes=VMEM),
        name="local_part",
    )(x_raw, rim_x, grad_y, conv_x, bc_raw, rim_bc, conv_bc, dt_raw, hv, seg)

    got = lax.all_to_all(pay, "ctx", 0, 0, tiled=True)
    carried = pl.pallas_call(
        lambda *refs: scan_kernel(peers, *refs),
        in_specs=[pl.BlockSpec(memory_space=pltpu.VMEM)],
        out_specs=pl.BlockSpec(memory_space=pltpu.VMEM),
        out_shape=shaped((peers, 64, NS), BF16),
        name="state_scan",
    )(got)
    states = lax.all_to_all(carried, "ctx", 0, 0, tiled=True)

    ssd_out, gx, last, spill, gw, grad_dt, gh, pay_bc = pl.pallas_call(
        final_kernel,
        grid=(steps,),
        in_specs=[
            columns(rows), columns(RIM), columns(rows), columns(4),
            whole((rows, 256)), whole((RIM, 256)), whole((4, 256)),
            whole((4, heads)), whole((8, rows)),
            pl.BlockSpec((8, 64, NS), lambda i: (i, 0, 0)),
            channel_rows(rows), channel_rows(rows), channel_rows(rows), channel_rows(rows),
            whole((5, heads, rows)), whole((256, rows)), whole((256, rows)), whole((rows, 256)),
        ],
        out_specs=[
            columns(rows), columns(rows), columns(RIM), columns(RIM), columns(8),
            whole((rows, heads)), whole((8, heads)), whole((shares, share + 16, 256)),
        ],
        out_shape=[
            shaped((rows, channels), BF16), shaped((rows, channels), BF16),
            shaped((RIM, channels), F32), shaped((RIM, channels), F32), shaped((8, channels), F32),
            shaped((rows, heads), F32), shaped((8, heads), F32),
            shaped((shares, share + 16, 256), F32),
        ],
        scratch_shapes=[
            pltpu.VMEM((3, heads, rows), F32), pltpu.VMEM((256, rows), F32),
        ],
        compiler_params=pltpu.CompilerParams(vmem_limit_bytes=VMEM),
        name="final_part",
    )(
        x_raw, rim_x, grad_y, conv_x, bc_raw, rim_bc, conv_bc, hv, seg,
        states, xa, slope, y_loc, du_loc, head_rows, dbc, bcslope, bctok,
    )

    spill_x = passed_along(spill, -1)
    grad_x = pl.pallas_call(
        patch_kernel,
        grid=(1,),
        in_specs=[
            pl.BlockSpec(memory_space=pl.ANY), whole((RIM, channels)), whole((RIM, channels)),
        ],
        out_specs=pl.BlockSpec((RIM, channels), lambda i: (rows // RIM - 1, 0)),
        out_shape=shaped((rows, channels), BF16),
        input_output_aliases={0: 0},
        name="last_rows",
    )(gx, last, spill_x)

    got_bc = jnp.sum(lax.all_to_all(pay_bc, "head", 0, 0, tiled=True), axis=0)
    spill_bc = passed_along(got_bc[share + 8 :], -1)
    sums = summed_over_ctx(
        jnp.concatenate([gw, got_bc[share : share + 8], jnp.pad(gh, ((0, 0), (0, 112)))], axis=1)
    )
    is_last = lax.axis_index("head") == shares - 1
    grad_bc = got_bc[:share] + jnp.pad(
        jnp.where(is_last, spill_bc, 0.0), ((share - 8, 0), (0, 0))
    )
    return (
        ssd_out, grad_x, grad_bc, grad_dt,
        sums[:4, :channels], sums[:4, channels : channels + 256],
        sums[:3, channels + 256 : channels + 256 + heads],
    )


def solution(mesh):
    in_specs = (
        P("ctx", "head"), P("ctx", None), P("ctx", "head"), P(None, "head"), P(),
        P("head"), P("head"), P("head"), P(), P("ctx", "head"),
    )
    out_specs = (
        P("ctx", "head"), P("ctx", "head"), P(("ctx", "head"), None), P("ctx", "head"),
        P(None, "head"), P(), P(None, "head"),
    )
    return jax.shard_map(local, mesh=mesh, in_specs=in_specs, out_specs=out_specs, check_vma=False)
```

```python
import jax
import jax.numpy as jnp
from jax import lax
from jax.experimental import pallas as pl
from jax.experimental.pallas import tpu as pltpu
from jax.sharding import PartitionSpec as P

F32 = jnp.float32
BF16 = jnp.bfloat16

BLK = 256
HD = 64
NS = 128
RIM = 16
PER = BLK // HD
VMEM = 24 * 1024 * 1024

DT, CUMUL, CARRY, END, SIG, SKIP, RATE, MASK = range(8)


def mm(a, b):
    return lax.dot_general(a, b, (((1,), (0,)), ((), ())), preferred_element_type=F32)


def mm_nt(a, b):
    return lax.dot_general(a, b, (((1,), (1,)), ((), ())), preferred_element_type=F32)


def split(value, count):
    parts = []
    for _ in range(count):
        part = value.astype(BF16)
        parts.append(part)
        value = value - part.astype(F32)
    return parts


def pick_nt(pick, value, count):
    return sum(mm_nt(pick, part) for part in split(value, count))


def pick_right(value, pick, count):
    return sum(mm(part, pick) for part in split(value, count))


def iota(shape, dim):
    return lax.broadcasted_iota(jnp.int32, shape, dim)


def eye(n, dtype):
    return (iota((n, n), 0) == iota((n, n), 1)).astype(dtype)


def silu_and_slope(pre):
    sig = 1.0 / (1.0 + jnp.exp(-pre))
    return pre * sig, sig * (1.0 + pre * (1.0 - sig))


def conv_own(raw, taps, masks):
    lane = iota((raw.shape[0], 128), 1)
    total = taps[:, 3:4] * raw
    for j in range(1, 4):
        rolled = pltpu.roll(raw, j, 1)
        shifted = jnp.concatenate(
            [jnp.where(lane < j, 0.0, rolled[:, :128]), rolled[:, 128:]], axis=1
        )
        total = total + shifted * (taps[:, 3 - j : 4 - j] * masks[3 - j])
    return total


def conv_rim(rim, taps, masks):
    lane = iota(rim.shape, 1)
    total = jnp.zeros(rim.shape, F32)
    for j in range(1, 4):
        before = jnp.where(lane < j, pltpu.roll(rim, j, 1), 0.0)
        total = total + before * (taps[:, 3 - j : 4 - j] * masks[3 - j][:, :128])
    return total


def conv_back(g, raw, rim, taps, masks):
    lane = iota((g.shape[0], 128), 1)
    grad = taps[:, 3:4] * g
    spill = jnp.zeros((g.shape[0], 128), F32)
    row = iota((8, 128), 0)

    def weight_row(k, product):
        return pick_nt((row == k).astype(BF16), product, 2)

    product = g * raw
    weights = weight_row(3, product[:, :128] + product[:, 128:])
    for j in range(1, 4):
        masked = g * masks[3 - j]
        rolled = pltpu.roll(masked, g.shape[1] - j, 1)
        wrapped = lane >= 128 - j
        first = rolled[:, :128]
        second = jnp.where(wrapped, 0.0, rolled[:, 128:])
        outer = jnp.where(wrapped, rolled[:, 128:], 0.0)
        tap = taps[:, 3 - j : 4 - j]
        grad = grad + tap * jnp.concatenate([first, second], axis=1)
        spill = spill + tap * outer
        weights = weights + weight_row(
            3 - j, first * raw[:, :128] + second * raw[:, 128:] + outer * rim
        )
    return grad, spill, weights


def wide_rim(rim):
    return jnp.concatenate([jnp.zeros((128 - RIM, rim.shape[1]), BF16), rim], axis=0)


def masks_of(rows_ref):
    return [rows_ref[MASK, k : k + 1, :] for k in range(4)]


def head_row(rows_ref, plane, head):
    return rows_ref[plane, pl.ds(head, 1), :]


def prep_kernel(
    x_ref, gy_ref, wx_ref, bc_ref, wbc_ref, dt_ref, hv_ref, seg_ref,
    xt_ref, dyt_ref, pre_ref, taps_ref, rows_ref, bct_ref, bcpre_ref, bctaps_ref,
):
    ident = eye(BLK, BF16)

    def taps_of(ref):
        taps = pick_nt(ident, ref[...], 3)
        return jnp.concatenate([taps, jnp.zeros((BLK, 124), F32)], axis=1)

    @pl.when(pl.program_id(0) == 0)
    def _():
        target = seg_ref[3:4, :]
        rows_ref[MASK] = jnp.concatenate(
            [(seg_ref[k : k + 1, :] == target).astype(F32) for k in range(4)]
            + [target, jnp.zeros((11, BLK), F32)],
            axis=0,
        )
        heads = dt_ref.shape[0]
        per_head = pick_nt(eye(heads, BF16), hv_ref[...], 3)
        rate = jnp.exp(per_head[:, 0:1])
        pre = dt_ref[...] + per_head[:, 1:2]
        dt = jnp.maximum(pre, 0.0) + jnp.log1p(jnp.exp(-jnp.abs(pre)))
        upto = (iota((BLK, BLK), 0) <= iota((BLK, BLK), 1)).astype(BF16)
        cumul = pick_right(-rate * dt, upto, 3)
        keep = (target == seg_ref[2:3, 0:1]).astype(F32)
        same_end = target == target[:, BLK - 1 :]
        rows_ref[DT] = dt
        rows_ref[CUMUL] = cumul
        rows_ref[CARRY] = keep * jnp.exp(cumul)
        rows_ref[END] = jnp.exp(jnp.where(same_end, cumul[:, BLK - 1 :] - cumul, -jnp.inf))
        rows_ref[SIG] = 1.0 / (1.0 + jnp.exp(-pre))
        rows_ref[SKIP] = jnp.broadcast_to(per_head[:, 2:3], (heads, BLK))
        rows_ref[RATE] = jnp.broadcast_to(rate, (heads, BLK))
        bct = mm_nt(ident, bc_ref[...])
        bct_ref[...] = bct.astype(BF16)
        bctaps = taps_of(wbc_ref)
        bctaps_ref[...] = bctaps
        bcpre_ref[...] = conv_own(bct, bctaps, masks_of(rows_ref))

    raw = mm_nt(ident, x_ref[...])
    xt_ref[...] = raw.astype(BF16)
    dyt_ref[...] = mm_nt(ident, gy_ref[...]).astype(BF16)
    taps = taps_of(wx_ref)
    taps_ref[...] = taps
    pre_ref[...] = conv_own(raw, taps, masks_of(rows_ref))


def state_kernel(
    pre_ref, rim_ref, taps_ref, dyt_ref, rows_ref, bcpre_ref, rimbc_ref, bctaps_ref,
    pay_ref, xa_ref, slope_ref, eu_ref, cdy_ref, rimt_ref,
    bctok_ref, bcact_ref, bcslope_ref, bcrimt_ref,
):
    step = pl.program_id(0)
    ident = eye(BLK, BF16)
    masks = masks_of(rows_ref)

    def activate(pre, rim_rows, taps):
        rim = mm_nt(ident, wide_rim(rim_rows))
        pre = jnp.concatenate([pre[:, :128] + conv_rim(rim, taps, masks), pre[:, 128:]], axis=1)
        act, slope = silu_and_slope(pre)
        return act.astype(BF16), slope, rim.astype(BF16)

    @pl.when(step == 0)
    def _():
        act, slope, rim = activate(bcpre_ref[...], rimbc_ref[...], bctaps_ref[...])
        bcact_ref[...] = act
        bcslope_ref[...] = slope
        bcrimt_ref[...] = rim
        bctok_ref[...] = mm_nt(ident, act).astype(BF16)

    act, slope, rim = activate(pre_ref[...], rim_ref[...], taps_ref[...])
    xa_ref[...] = act
    slope_ref[...] = slope
    rimt_ref[...] = rim
    for k in range(PER):
        head = step * PER + k
        lo, hi = k * HD, (k + 1) * HD
        u = head_row(rows_ref, DT, head) * act[lo:hi].astype(F32)
        eu_ref[lo:hi, :] = (head_row(rows_ref, END, head) * u).astype(BF16)
        carry = head_row(rows_ref, CARRY, head)
        cdy_ref[lo:hi, :] = (carry * dyt_ref[lo:hi, :].astype(F32)).astype(BF16)
        parts = split(carry[:, BLK - 1 :], 3)
        which = iota((16, NS), 0)
        through = jnp.where(
            which == 0, parts[0].astype(F32),
            jnp.where(which == 1, parts[1].astype(F32), parts[2].astype(F32)),
        ).astype(BF16)
        pay_ref[2 * k, 64:80, :] = through
        pay_ref[2 * k + 1, 64:80, :] = through
    state = mm(eu_ref[...], bctok_ref[:, :NS]).astype(BF16)
    back = mm(cdy_ref[...], bctok_ref[:, NS:]).astype(BF16)
    for j in range(2 * PER):
        pay_ref[j, 0:32, :] = state[j * 32 : j * 32 + 32]
        pay_ref[j, 32:64, :] = back[j * 32 : j * 32 + 32]


def block_kernel(
    xa_ref, gy_ref, dyt_ref, rows_ref, bctok_ref, bcact_ref,
    y_ref, du_ref, dbc_ref,
    scores_ref, link_ref, acol_ref, dg_ref,
):
    step = pl.program_id(0)

    @pl.when(step == 0)
    def _():
        ident = eye(BLK, BF16)
        scores_ref[...] = mm_nt(bctok_ref[:, NS:], bctok_ref[:, :NS])
        seg_row = rows_ref[MASK, 4:5, :]
        seg_col = mm_nt(ident, rows_ref[MASK].astype(BF16))[:, 4:5]
        later = iota((BLK, BLK), 0) >= iota((BLK, BLK), 1)
        linked = jnp.logical_and(later, seg_col == seg_row)
        link_ref[...] = jnp.where(linked, 0.0, -jnp.inf)
        dg_ref[...] = jnp.zeros_like(dg_ref)
        cumul = pick_nt(ident, rows_ref[CUMUL], 3)
        for at in range(acol_ref.shape[0]):
            acol_ref[at] = cumul[:, at * PER : (at + 1) * PER]

    acols = acol_ref[step]
    for k in range(PER):
        head = step * PER + k
        lo, hi = k * HD, (k + 1) * HD
        arow = head_row(rows_ref, CUMUL, head)
        u_low = (head_row(rows_ref, DT, head) * xa_ref[lo:hi, :].astype(F32)).astype(BF16)
        du_first = None
        for tb in range(2):
            t0, t1 = tb * 128, tb * 128 + 128
            decay = jnp.exp(acols[t0:t1, k : k + 1] - arow[:, :t1] + link_ref[t0:t1, :t1])
            mixed = (decay * scores_ref[t0:t1, :t1]).astype(BF16)
            y_ref[lo:hi, t0:t1] = mm_nt(u_low[:, :t1], mixed)
            du = mm(dyt_ref[lo:hi, t0:t1], mixed)
            if tb == 0:
                du_first = du
            else:
                du_ref[lo:hi, :128] = du_first + du[:, :128]
                du_ref[lo:hi, 128:] = du[:, 128:]
            dmix = mm(gy_ref[t0:t1, lo:hi], u_low[:, :t1])
            dg_ref[t0:t1, :t1] += decay * dmix

    @pl.when(step == pl.num_programs(0) - 1)
    def _():
        dg = dg_ref[...].astype(BF16)
        dbc_ref[:NS, :] = mm(bcact_ref[NS:, :], dg)
        dbc_ref[NS:, :] = mm_nt(bcact_ref[:NS, :], dg)


def scan_kernel(in_ref, out_ref):
    peers = in_ref.shape[0]
    ahead = jnp.zeros((32, NS), F32)
    behind = jnp.zeros((32, NS), F32)

    def through(at):
        parts = in_ref[at, 64:80, :].astype(F32)
        return parts[0:1] + parts[1:2] + parts[2:3]

    for i in range(peers):
        out_ref[i, 0:32, :] = ahead.astype(BF16)
        ahead = through(i) * ahead + in_ref[i, 0:32, :].astype(F32)
        at = peers - 1 - i
        out_ref[at, 32:64, :] = behind.astype(BF16)
        behind = through(at) * behind + in_ref[at, 32:64, :].astype(F32)


def bc_kernel(
    state_ref, eu_ref, cdy_ref, dbc_ref, bcslope_ref, bct_ref, bcrimt_ref, bctaps_ref, rows_ref,
    pay_ref,
    acc_ref,
):
    step = pl.program_id(0)

    @pl.when(step == 0)
    def _():
        acc_ref[...] = dbc_ref[...]

    small = eye(NS, BF16)
    state_in = state_ref[:, 0:32, :].reshape(BLK, NS)
    state_back = state_ref[:, 32:64, :].reshape(BLK, NS)
    acc_ref[:NS, :] += mm(mm_nt(small, state_back).astype(BF16), eu_ref[...])
    acc_ref[NS:, :] += mm(mm_nt(small, state_in).astype(BF16), cdy_ref[...])

    @pl.when(step == pl.num_programs(0) - 1)
    def _():
        grad, spill, weights = conv_back(
            acc_ref[...] * bcslope_ref[...], bct_ref[...].astype(F32),
            bcrimt_ref[...].astype(F32), bctaps_ref[...], masks_of(rows_ref),
        )
        token = mm_nt(eye(BLK, BF16), grad.astype(BF16)).astype(BF16)
        last8 = (iota((8, 128), 0) + 120 == iota((8, 128), 1)).astype(BF16)
        rest = jnp.concatenate([weights, mm_nt(last8, spill.astype(BF16))], axis=0).astype(BF16)
        shares = pay_ref.shape[0]
        share = BLK // shares
        for j in range(shares):
            pay_ref[j, 0:share, :] = token[j * share : (j + 1) * share]
            pay_ref[j, share : share + 16, :] = rest


def x_kernel(
    state_ref, xa_ref, slope_ref, y_ref, du_ref, xt_ref, dyt_ref, rimt_ref, taps_ref, rows_ref,
    bctok_ref,
    out_ref, gx_ref, last_ref, spill_ref, gw_ref, gdt_ref, gh_ref,
    red_ref,
):
    step = pl.program_id(0)
    ident = eye(BLK, BF16)
    masks = masks_of(rows_ref)
    state_in = state_ref[:, 0:32, :].reshape(BLK, NS)
    state_back = state_ref[:, 32:64, :].reshape(BLK, NS)
    carried = mm_nt(state_in, bctok_ref[:, NS:])
    from_end = mm_nt(state_back, bctok_ref[:, :NS])
    both = state_in.astype(F32) * state_back.astype(F32)
    last_lane = iota((1, BLK), 1) == BLK - 1
    y_parts, g_parts = [], []
    for k in range(PER):
        head = step * PER + k
        lo, hi = k * HD, (k + 1) * HD
        dt = head_row(rows_ref, DT, head)
        carry = head_row(rows_ref, CARRY, head)
        skip = head_row(rows_ref, SKIP, head)
        x_h = xa_ref[lo:hi, :].astype(F32)
        dy_h = dyt_ref[lo:hi, :].astype(F32)
        y_h = y_ref[lo:hi, :] + carry * carried[lo:hi]
        ext = head_row(rows_ref, END, head) * from_end[lo:hi]
        du = du_ref[lo:hi, :] + ext
        u_low = (dt * x_h).astype(BF16).astype(F32)
        at_end = jnp.sum(jnp.sum(u_low * ext, axis=0, keepdims=True), axis=1, keepdims=True)
        joint = jnp.sum(jnp.sum(both[lo:hi], axis=0, keepdims=True), axis=1, keepdims=True)
        at_end = at_end + carry[:, BLK - 1 :] * joint
        ga = jnp.sum(dy_h * y_h - u_low * du, axis=0, keepdims=True)
        red_ref[0, pl.ds(head, 1), :] = ga + jnp.where(last_lane, at_end, 0.0)
        red_ref[1, pl.ds(head, 1), :] = jnp.sum(x_h * du, axis=0, keepdims=True)
        red_ref[2, pl.ds(head, 1), :] = jnp.sum(x_h * dy_h, axis=0, keepdims=True)
        y_parts.append((y_h + skip * x_h).astype(BF16))
        g_parts.append((dt * du + skip * dy_h) * slope_ref[lo:hi, :])
    out_ref[...] = mm_nt(ident, jnp.concatenate(y_parts, axis=0)).astype(BF16)
    grad, spill, weights = conv_back(
        jnp.concatenate(g_parts, axis=0), xt_ref[...].astype(F32), rimt_ref[...].astype(F32),
        taps_ref[...], masks,
    )
    gx_ref[...] = mm_nt(ident, grad.astype(BF16)).astype(BF16)
    pick = (iota((RIM, 128), 0) + (128 - RIM) == iota((RIM, 128), 1)).astype(BF16)
    last_ref[...] = pick_nt(pick, grad[:, 128:], 2)
    spill_ref[...] = pick_nt(pick, spill, 2)
    gw_ref[...] = weights

    @pl.when(step == pl.num_programs(0) - 1)
    def _():
        later = (iota((BLK, BLK), 0) >= iota((BLK, BLK), 1)).astype(BF16)
        grad_log = pick_right(red_ref[0], later, 3)
        rate = rows_ref[RATE]
        grad_step = (red_ref[1] - rate * grad_log) * rows_ref[SIG]
        gdt_ref[...] = grad_step
        which = iota((8, BLK), 0)
        terms = (-rate * rows_ref[DT] * grad_log, grad_step, red_ref[2])
        gh_ref[...] = jnp.zeros_like(gh_ref)
        gh_ref[:, : rate.shape[0]] = sum(
            pick_nt((which == k).astype(BF16), term, 3) for k, term in enumerate(terms)
        )


def patch_kernel(gx_ref, last_ref, spill_ref, out_ref):
    del gx_ref
    out_ref[...] = (last_ref[...] + spill_ref[...]).astype(BF16)


def pack_kernel(got_ref, gw_ref, gh_ref, sums_ref, own_ref, spill_ref):
    share = own_ref.shape[0]
    total = jnp.sum(got_ref[...].astype(F32), axis=0)
    own_ref[...] = total[:share]
    spill_ref[...] = total[share + 8 :]
    width = gw_ref.shape[1]
    sums_ref[:, :width] = gw_ref[...]
    sums_ref[:, width : width + 256] = total[share : share + 8]
    sums_ref[:, width + 256 :] = gh_ref[...]


def finish_kernel(a_ref, b_ref, c_ref, d_ref, wx_ref, wbc_ref, heads_ref):
    total = (a_ref[...] + b_ref[...]) + (c_ref[...] + d_ref[...])
    width = wx_ref.shape[1]
    wx_ref[...] = total[:4, :width]
    wbc_ref[...] = total[:4, width : width + 256]
    heads_ref[...] = total[:3, width + 256 : width + 256 + heads_ref.shape[1]]


def whole(shape):
    zeros = (0,) * len(shape)
    return pl.BlockSpec(shape, lambda *_: zeros)


def columns(rows):
    return pl.BlockSpec((rows, BLK), lambda i: (0, i))


def channel_rows(width):
    return pl.BlockSpec((BLK, width), lambda i: (i, 0))


def shaped(shape, dtype):
    return jax.ShapeDtypeStruct(shape, dtype)


def stored(shape, dtype):
    return pltpu.HBM(shape, dtype)


def from_hbm(*values):
    return [pltpu.with_memory_space_constraint(value, pltpu.HBM) for value in values]


def passed_along(value, by):
    peers = lax.axis_size("ctx")
    pairs = [(i, i + by) for i in range(peers) if 0 <= i + by < peers]
    return lax.ppermute(value, "ctx", pairs)


def summed_over_ctx(value):
    peers = lax.axis_size("ctx")

    def turned(value, stride):
        def to(i, by):
            at = i // stride % 4
            return i + ((at + by) % 4 - at) * stride

        return [value] + [
            lax.ppermute(value, "ctx", [(i, to(i, by)) for i in range(peers)])
            for by in (1, 2, 3)
        ]

    value = value + lax.ppermute(value, "ctx", [(i, i ^ 1) for i in range(peers)])
    own, one, two, three = turned(value, 2)
    return turned((own + one) + (two + three), 8)


def cost(micros):
    return pl.CostEstimate(
        flops=int(micros * 1e8), bytes_accessed=int(micros * 3e6), transcendentals=0
    )


def local(x_raw, bc_raw, dt_raw, conv_x, conv_bc, a_log, dt_bias, skip_weight, segment, grad_y):
    rows, channels = x_raw.shape
    heads = dt_raw.shape[1]
    steps = channels // BLK
    peers = lax.axis_size("ctx")
    shares = lax.axis_size("head")
    share = rows // shares
    params = pltpu.CompilerParams(vmem_limit_bytes=VMEM)
    rim = passed_along(jnp.concatenate([x_raw[rows - RIM :], bc_raw[rows - RIM :]], axis=1), 1)
    padded = jnp.concatenate([jnp.full((3,), -1, jnp.int32), segment])
    seg_ext = lax.dynamic_slice_in_dim(padded, lax.axis_index("ctx") * rows, rows + 3)
    seg = jnp.stack([seg_ext[min(k, 3) : min(k, 3) + rows] for k in range(8)]).astype(F32)
    hv = jnp.stack([a_log, dt_bias, skip_weight, skip_weight])
    row_spec = whole((8, heads, rows))
    square = whole((256, rows))
    by_channel = channel_rows(rows)

    def chan(dtype):
        return stored((channels, rows), dtype)

    xt, dyt, pre, taps, head_rows, bct, bcpre, bctaps = pl.pallas_call(
        prep_kernel,
        grid=(steps,),
        in_specs=[
            columns(rows), columns(rows), columns(4), whole((rows, 256)), whole((4, 256)),
            whole((heads, rows)), whole((4, heads)), whole((8, rows)),
        ],
        out_specs=[
            by_channel, by_channel, by_channel, channel_rows(128), row_spec,
            square, square, whole((256, 128)),
        ],
        out_shape=[
            chan(BF16), chan(BF16), shaped((channels, rows), F32), stored((channels, 128), F32),
            stored((8, heads, rows), F32), stored((256, rows), BF16), shaped((256, rows), F32),
            stored((256, 128), F32),
        ],
        compiler_params=params,
        cost_estimate=cost(4),
        name="prep",
    )(*from_hbm(x_raw, grad_y, conv_x, bc_raw, conv_bc, dt_raw.T), hv, seg)

    pay, xa, slope, eu, cdy, rimt, bctok, bcact, bcslope, bcrimt = pl.pallas_call(
        state_kernel,
        grid=(steps,),
        in_specs=[
            by_channel, columns(RIM), channel_rows(128), by_channel, row_spec,
            square, pl.BlockSpec((RIM, 256), lambda i: (0, channels // 256)), whole((256, 128)),
        ],
        out_specs=[
            pl.BlockSpec((8, 80, NS), lambda i: (i, 0, 0)),
            by_channel, by_channel, by_channel, by_channel, channel_rows(128),
            whole((rows, 256)), square, square, whole((256, 128)),
        ],
        out_shape=[
            shaped((peers, 80, NS), BF16), chan(BF16), chan(F32), chan(BF16), chan(BF16),
            stored((channels, 128), BF16), stored((rows, 256), BF16), stored((256, rows), BF16),
            stored((256, rows), F32), stored((256, 128), BF16),
        ],
        compiler_params=params,
        cost_estimate=cost(4),
        name="states",
    )(pre, rim, *from_hbm(taps, dyt, head_rows), bcpre, rim, *from_hbm(bctaps))

    got = lax.all_to_all(pay, "ctx", 0, 0, tiled=True)

    y_loc, du_loc, dbc = pl.pallas_call(
        block_kernel,
        grid=(steps,),
        in_specs=[
            by_channel, columns(rows), by_channel, row_spec, whole((rows, 256)), square,
        ],
        out_specs=[by_channel, by_channel, square],
        out_shape=[chan(F32), chan(F32), stored((256, rows), F32)],
        scratch_shapes=[
            pltpu.VMEM((rows, rows), F32), pltpu.VMEM((rows, rows), F32),
            pltpu.VMEM((steps, rows, PER), F32), pltpu.VMEM((rows, rows), F32),
        ],
        compiler_params=params,
        cost_estimate=cost(8),
        name="in_block",
    )(*from_hbm(xa, grad_y, dyt, head_rows, bctok, bcact))

    carried = pl.pallas_call(
        scan_kernel,
        in_specs=[pl.BlockSpec(memory_space=pltpu.VMEM)],
        out_specs=pl.BlockSpec(memory_space=pltpu.VMEM),
        out_shape=stored((peers, 64, NS), BF16),
        compiler_params=params,
        cost_estimate=cost(1),
        name="state_scan",
    )(*from_hbm(got))
    states = lax.all_to_all(carried, "ctx", 0, 0, tiled=True)

    state_spec = pl.BlockSpec((8, 64, NS), lambda i: (i, 0, 0))
    pay_bc = pl.pallas_call(
        bc_kernel,
        grid=(steps,),
        in_specs=[
            state_spec, by_channel, by_channel, square, square, square, whole((256, 128)),
            whole((256, 128)), row_spec,
        ],
        out_specs=whole((shares, share + 16, 256)),
        out_shape=shaped((shares, share + 16, 256), BF16),
        scratch_shapes=[pltpu.VMEM((256, rows), F32)],
        compiler_params=params,
        cost_estimate=cost(4),
        name="bc_part",
    )(states, *from_hbm(eu, cdy, dbc, bcslope, bct, bcrimt, bctaps, head_rows))
    got_bc = lax.all_to_all(pay_bc, "head", 0, 0, tiled=True)

    ssd_out, gx, last, spill, gw, grad_dt, gh = pl.pallas_call(
        x_kernel,
        grid=(steps,),
        in_specs=[
            state_spec, by_channel, by_channel, by_channel, by_channel, by_channel, by_channel,
            channel_rows(128), channel_rows(128), row_spec, whole((rows, 256)),
        ],
        out_specs=[
            columns(rows), columns(rows), columns(RIM), columns(RIM), columns(8),
            whole((heads, rows)), whole((8, 128)),
        ],
        out_shape=[
            stored((rows, channels), BF16), stored((rows, channels), BF16),
            stored((RIM, channels), F32), stored((RIM, channels), F32), stored((8, channels), F32),
            stored((heads, rows), F32), stored((8, 128), F32),
        ],
        scratch_shapes=[pltpu.VMEM((3, heads, rows), F32)],
        compiler_params=params,
        cost_estimate=cost(10),
        name="x_part",
    )(states, *from_hbm(xa, slope, y_loc, du_loc, xt, dyt, rimt, taps, head_rows, bctok))

    spill_x = passed_along(spill, -1)
    grad_x = pl.pallas_call(
        patch_kernel,
        grid=(1,),
        in_specs=[
            pl.BlockSpec(memory_space=pl.ANY), whole((RIM, channels)), whole((RIM, channels)),
        ],
        out_specs=pl.BlockSpec((RIM, channels), lambda i: (rows // RIM - 1, 0)),
        out_shape=stored((rows, channels), BF16),
        input_output_aliases={0: 0},
        compiler_params=params,
        cost_estimate=cost(1),
        name="last_rows",
    )(*from_hbm(gx, last), spill_x)

    vmem = pl.BlockSpec(memory_space=pltpu.VMEM)
    width = channels + 256 + 128
    sums, own_bc, spill_bc = pl.pallas_call(
        pack_kernel,
        in_specs=[vmem] * 3,
        out_specs=[vmem] * 3,
        out_shape=[shaped((8, width), F32), shaped((share, 256), F32), shaped((8, 256), F32)],
        compiler_params=params,
        cost_estimate=cost(1),
        name="pack_sums",
    )(got_bc, *from_hbm(gw, gh))
    spill_bc = passed_along(spill_bc, -1)
    parts = summed_over_ctx(sums)
    grad_wx, grad_wbc, grad_heads = pl.pallas_call(
        finish_kernel,
        in_specs=[vmem] * 4,
        out_specs=[vmem] * 3,
        out_shape=[stored((4, channels), F32), stored((4, 256), F32), stored((3, heads), F32)],
        compiler_params=params,
        cost_estimate=cost(1),
        name="finish_sums",
    )(*parts)
    is_last = lax.axis_index("head") == shares - 1
    grad_bc = own_bc + jnp.pad(jnp.where(is_last, spill_bc, 0.0), ((share - 8, 0), (0, 0)))
    return ssd_out, grad_x, grad_bc, grad_dt.T, grad_wx, grad_wbc, grad_heads


def solution(mesh):
    in_specs = (
        P("ctx", "head"), P("ctx", None), P("ctx", "head"), P(None, "head"), P(),
        P("head"), P("head"), P("head"), P(), P("ctx", "head"),
    )
    out_specs = (
        P("ctx", "head"), P("ctx", "head"), P(("ctx", "head"), None), P("ctx", "head"),
        P(None, "head"), P(), P(None, "head"),
    )
    return jax.shard_map(local, mesh=mesh, in_specs=in_specs, out_specs=out_specs, check_vma=False)
```

```python
import jax
import jax.numpy as jnp
from jax import lax
from jax.experimental import pallas as pl
from jax.experimental.pallas import tpu as pltpu
from jax.sharding import PartitionSpec as P

F32 = jnp.float32
BF16 = jnp.bfloat16

BLK = 256
HD = 64
NS = 128
RIM = 16
PER = BLK // HD
VMEM = 24 * 1024 * 1024

DT, CUMUL, CARRY, END, SIG, SKIP, RATE, MASK = range(8)


def mm(a, b):
    return lax.dot_general(a, b, (((1,), (0,)), ((), ())), preferred_element_type=F32)


def mm_nt(a, b):
    return lax.dot_general(a, b, (((1,), (1,)), ((), ())), preferred_element_type=F32)


def split(value, count):
    parts = []
    for _ in range(count):
        part = value.astype(BF16)
        parts.append(part)
        value = value - part.astype(F32)
    return parts


def pick_nt(pick, value, count):
    return sum(mm_nt(pick, part) for part in split(value, count))


def pick_right(value, pick, count):
    return sum(mm(part, pick) for part in split(value, count))


def iota(shape, dim):
    return lax.broadcasted_iota(jnp.int32, shape, dim)


def eye(n, dtype):
    return (iota((n, n), 0) == iota((n, n), 1)).astype(dtype)


def conv_own(raw, taps, masks):
    lane = iota((raw.shape[0], 128), 1)
    total = taps[:, 3:4] * raw
    for j in range(1, 4):
        rolled = pltpu.roll(raw, j, 1)
        shifted = jnp.concatenate(
            [jnp.where(lane < j, 0.0, rolled[:, :128]), rolled[:, 128:]], axis=1
        )
        total = total + shifted * (taps[:, 3 - j : 4 - j] * masks[3 - j])
    return total


def conv_rim(rim, taps, masks):
    lane = iota(rim.shape, 1)
    total = jnp.zeros(rim.shape, F32)
    for j in range(1, 4):
        before = jnp.where(lane < j, pltpu.roll(rim, j, 1), 0.0)
        total = total + before * (taps[:, 3 - j : 4 - j] * masks[3 - j][:, :128])
    return total


def conv_back(g, raw, rim, taps, masks):
    lane = iota((g.shape[0], 128), 1)
    grad = taps[:, 3:4] * g
    spill = jnp.zeros((g.shape[0], 128), F32)
    row = iota((8, 128), 0)

    def weight_row(k, product):
        return pick_nt((row == k).astype(BF16), product, 2)

    product = g * raw
    weights = weight_row(3, product[:, :128] + product[:, 128:])
    for j in range(1, 4):
        masked = g * masks[3 - j]
        rolled = pltpu.roll(masked, g.shape[1] - j, 1)
        wrapped = lane >= 128 - j
        first = rolled[:, :128]
        second = jnp.where(wrapped, 0.0, rolled[:, 128:])
        outer = jnp.where(wrapped, rolled[:, 128:], 0.0)
        tap = taps[:, 3 - j : 4 - j]
        grad = grad + tap * jnp.concatenate([first, second], axis=1)
        spill = spill + tap * outer
        weights = weights + weight_row(
            3 - j, first * raw[:, :128] + second * raw[:, 128:] + outer * rim
        )
    return grad, spill, weights


def wide_rim(rim):
    return jnp.concatenate([jnp.zeros((128 - RIM, rim.shape[1]), BF16), rim], axis=0)


def masks_of(rows_ref):
    return [rows_ref[MASK, k : k + 1, :] for k in range(4)]


def head_row(rows_ref, plane, head):
    return rows_ref[plane, pl.ds(head, 1), :]


def taps_of(ref):
    return pick_nt(eye(BLK, BF16), ref[...], 3)


def conv_all(raw_ref, rim_ref, w_ref, masks):
    ident = eye(BLK, BF16)
    raw = mm_nt(ident, raw_ref[...])
    rim = mm_nt(ident, wide_rim(rim_ref[...]))
    taps = taps_of(w_ref)
    pre = conv_own(raw, taps, masks)
    return raw, jnp.concatenate(
        [pre[:, :128] + conv_rim(rim, taps, masks), pre[:, 128:]], axis=1
    )


def sigmoid(value):
    return 1.0 / (1.0 + jnp.exp(-value))


def state_kernel(
    x_ref, rim_ref, gy_ref, wx_ref, bc_ref, rimbc_ref, wbc_ref, dt_ref, hv_ref, seg_ref,
    pay_ref, xa_ref, dyt_ref, rows_ref, bctok_ref, bcact_ref,
):
    step = pl.program_id(0)
    ident = eye(BLK, BF16)

    @pl.when(step == 0)
    def _():
        target = seg_ref[3:4, :]
        rows_ref[MASK] = jnp.concatenate(
            [(seg_ref[k : k + 1, :] == target).astype(F32) for k in range(4)]
            + [target, jnp.zeros((11, BLK), F32)],
            axis=0,
        )
        heads = dt_ref.shape[0]
        per_head = pick_nt(eye(heads, BF16), hv_ref[...], 3)
        rate = jnp.exp(per_head[:, 0:1])
        pre = dt_ref[...] + per_head[:, 1:2]
        dt = jnp.maximum(pre, 0.0) + jnp.log1p(jnp.exp(-jnp.abs(pre)))
        upto = (iota((BLK, BLK), 0) <= iota((BLK, BLK), 1)).astype(BF16)
        cumul = pick_right(-rate * dt, upto, 3)
        keep = (target == seg_ref[2:3, 0:1]).astype(F32)
        same_end = target == target[:, BLK - 1 :]
        rows_ref[DT] = dt
        rows_ref[CUMUL] = cumul
        rows_ref[CARRY] = keep * jnp.exp(cumul)
        rows_ref[END] = jnp.exp(jnp.where(same_end, cumul[:, BLK - 1 :] - cumul, -jnp.inf))
        rows_ref[SIG] = sigmoid(pre)
        rows_ref[SKIP] = jnp.broadcast_to(per_head[:, 2:3], (heads, BLK))
        rows_ref[RATE] = jnp.broadcast_to(rate, (heads, BLK))
        _, bcpre = conv_all(bc_ref, rimbc_ref, wbc_ref, masks_of(rows_ref))
        act = (bcpre * sigmoid(bcpre)).astype(BF16)
        bcact_ref[...] = act
        bctok_ref[...] = mm_nt(ident, act).astype(BF16)

    _, pre = conv_all(x_ref, rim_ref, wx_ref, masks_of(rows_ref))
    act = (pre * sigmoid(pre)).astype(BF16)
    xa_ref[...] = act
    act = act.astype(F32)
    dy = mm_nt(ident, gy_ref[...])
    dyt_ref[...] = dy.astype(BF16)
    ends, carries = [], []
    for k in range(PER):
        head = step * PER + k
        lo, hi = k * HD, (k + 1) * HD
        carry = head_row(rows_ref, CARRY, head)
        weight = head_row(rows_ref, END, head) * head_row(rows_ref, DT, head)
        ends.append((weight * act[lo:hi]).astype(BF16))
        carries.append((carry * dy[lo:hi]).astype(BF16))
        parts = split(carry[:, BLK - 1 :], 3)
        which = iota((8, NS), 0)
        through = jnp.where(
            which == 0, parts[0].astype(F32),
            jnp.where(which == 1, parts[1].astype(F32), parts[2].astype(F32)),
        ).astype(BF16)
        pay_ref[2 * k, 64:72, :] = through
        pay_ref[2 * k + 1, 64:72, :] = through
    state = mm(jnp.concatenate(ends, axis=0), bctok_ref[:, :NS]).astype(BF16)
    back = mm(jnp.concatenate(carries, axis=0), bctok_ref[:, NS:]).astype(BF16)
    for j in range(2 * PER):
        pay_ref[j, 0:32, :] = state[j * 32 : j * 32 + 32]
        pay_ref[j, 32:64, :] = back[j * 32 : j * 32 + 32]


def slope_kernel(
    x_ref, rim_ref, wx_ref, bc_ref, rimbc_ref, wbc_ref, xa_ref, dyt_ref, rows_ref,
    xt_ref, slope_ref, eu_ref, cdy_ref, bct_ref, bcslope_ref,
):
    step = pl.program_id(0)
    masks = masks_of(rows_ref)

    def slope_of(pre):
        sig = sigmoid(pre)
        return sig * (1.0 + pre * (1.0 - sig))

    @pl.when(step == 0)
    def _():
        raw, pre = conv_all(bc_ref, rimbc_ref, wbc_ref, masks)
        bct_ref[...] = raw.astype(BF16)
        bcslope_ref[...] = slope_of(pre)

    raw, pre = conv_all(x_ref, rim_ref, wx_ref, masks)
    xt_ref[...] = raw.astype(BF16)
    slope_ref[...] = slope_of(pre)
    for k in range(PER):
        head = step * PER + k
        lo, hi = k * HD, (k + 1) * HD
        weight = head_row(rows_ref, END, head) * head_row(rows_ref, DT, head)
        eu_ref[lo:hi, :] = (weight * xa_ref[lo:hi, :].astype(F32)).astype(BF16)
        carry = head_row(rows_ref, CARRY, head)
        cdy_ref[lo:hi, :] = (carry * dyt_ref[lo:hi, :].astype(F32)).astype(BF16)


def block_kernel(
    xa_ref, gy_ref, dyt_ref, rows_ref, bctok_ref, bcact_ref, slope_ref,
    y_ref, g_ref, ends_ref, red_ref, dbc_ref,
    scores_ref, link_ref, acol_ref, dg_ref, yt_ref, du_ref,
):
    step = pl.program_id(0)

    @pl.when(step == 0)
    def _():
        ident = eye(BLK, BF16)
        scores_ref[...] = mm_nt(bctok_ref[:, NS:], bctok_ref[:, :NS])
        seg_row = rows_ref[MASK, 4:5, :]
        seg_col = mm_nt(ident, rows_ref[MASK].astype(BF16))[:, 4:5]
        later = iota((BLK, BLK), 0) >= iota((BLK, BLK), 1)
        linked = jnp.logical_and(later, seg_col == seg_row)
        link_ref[...] = jnp.where(linked, 0.0, -jnp.inf)
        dg_ref[...] = jnp.zeros_like(dg_ref)
        cumul = pick_nt(ident, rows_ref[CUMUL], 3)
        for at in range(acol_ref.shape[0]):
            acol_ref[at] = cumul[:, at * PER : (at + 1) * PER]

    acols = acol_ref[step]
    for k in range(PER):
        head = step * PER + k
        lo, hi = k * HD, (k + 1) * HD
        arow = head_row(rows_ref, CUMUL, head)
        dt = head_row(rows_ref, DT, head)
        skip = head_row(rows_ref, SKIP, head)
        u_low = (dt * xa_ref[lo:hi, :].astype(F32)).astype(BF16)
        du_first = None
        for tb in range(2):
            t0, t1 = tb * 128, tb * 128 + 128
            decay = jnp.exp(acols[t0:t1, k : k + 1] - arow[:, :t1] + link_ref[t0:t1, :t1])
            mixed = (decay * scores_ref[t0:t1, :t1]).astype(BF16)
            yt_ref[:, t0:t1] = mm_nt(u_low[:, :t1], mixed)
            du = mm(dyt_ref[lo:hi, t0:t1], mixed)
            if tb == 0:
                du_first = du
            else:
                du_ref[:, :128] = du_first + du[:, :128]
                du_ref[:, 128:] = du[:, 128:]
            dmix = mm(gy_ref[t0:t1, lo:hi], u_low[:, :t1])
            dg_ref[t0:t1, :t1] += decay * dmix
        x_h = xa_ref[lo:hi, :].astype(F32)
        dy_h = dyt_ref[lo:hi, :].astype(F32)
        y_h = yt_ref[...]
        du_h = du_ref[...]
        slope = slope_ref[lo:hi, :]
        y_ref[lo:hi, :] = y_h + skip * x_h
        g_ref[lo:hi, :] = slope * (dt * du_h + skip * dy_h)
        ends_ref[lo:hi, :] = slope * (dt * head_row(rows_ref, END, head))
        ga = jnp.sum(dy_h * y_h - u_low.astype(F32) * du_h, axis=0, keepdims=True)
        red_ref[0, pl.ds(head, 1), :] = ga
        red_ref[1, pl.ds(head, 1), :] = jnp.sum(x_h * du_h, axis=0, keepdims=True)
        red_ref[2, pl.ds(head, 1), :] = jnp.sum(x_h * dy_h, axis=0, keepdims=True)

    @pl.when(step == pl.num_programs(0) - 1)
    def _():
        dg = dg_ref[...].astype(BF16)
        dbc_ref[:NS, :] = mm(bcact_ref[NS:, :], dg)
        dbc_ref[NS:, :] = mm_nt(bcact_ref[:NS, :], dg)


def scan_kernel(in_ref, out_ref):
    peers = in_ref.shape[0]
    ahead = jnp.zeros((32, NS), F32)
    behind = jnp.zeros((32, NS), F32)

    def through(at):
        parts = in_ref[at, 64:72, :].astype(F32)
        return parts[0:1] + parts[1:2] + parts[2:3]

    for i in range(peers):
        out_ref[i, 0:32, :] = ahead.astype(BF16)
        ahead = through(i) * ahead + in_ref[i, 0:32, :].astype(F32)
        at = peers - 1 - i
        out_ref[at, 32:64, :] = behind.astype(BF16)
        behind = through(at) * behind + in_ref[at, 32:64, :].astype(F32)


def bc_kernel(
    state_ref, eu_ref, cdy_ref, dbc_ref, bcslope_ref, bct_ref, rimbc_ref, wbc_ref, rows_ref,
    pay_ref,
    acc_ref,
):
    step = pl.program_id(0)

    @pl.when(step == 0)
    def _():
        acc_ref[...] = dbc_ref[...]

    small = eye(NS, BF16)
    state_in = state_ref[:, 0:32, :].reshape(BLK, NS)
    state_back = state_ref[:, 32:64, :].reshape(BLK, NS)
    acc_ref[:NS, :] += mm(mm_nt(small, state_back).astype(BF16), eu_ref[...])
    acc_ref[NS:, :] += mm(mm_nt(small, state_in).astype(BF16), cdy_ref[...])

    @pl.when(step == pl.num_programs(0) - 1)
    def _():
        grad, spill, weights = conv_back(
            acc_ref[...] * bcslope_ref[...], bct_ref[...].astype(F32),
            mm_nt(eye(BLK, BF16), wide_rim(rimbc_ref[...])), taps_of(wbc_ref), masks_of(rows_ref),
        )
        token = mm_nt(eye(BLK, BF16), grad.astype(BF16)).astype(BF16)
        last8 = (iota((8, 128), 0) + 120 == iota((8, 128), 1)).astype(BF16)
        rest = jnp.concatenate([weights, mm_nt(last8, spill.astype(BF16))], axis=0).astype(BF16)
        shares = pay_ref.shape[0]
        share = BLK // shares
        for j in range(shares):
            pay_ref[j, 0:share, :] = token[j * share : (j + 1) * share]
            pay_ref[j, share : share + 16, :] = rest


def x_kernel(
    state_ref, xa_ref, y_ref, g_ref, ends_ref, xt_ref, dyt_ref, rim_ref, wx_ref, rows_ref,
    bctok_ref, local_ref,
    out_ref, gx_ref, last_ref, spill_ref, gw_ref, gdt_ref, gh_ref,
    red_ref,
):
    step = pl.program_id(0)
    ident = eye(BLK, BF16)
    masks = masks_of(rows_ref)
    state_in = state_ref[:, 0:32, :].reshape(BLK, NS)
    state_back = state_ref[:, 32:64, :].reshape(BLK, NS)
    carried = mm_nt(state_in, bctok_ref[:, NS:])
    from_end = mm_nt(state_back, bctok_ref[:, :NS])
    both = state_in.astype(F32) * state_back.astype(F32)
    last_lane = iota((1, BLK), 1) == BLK - 1
    y_parts = []
    for k in range(PER):
        head = step * PER + k
        lo, hi = k * HD, (k + 1) * HD
        dt = head_row(rows_ref, DT, head)
        carry = head_row(rows_ref, CARRY, head)
        end = head_row(rows_ref, END, head)
        x_h = xa_ref[lo:hi, :].astype(F32)
        add = carry * carried[lo:hi]
        u_low = (dt * x_h).astype(BF16).astype(F32)
        fed = jnp.sum(u_low * from_end[lo:hi], axis=0, keepdims=True) * end
        at_end = jnp.sum(fed, axis=1, keepdims=True)
        joint = jnp.sum(jnp.sum(both[lo:hi], axis=0, keepdims=True), axis=1, keepdims=True)
        at_end = at_end + carry[:, BLK - 1 :] * joint
        ga = jnp.sum(dyt_ref[lo:hi, :].astype(F32) * add, axis=0, keepdims=True) - fed
        red_ref[0, pl.ds(head, 1), :] = ga + jnp.where(last_lane, at_end, 0.0)
        red_ref[1, pl.ds(head, 1), :] = end * jnp.sum(
            x_h * from_end[lo:hi], axis=0, keepdims=True
        )
        y_parts.append((y_ref[lo:hi, :] + add).astype(BF16))
    out_ref[...] = mm_nt(ident, jnp.concatenate(y_parts, axis=0)).astype(BF16)
    grad, spill, weights = conv_back(
        g_ref[...] + ends_ref[...] * from_end, xt_ref[...].astype(F32),
        mm_nt(ident, wide_rim(rim_ref[...])), taps_of(wx_ref), masks,
    )
    gx_ref[...] = mm_nt(ident, grad.astype(BF16)).astype(BF16)
    pick = (iota((RIM, 128), 0) + (128 - RIM) == iota((RIM, 128), 1)).astype(BF16)
    last_ref[...] = pick_nt(pick, grad[:, 128:], 2)
    spill_ref[...] = pick_nt(pick, spill, 2)
    gw_ref[...] = weights

    @pl.when(step == pl.num_programs(0) - 1)
    def _():
        later = (iota((BLK, BLK), 0) >= iota((BLK, BLK), 1)).astype(BF16)
        grad_log = pick_right(local_ref[0] + red_ref[0], later, 3)
        rate = rows_ref[RATE]
        grad_step = (local_ref[1] + red_ref[1] - rate * grad_log) * rows_ref[SIG]
        gdt_ref[...] = grad_step
        which = iota((8, BLK), 0)
        terms = (-rate * rows_ref[DT] * grad_log, grad_step, local_ref[2])
        gh_ref[...] = jnp.zeros_like(gh_ref)
        gh_ref[:, : rate.shape[0]] = sum(
            pick_nt((which == k).astype(BF16), term, 3) for k, term in enumerate(terms)
        )


def patch_kernel(gx_ref, last_ref, own_ref, spill_ref, out_ref, bc_ref):
    del gx_ref
    width = last_ref.shape[1]
    out_ref[...] = (last_ref[...] + spill_ref[:, :width]).astype(BF16)
    share = own_ref.shape[0]
    bc_ref[: share - 8, :] = own_ref[: share - 8, :]
    is_last = lax.axis_index("head") == lax.axis_size("head") - 1
    came = spill_ref[RIM - 8 :, width:]
    bc_ref[share - 8 :, :] = own_ref[share - 8 :, :] + jnp.where(is_last, came, 0.0)


def pack_kernel(got_ref, gw_ref, gh_ref, spill_ref, sums_ref, own_ref, out_ref):
    share = own_ref.shape[0]
    total = jnp.sum(got_ref[...].astype(F32), axis=0)
    own_ref[...] = total[:share]
    width = gw_ref.shape[1]
    out_ref[:, :width] = spill_ref[...]
    out_ref[: RIM - 8, width:] = jnp.zeros((RIM - 8, 256), F32)
    out_ref[RIM - 8 :, width:] = total[share + 8 :]
    sums_ref[:, :width] = gw_ref[...]
    sums_ref[:, width : width + 256] = total[share : share + 8]
    sums_ref[:, width + 256 :] = gh_ref[...]


def finish_kernel(a_ref, b_ref, c_ref, d_ref, wx_ref, wbc_ref, heads_ref):
    total = (a_ref[...] + b_ref[...]) + (c_ref[...] + d_ref[...])
    width = wx_ref.shape[1]
    wx_ref[...] = total[:4, :width]
    wbc_ref[...] = total[:4, width : width + 256]
    heads_ref[...] = total[:3, width + 256 : width + 256 + heads_ref.shape[1]]


def whole(shape):
    zeros = (0,) * len(shape)
    return pl.BlockSpec(shape, lambda *_: zeros)


def columns(rows):
    return pl.BlockSpec((rows, BLK), lambda i: (0, i))


def channel_rows(width):
    return pl.BlockSpec((BLK, width), lambda i: (i, 0))


def shaped(shape, dtype):
    return jax.ShapeDtypeStruct(shape, dtype)


def stored(shape, dtype):
    return pltpu.HBM(shape, dtype)


def from_hbm(*values):
    return [pltpu.with_memory_space_constraint(value, pltpu.HBM) for value in values]


def passed_along(value, by):
    peers = lax.axis_size("ctx")
    pairs = [(i, i + by) for i in range(peers) if 0 <= i + by < peers]
    return lax.ppermute(value, "ctx", pairs)


def summed_over_ctx(value):
    peers = lax.axis_size("ctx")

    def turned(value, stride):
        def to(i, by):
            at = i // stride % 4
            return i + ((at + by) % 4 - at) * stride

        return [value] + [
            lax.ppermute(value, "ctx", [(i, to(i, by)) for i in range(peers)])
            for by in (1, 2, 3)
        ]

    value = value + lax.ppermute(value, "ctx", [(i, i ^ 1) for i in range(peers)])
    own, one, two, three = turned(value, 2)
    return turned((own + one) + (two + three), 8)


def cost(micros):
    return pl.CostEstimate(
        flops=int(micros * 1e8), bytes_accessed=int(micros * 3e6), transcendentals=0
    )


def local(x_raw, bc_raw, dt_raw, conv_x, conv_bc, a_log, dt_bias, skip_weight, segment, grad_y):
    rows, channels = x_raw.shape
    heads = dt_raw.shape[1]
    steps = channels // BLK
    peers = lax.axis_size("ctx")
    shares = lax.axis_size("head")
    share = rows // shares
    params = pltpu.CompilerParams(vmem_limit_bytes=VMEM)
    rim = passed_along(jnp.concatenate([x_raw[rows - RIM :], bc_raw[rows - RIM :]], axis=1), 1)
    padded = jnp.concatenate([jnp.full((3,), -1, jnp.int32), segment])
    seg_ext = lax.dynamic_slice_in_dim(padded, lax.axis_index("ctx") * rows, rows + 3)
    seg = jnp.stack([seg_ext[min(k, 3) : min(k, 3) + rows] for k in range(8)]).astype(F32)
    hv = jnp.stack([a_log, dt_bias, skip_weight, skip_weight])
    row_spec = whole((8, heads, rows))
    square = whole((256, rows))
    by_channel = channel_rows(rows)

    def chan(dtype):
        return stored((channels, rows), dtype)

    rim_bc_spec = pl.BlockSpec((RIM, 256), lambda i: (0, channels // 256))
    local_spec = whole((3, heads, rows))

    pay, xa, dyt, head_rows, bctok, bcact = pl.pallas_call(
        state_kernel,
        grid=(steps,),
        in_specs=[
            columns(rows), columns(RIM), columns(rows), columns(4),
            whole((rows, 256)), rim_bc_spec, whole((4, 256)),
            whole((heads, rows)), whole((4, heads)), whole((8, rows)),
        ],
        out_specs=[
            pl.BlockSpec((8, 72, NS), lambda i: (i, 0, 0)),
            by_channel, by_channel, row_spec, whole((rows, 256)), square,
        ],
        out_shape=[
            shaped((peers, 72, NS), BF16), chan(BF16), chan(BF16),
            stored((8, heads, rows), F32), stored((rows, 256), BF16), stored((256, rows), BF16),
        ],
        compiler_params=params,
        cost_estimate=cost(7),
        name="states",
    )(
        *from_hbm(x_raw), rim, *from_hbm(grad_y, conv_x, bc_raw), rim,
        *from_hbm(conv_bc, dt_raw.T), hv, seg,
    )

    got = lax.all_to_all(pay, "ctx", 0, 0, tiled=True)

    xt, slope, eu, cdy, bct, bcslope = pl.pallas_call(
        slope_kernel,
        grid=(steps,),
        in_specs=[
            columns(rows), columns(RIM), columns(4), whole((rows, 256)), rim_bc_spec,
            whole((4, 256)), by_channel, by_channel, row_spec,
        ],
        out_specs=[by_channel, by_channel, by_channel, by_channel, square, square],
        out_shape=[
            chan(BF16), chan(F32), chan(BF16), chan(BF16),
            stored((256, rows), BF16), stored((256, rows), F32),
        ],
        compiler_params=params,
        cost_estimate=cost(6),
        name="slopes",
    )(*from_hbm(x_raw, rim, conv_x, bc_raw, rim, conv_bc, xa, dyt, head_rows))
    got, xt = lax.optimization_barrier((got, xt))

    carried = pl.pallas_call(
        scan_kernel,
        in_specs=[pl.BlockSpec(memory_space=pltpu.VMEM)],
        out_specs=pl.BlockSpec(memory_space=pltpu.VMEM),
        out_shape=shaped((peers, 64, NS), BF16),
        compiler_params=params,
        cost_estimate=cost(1),
        name="state_scan",
    )(got)
    states = lax.all_to_all(carried, "ctx", 0, 0, tiled=True)

    y_loc, g_loc, ends, red_loc, dbc = pl.pallas_call(
        block_kernel,
        grid=(steps,),
        in_specs=[
            by_channel, columns(rows), by_channel, row_spec, whole((rows, 256)), square,
            by_channel,
        ],
        out_specs=[by_channel, by_channel, by_channel, local_spec, square],
        out_shape=[
            chan(F32), chan(F32), chan(F32), stored((3, heads, rows), F32),
            stored((256, rows), F32),
        ],
        scratch_shapes=[
            pltpu.VMEM((rows, rows), F32), pltpu.VMEM((rows, rows), F32),
            pltpu.VMEM((steps, rows, PER), F32), pltpu.VMEM((rows, rows), F32),
            pltpu.VMEM((HD, rows), F32), pltpu.VMEM((HD, rows), F32),
        ],
        compiler_params=params,
        cost_estimate=cost(8),
        name="in_block",
    )(*from_hbm(xa, grad_y, dyt, head_rows, bctok, bcact, slope))

    state_spec = pl.BlockSpec((8, 64, NS), lambda i: (i, 0, 0))
    pay_bc = pl.pallas_call(
        bc_kernel,
        grid=(steps,),
        in_specs=[
            state_spec, by_channel, by_channel, square, square, square, rim_bc_spec,
            whole((4, 256)), row_spec,
        ],
        out_specs=whole((shares, share + 16, 256)),
        out_shape=shaped((shares, share + 16, 256), BF16),
        scratch_shapes=[pltpu.VMEM((256, rows), F32)],
        compiler_params=params,
        cost_estimate=cost(4),
        name="bc_part",
    )(states, *from_hbm(eu, cdy, dbc, bcslope, bct, rim, conv_bc, head_rows))
    got_bc = lax.all_to_all(pay_bc, "head", 0, 0, tiled=True)

    ssd_out, gx, last, spill, gw, grad_dt, gh = pl.pallas_call(
        x_kernel,
        grid=(steps,),
        in_specs=[
            state_spec, by_channel, by_channel, by_channel, by_channel, by_channel, by_channel,
            columns(RIM), columns(4), row_spec, whole((rows, 256)), local_spec,
        ],
        out_specs=[
            columns(rows), columns(rows), columns(RIM), columns(RIM), columns(8),
            whole((heads, rows)), whole((8, 128)),
        ],
        out_shape=[
            stored((rows, channels), BF16), stored((rows, channels), BF16),
            stored((RIM, channels), F32), stored((RIM, channels), F32), stored((8, channels), F32),
            stored((heads, rows), F32), stored((8, 128), F32),
        ],
        scratch_shapes=[pltpu.VMEM((2, heads, rows), F32)],
        compiler_params=params,
        cost_estimate=cost(10),
        name="x_part",
    )(
        states,
        *from_hbm(xa, y_loc, g_loc, ends, xt, dyt, rim, conv_x, head_rows, bctok, red_loc),
    )

    vmem = pl.BlockSpec(memory_space=pltpu.VMEM)
    width = channels + 256 + 128
    sums, own_bc, spills = pl.pallas_call(
        pack_kernel,
        in_specs=[vmem] * 4,
        out_specs=[vmem] * 3,
        out_shape=[
            shaped((8, width), F32), shaped((share, 256), F32),
            shaped((RIM, channels + 256), F32),
        ],
        compiler_params=params,
        cost_estimate=cost(1),
        name="pack_sums",
    )(got_bc, *from_hbm(gw, gh, spill))
    parts = summed_over_ctx(sums)
    spills = passed_along(spills, -1)
    grad_x, grad_bc = pl.pallas_call(
        patch_kernel,
        grid=(1,),
        in_specs=[
            pl.BlockSpec(memory_space=pl.ANY), whole((RIM, channels)), whole((share, 256)),
            whole((RIM, channels + 256)),
        ],
        out_specs=[
            pl.BlockSpec((RIM, channels), lambda i: (rows // RIM - 1, 0)), whole((share, 256)),
        ],
        out_shape=[stored((rows, channels), BF16), stored((share, 256), F32)],
        input_output_aliases={0: 0},
        compiler_params=params,
        cost_estimate=cost(1),
        name="last_rows",
    )(*from_hbm(gx, last), own_bc, spills)
    grad_wx, grad_wbc, grad_heads = pl.pallas_call(
        finish_kernel,
        in_specs=[vmem] * 4,
        out_specs=[vmem] * 3,
        out_shape=[stored((4, channels), F32), stored((4, 256), F32), stored((3, heads), F32)],
        compiler_params=params,
        cost_estimate=cost(1),
        name="finish_sums",
    )(*parts)
    return ssd_out, grad_x, grad_bc, grad_dt.T, grad_wx, grad_wbc, grad_heads


def solution(mesh):
    in_specs = (
        P("ctx", "head"), P("ctx", None), P("ctx", "head"), P(None, "head"), P(),
        P("head"), P("head"), P("head"), P(), P("ctx", "head"),
    )
    out_specs = (
        P("ctx", "head"), P("ctx", "head"), P(("ctx", "head"), None), P("ctx", "head"),
        P(None, "head"), P(), P(None, "head"),
    )
    return jax.shard_map(local, mesh=mesh, in_specs=in_specs, out_specs=out_specs, check_vma=False)
```

```python
import jax
import jax.numpy as jnp
from jax import lax
from jax.experimental import pallas as pl
from jax.experimental.pallas import tpu as pltpu
from jax.sharding import PartitionSpec as P

F32 = jnp.float32
BF16 = jnp.bfloat16

BLK = 256
HD = 64
NS = 128
RIM = 16
PER = BLK // HD
VMEM = 24 * 1024 * 1024

DT, CUMUL, CARRY, END, SIG, SKIP, RATE, MASK = range(8)


def mm(a, b):
    return lax.dot_general(a, b, (((1,), (0,)), ((), ())), preferred_element_type=F32)


def mm_nt(a, b):
    return lax.dot_general(a, b, (((1,), (1,)), ((), ())), preferred_element_type=F32)


def split(value, count):
    parts = []
    for _ in range(count):
        part = value.astype(BF16)
        parts.append(part)
        value = value - part.astype(F32)
    return parts


def pick_nt(pick, value, count):
    return sum(mm_nt(pick, part) for part in split(value, count))


def pick_right(value, pick, count):
    return sum(mm(part, pick) for part in split(value, count))


def iota(shape, dim):
    return lax.broadcasted_iota(jnp.int32, shape, dim)


def eye(n, dtype):
    return (iota((n, n), 0) == iota((n, n), 1)).astype(dtype)


def conv_own(raw, taps, masks):
    lane = iota((raw.shape[0], 128), 1)
    total = taps[:, 3:4] * raw
    for j in range(1, 4):
        rolled = pltpu.roll(raw, j, 1)
        shifted = jnp.concatenate(
            [jnp.where(lane < j, 0.0, rolled[:, :128]), rolled[:, 128:]], axis=1
        )
        total = total + shifted * (taps[:, 3 - j : 4 - j] * masks[3 - j])
    return total


def conv_rim(rim, taps, masks):
    lane = iota(rim.shape, 1)
    total = jnp.zeros(rim.shape, F32)
    for j in range(1, 4):
        before = jnp.where(lane < j, pltpu.roll(rim, j, 1), 0.0)
        total = total + before * (taps[:, 3 - j : 4 - j] * masks[3 - j][:, :128])
    return total


def conv_back(g, raw, rim, taps, masks):
    lane = iota((g.shape[0], 128), 1)
    grad = taps[:, 3:4] * g
    spill = jnp.zeros((g.shape[0], 128), F32)
    product = g * raw
    products = [None, None, None, product[:, :128] + product[:, 128:]]
    for j in range(1, 4):
        masked = g * masks[3 - j]
        rolled = pltpu.roll(masked, g.shape[1] - j, 1)
        wrapped = lane >= 128 - j
        first = rolled[:, :128]
        second = jnp.where(wrapped, 0.0, rolled[:, 128:])
        outer = jnp.where(wrapped, rolled[:, 128:], 0.0)
        tap = taps[:, 3 - j : 4 - j]
        grad = grad + tap * jnp.concatenate([first, second], axis=1)
        spill = spill + tap * outer
        products[3 - j] = first * raw[:, :128] + second * raw[:, 128:] + outer * rim
    chosen = (iota((512, 128), 0) // 128 == iota((512, 128), 1)).astype(BF16)
    sums = pick_right(jnp.concatenate(products, axis=1), chosen, 2)
    moved = pltpu.roll(spill, 128 - RIM, 1)
    sides = jnp.where(lane >= 128 - RIM, grad[:, 128:], jnp.where(lane >= 96, moved, sums))
    return grad, sides


def wide_rim(rim):
    return jnp.concatenate([jnp.zeros((128 - RIM, rim.shape[1]), BF16), rim], axis=0)


def masks_of(rows_ref):
    return [rows_ref[MASK, k : k + 1, :] for k in range(4)]


def head_row(rows_ref, plane, head):
    return rows_ref[plane, pl.ds(head, 1), :]


def taps_of(w):
    padded = jnp.concatenate([w, jnp.zeros((124, BLK), F32)], axis=0)
    return jnp.transpose(padded)


def conv_all(raw_ref, rim_ref, taps, masks):
    ident = eye(BLK, BF16)
    raw = mm_nt(ident, raw_ref[...])
    rim = mm_nt(ident, wide_rim(rim_ref[...]))
    pre = conv_own(raw, taps, masks)
    pre = jnp.concatenate([pre[:, :128] + conv_rim(rim, taps, masks), pre[:, 128:]], axis=1)
    return raw, rim, pre


def with_taps(rim, taps):
    return jnp.where(iota(rim.shape, 1) < 4, taps, rim)


def sigmoid(value):
    return 1.0 / (1.0 + jnp.exp(-value))


def rim_kernel(x_ref, bc_ref, out_ref, sems):
    rows, width = x_ref.shape
    copies = [
        pltpu.make_async_copy(
            x_ref.at[pl.ds(rows - RIM, RIM), :], out_ref.at[:, pl.ds(0, width)], sems.at[0]
        ),
        pltpu.make_async_copy(
            bc_ref.at[pl.ds(rows - RIM, RIM), :],
            out_ref.at[:, pl.ds(width, bc_ref.shape[1])],
            sems.at[1],
        ),
    ]
    for copy in copies:
        copy.start()
    for copy in copies:
        copy.wait()


def head_rows_of(rows_ref, seg_ref, rate_ref, bias_ref, skip_ref, dt_ref):
    here = lax.axis_index("ctx")
    own = [seg_ref[pl.ds(2 * here + half, 1), :] for half in range(2)]
    target = jnp.concatenate(own, axis=1).astype(F32)
    before = seg_ref[pl.ds(jnp.maximum(2 * here - 1, 0), 1), :].astype(F32)
    before = jnp.where(here == 0, -1.0, before)
    lane = iota((1, 128), 1)
    masks = []
    for j in (3, 2, 1):
        rolled = pltpu.roll(target, j, 1)
        first = jnp.where(lane < j, pltpu.roll(before, j, 1), rolled[:, :128])
        shifted = jnp.concatenate([first, rolled[:, 128:]], axis=1)
        masks.append((shifted == target).astype(F32))
    rows_ref[MASK] = jnp.concatenate(
        masks + [jnp.ones((1, BLK), F32), target, jnp.zeros((11, BLK), F32)], axis=0
    )
    heads = dt_ref.shape[0]
    values = jnp.concatenate(
        [rate_ref[...], bias_ref[...], skip_ref[...], jnp.zeros((5, heads), F32)], axis=0
    )
    per_head = pick_nt(eye(heads, BF16), values, 3)
    rate = jnp.exp(per_head[:, 0:1])
    pre = dt_ref[...] + per_head[:, 1:2]
    dt = jnp.maximum(pre, 0.0) + jnp.log1p(jnp.exp(-jnp.abs(pre)))
    upto = (iota((BLK, BLK), 0) <= iota((BLK, BLK), 1)).astype(BF16)
    cumul = pick_right(-rate * dt, upto, 3)
    keep = (target == before[:, 127:]).astype(F32)
    same_end = target == target[:, BLK - 1 :]
    rows_ref[DT] = dt
    rows_ref[CUMUL] = cumul
    rows_ref[CARRY] = keep * jnp.exp(cumul)
    rows_ref[END] = jnp.exp(jnp.where(same_end, cumul[:, BLK - 1 :] - cumul, -jnp.inf))
    rows_ref[SIG] = sigmoid(pre)
    rows_ref[SKIP] = jnp.broadcast_to(per_head[:, 2:3], (heads, BLK))
    rows_ref[RATE] = jnp.broadcast_to(rate, (heads, BLK))


def state_kernel(
    x_ref, rim_ref, gy_ref, wx_ref, bc_ref, rimbc_ref, wbc_ref, seg_ref, rate_ref, bias_ref,
    skip_ref, dt_ref,
    pay_ref, rows_ref, bctok_ref,
):
    step = pl.program_id(0)
    ident = eye(BLK, BF16)

    @pl.when(step == 0)
    def _():
        head_rows_of(rows_ref, seg_ref, rate_ref, bias_ref, skip_ref, dt_ref)
        _, _, pre = conv_all(bc_ref, rimbc_ref, taps_of(wbc_ref[...]), masks_of(rows_ref))
        bctok_ref[...] = mm_nt(ident, (pre * sigmoid(pre)).astype(BF16)).astype(BF16)

    _, _, pre = conv_all(x_ref, rim_ref, taps_of(wx_ref[...]), masks_of(rows_ref))
    act = (pre * sigmoid(pre)).astype(BF16).astype(F32)
    dy = mm_nt(ident, gy_ref[...])
    ends, carries = [], []
    for k in range(PER):
        head = step * PER + k
        lo, hi = k * HD, (k + 1) * HD
        carry = head_row(rows_ref, CARRY, head)
        weight = head_row(rows_ref, END, head) * head_row(rows_ref, DT, head)
        ends.append((weight * act[lo:hi]).astype(BF16))
        carries.append((carry * dy[lo:hi]).astype(BF16))
        parts = split(carry[:, BLK - 1 :], 3)
        which = iota((8, NS), 0)
        through = jnp.where(
            which == 0, parts[0].astype(F32),
            jnp.where(which == 1, parts[1].astype(F32), parts[2].astype(F32)),
        ).astype(BF16)
        pay_ref[2 * k, 64:72, :] = through
        pay_ref[2 * k + 1, 64:72, :] = through
    state = mm(jnp.concatenate(ends, axis=0), bctok_ref[:, :NS]).astype(BF16)
    back = mm(jnp.concatenate(carries, axis=0), bctok_ref[:, NS:]).astype(BF16)
    for j in range(2 * PER):
        pay_ref[j, 0:32, :] = state[j * 32 : j * 32 + 32]
        pay_ref[j, 32:64, :] = back[j * 32 : j * 32 + 32]


def slope_kernel(
    x_ref, rim_ref, gy_ref, wx_ref, bc_ref, rimbc_ref, wbc_ref, rows_ref,
    low_ref, slope_ref, scaled_ref, sides_ref, bclow_ref, bcslope_ref, bcsides_ref,
):
    step = pl.program_id(0)
    masks = masks_of(rows_ref)

    @pl.when(step == 0)
    def _():
        taps = taps_of(wbc_ref[...])
        raw, rim, pre = conv_all(bc_ref, rimbc_ref, taps, masks)
        bcsides_ref[...] = with_taps(rim, taps)
        sig = sigmoid(pre)
        bclow_ref[0] = raw.astype(BF16)
        bclow_ref[1] = (pre * sig).astype(BF16)
        bcslope_ref[...] = sig * (1.0 + pre * (1.0 - sig))

    taps = taps_of(wx_ref[...])
    raw, rim, pre = conv_all(x_ref, rim_ref, taps, masks)
    sides_ref[...] = with_taps(rim, taps)
    sig = sigmoid(pre)
    slope_ref[...] = sig * (1.0 + pre * (1.0 - sig))
    low = (pre * sig).astype(BF16)
    dy = mm_nt(eye(BLK, BF16), gy_ref[...])
    low_ref[0] = low
    low_ref[1] = dy.astype(BF16)
    low_ref[2] = raw.astype(BF16)
    act = low.astype(F32)
    for k in range(PER):
        head = step * PER + k
        lo, hi = k * HD, (k + 1) * HD
        weight = head_row(rows_ref, END, head) * head_row(rows_ref, DT, head)
        scaled_ref[0, lo:hi, :] = (weight * act[lo:hi]).astype(BF16)
        scaled_ref[1, lo:hi, :] = (head_row(rows_ref, CARRY, head) * dy[lo:hi]).astype(BF16)


def block_kernel(
    low_ref, gy_ref, rows_ref, bctok_ref, bclow_ref, slope_ref,
    high_ref, red_ref, dbc_ref,
    scores_ref, link_ref, acol_ref, dg_ref, yt_ref, du_ref,
):
    step = pl.program_id(0)

    @pl.when(step == 0)
    def _():
        ident = eye(BLK, BF16)
        scores_ref[...] = mm_nt(bctok_ref[:, NS:], bctok_ref[:, :NS])
        seg_row = rows_ref[MASK, 4:5, :]
        seg_col = mm_nt(ident, rows_ref[MASK].astype(BF16))[:, 4:5]
        later = iota((BLK, BLK), 0) >= iota((BLK, BLK), 1)
        linked = jnp.logical_and(later, seg_col == seg_row)
        link_ref[...] = jnp.where(linked, 0.0, -jnp.inf)
        dg_ref[...] = jnp.zeros_like(dg_ref)
        cumul = pick_nt(ident, rows_ref[CUMUL], 3)
        for at in range(acol_ref.shape[0]):
            acol_ref[at] = cumul[:, at * PER : (at + 1) * PER]

    acols = acol_ref[step]
    for k in range(PER):
        head = step * PER + k
        lo, hi = k * HD, (k + 1) * HD
        arow = head_row(rows_ref, CUMUL, head)
        dt = head_row(rows_ref, DT, head)
        skip = head_row(rows_ref, SKIP, head)
        u_low = (dt * low_ref[0, lo:hi, :].astype(F32)).astype(BF16)
        du_first = None
        for tb in range(2):
            t0, t1 = tb * 128, tb * 128 + 128
            decay = jnp.exp(acols[t0:t1, k : k + 1] - arow[:, :t1] + link_ref[t0:t1, :t1])
            mixed = (decay * scores_ref[t0:t1, :t1]).astype(BF16)
            yt_ref[:, t0:t1] = mm_nt(u_low[:, :t1], mixed)
            du = mm(low_ref[1, lo:hi, t0:t1], mixed)
            if tb == 0:
                du_first = du
            else:
                du_ref[:, :128] = du_first + du[:, :128]
                du_ref[:, 128:] = du[:, 128:]
            dmix = mm(gy_ref[t0:t1, lo:hi], u_low[:, :t1])
            dg_ref[t0:t1, :t1] += decay * dmix
        x_h = low_ref[0, lo:hi, :].astype(F32)
        dy_h = low_ref[1, lo:hi, :].astype(F32)
        y_h = yt_ref[...]
        du_h = du_ref[...]
        slope = slope_ref[lo:hi, :]
        high_ref[0, lo:hi, :] = y_h + skip * x_h
        high_ref[1, lo:hi, :] = slope * (dt * du_h + skip * dy_h)
        high_ref[2, lo:hi, :] = slope * (dt * head_row(rows_ref, END, head))
        ga = jnp.sum(dy_h * y_h - u_low.astype(F32) * du_h, axis=0, keepdims=True)
        red_ref[0, pl.ds(head, 1), :] = ga
        red_ref[1, pl.ds(head, 1), :] = jnp.sum(x_h * du_h, axis=0, keepdims=True)
        red_ref[2, pl.ds(head, 1), :] = jnp.sum(x_h * dy_h, axis=0, keepdims=True)

    @pl.when(step == pl.num_programs(0) - 1)
    def _():
        dg = dg_ref[...].astype(BF16)
        dbc_ref[:NS, :] = mm(bclow_ref[1, NS:, :], dg)
        dbc_ref[NS:, :] = mm_nt(bclow_ref[1, :NS, :], dg)


def scan_kernel(in_ref, out_ref):
    peers = in_ref.shape[0]
    ahead = jnp.zeros((32, NS), F32)
    behind = jnp.zeros((32, NS), F32)

    def through(at):
        parts = in_ref[at, 64:72, :].astype(F32)
        return parts[0:1] + parts[1:2] + parts[2:3]

    for i in range(peers):
        out_ref[i, 0:32, :] = ahead.astype(BF16)
        ahead = through(i) * ahead + in_ref[i, 0:32, :].astype(F32)
        at = peers - 1 - i
        out_ref[at, 32:64, :] = behind.astype(BF16)
        behind = through(at) * behind + in_ref[at, 32:64, :].astype(F32)


def bc_kernel(
    state_ref, scaled_ref, dbc_ref, bcslope_ref, bclow_ref, bcsides_ref, rows_ref, pay_ref
):
    small = eye(NS, BF16)
    channels = scaled_ref.shape[1]
    state_in = state_ref[:, 0:32, :].reshape(channels, NS)
    state_back = state_ref[:, 32:64, :].reshape(channels, NS)
    grad_b = mm(mm_nt(small, state_back).astype(BF16), scaled_ref[0])
    grad_c = mm(mm_nt(small, state_in).astype(BF16), scaled_ref[1])
    grad_act = dbc_ref[...] + jnp.concatenate([grad_b, grad_c], axis=0)
    grad, sides = conv_back(
        grad_act * bcslope_ref[...], bclow_ref[0].astype(F32), bcsides_ref[...],
        bcsides_ref[...], masks_of(rows_ref),
    )
    token = mm_nt(eye(BLK, BF16), grad.astype(BF16)).astype(BF16)
    row = iota((16, 128), 0)
    pick = (jnp.where(row < 8, row, row + 96) == iota((16, 128), 1)).astype(BF16)
    rest = mm_nt(pick, sides.astype(BF16)).astype(BF16)
    shares = pay_ref.shape[0]
    share = BLK // shares
    for j in range(shares):
        pay_ref[j, 0:share, :] = token[j * share : (j + 1) * share]
        pay_ref[j, share : share + 16, :] = rest


def x_kernel(
    state_ref, low_ref, high_ref, taps_ref, rows_ref, bctok_ref, local_ref,
    out_ref, gx_ref, sides_ref, gdt_ref, gh_ref,
    red_ref,
):
    step = pl.program_id(0)
    ident = eye(BLK, BF16)
    masks = masks_of(rows_ref)
    state_in = state_ref[:, 0:32, :].reshape(BLK, NS)
    state_back = state_ref[:, 32:64, :].reshape(BLK, NS)
    carried = mm_nt(state_in, bctok_ref[:, NS:])
    from_end = mm_nt(state_back, bctok_ref[:, :NS])
    both = state_in.astype(F32) * state_back.astype(F32)
    last_lane = iota((1, BLK), 1) == BLK - 1
    y_parts = []
    for k in range(PER):
        head = step * PER + k
        lo, hi = k * HD, (k + 1) * HD
        dt = head_row(rows_ref, DT, head)
        carry = head_row(rows_ref, CARRY, head)
        end = head_row(rows_ref, END, head)
        x_h = low_ref[0, lo:hi, :].astype(F32)
        add = carry * carried[lo:hi]
        fed = end * jnp.sum(x_h * from_end[lo:hi], axis=0, keepdims=True)
        from_step = dt * fed
        at_end = jnp.sum(from_step, axis=1, keepdims=True)
        joint = jnp.sum(jnp.sum(both[lo:hi], axis=0, keepdims=True), axis=1, keepdims=True)
        at_end = at_end + carry[:, BLK - 1 :] * joint
        ga = jnp.sum(low_ref[1, lo:hi, :].astype(F32) * add, axis=0, keepdims=True) - from_step
        red_ref[0, pl.ds(head, 1), :] = ga + jnp.where(last_lane, at_end, 0.0)
        red_ref[1, pl.ds(head, 1), :] = fed
        y_parts.append((high_ref[0, lo:hi, :] + add).astype(BF16))
    out_ref[...] = mm_nt(ident, jnp.concatenate(y_parts, axis=0)).astype(BF16)
    grad, sides = conv_back(
        high_ref[1] + high_ref[2] * from_end, low_ref[2].astype(F32),
        taps_ref[...], taps_ref[...], masks,
    )
    gx_ref[...] = mm_nt(ident, grad.astype(BF16)).astype(BF16)
    row = iota((8 + 2 * RIM, 128), 0)
    pick = (jnp.where(row < 8, row, row + 88) == iota((8 + 2 * RIM, 128), 1)).astype(BF16)
    sides_ref[...] = pick_nt(pick, sides, 2)

    @pl.when(step == pl.num_programs(0) - 1)
    def _():
        later = (iota((BLK, BLK), 0) >= iota((BLK, BLK), 1)).astype(BF16)
        grad_log = pick_right(local_ref[0] + red_ref[0], later, 3)
        rate = rows_ref[RATE]
        grad_step = (local_ref[1] + red_ref[1] - rate * grad_log) * rows_ref[SIG]
        gdt_ref[...] = grad_step
        which = iota((8, BLK), 0)
        terms = (-rate * rows_ref[DT] * grad_log, grad_step, local_ref[2])
        gh_ref[...] = jnp.zeros_like(gh_ref)
        gh_ref[:, : rate.shape[0]] = sum(
            pick_nt((which == k).astype(BF16), term, 3) for k, term in enumerate(terms)
        )


def patch_kernel(gx_ref, sides_ref, own_ref, spill_ref, out_ref, bc_ref):
    del gx_ref
    width = sides_ref.shape[1]
    out_ref[...] = (sides_ref[8 + RIM :, :] + spill_ref[:, :width]).astype(BF16)
    share = own_ref.shape[0]
    bc_ref[: share - 8, :] = own_ref[: share - 8, :]
    is_last = lax.axis_index("head") == lax.axis_size("head") - 1
    came = spill_ref[RIM - 8 :, width:]
    bc_ref[share - 8 :, :] = own_ref[share - 8 :, :] + jnp.where(is_last, came, 0.0)


def pack_kernel(got_ref, sides_ref, gh_ref, sums_ref, own_ref, out_ref):
    share = own_ref.shape[0]
    total = jnp.sum(got_ref[...].astype(F32), axis=0)
    own_ref[...] = total[:share]
    width = sides_ref.shape[1]
    out_ref[:, :width] = sides_ref[8 : 8 + RIM, :]
    out_ref[: RIM - 8, width:] = jnp.zeros((RIM - 8, 256), F32)
    out_ref[RIM - 8 :, width:] = total[share + 8 :]
    sums_ref[:, :width] = sides_ref[:8, :]
    sums_ref[:, width : width + 256] = total[share : share + 8]
    sums_ref[:, width + 256 :] = gh_ref[...]


def finish_kernel(a_ref, b_ref, c_ref, d_ref, wx_ref, wbc_ref, heads_ref):
    total = (a_ref[...] + b_ref[...]) + (c_ref[...] + d_ref[...])
    width = wx_ref.shape[1]
    wx_ref[...] = total[:4, :width]
    wbc_ref[...] = total[:4, width : width + 256]
    heads_ref[...] = total[:3, width + 256 : width + 256 + heads_ref.shape[1]]


def whole(shape):
    zeros = (0,) * len(shape)
    return pl.BlockSpec(shape, lambda *_: zeros)


def columns(rows):
    return pl.BlockSpec((rows, BLK), lambda i: (0, i))


def channel_rows(width):
    return pl.BlockSpec((BLK, width), lambda i: (i, 0))


def shaped(shape, dtype):
    return jax.ShapeDtypeStruct(shape, dtype)


def stored(shape, dtype):
    return pltpu.HBM(shape, dtype)


def from_hbm(*values):
    return [pltpu.with_memory_space_constraint(value, pltpu.HBM) for value in values]


def passed_along(value, by):
    peers = lax.axis_size("ctx")
    pairs = [(i, i + by) for i in range(peers) if 0 <= i + by < peers]
    return lax.ppermute(value, "ctx", pairs)


def summed_over_ctx(value):
    peers = lax.axis_size("ctx")

    def turned(value, stride):
        def to(i, by):
            at = i // stride % 4
            return i + ((at + by) % 4 - at) * stride

        return [value] + [
            lax.ppermute(value, "ctx", [(i, to(i, by)) for i in range(peers)])
            for by in (1, 2, 3)
        ]

    value = value + lax.ppermute(value, "ctx", [(i, i ^ 1) for i in range(peers)])
    own, one, two, three = turned(value, 2)
    return turned((own + one) + (two + three), 8)


def cost(micros):
    return pl.CostEstimate(
        flops=int(micros * 1e8), bytes_accessed=int(micros * 3e6), transcendentals=0
    )


def local(x_raw, bc_raw, dt_raw, conv_x, conv_bc, a_log, dt_bias, skip_weight, segment, grad_y):
    rows, channels = x_raw.shape
    heads = dt_raw.shape[1]
    steps = channels // BLK
    peers = lax.axis_size("ctx")
    shares = lax.axis_size("head")
    share = rows // shares
    params = pltpu.CompilerParams(vmem_limit_bytes=VMEM)
    last_inputs = pl.pallas_call(
        rim_kernel,
        in_specs=[pl.BlockSpec(memory_space=pl.ANY)] * 2,
        out_specs=pl.BlockSpec(memory_space=pltpu.VMEM),
        out_shape=shaped((RIM, channels + 256), BF16),
        scratch_shapes=[pltpu.SemaphoreType.DMA((2,))],
        compiler_params=params,
        name="rim_rows",
    )(*from_hbm(x_raw, bc_raw))
    rim = passed_along(last_inputs, 1)
    row_spec = whole((8, heads, rows))
    square = whole((256, rows))
    by_channel = channel_rows(rows)

    def chan(dtype):
        return stored((channels, rows), dtype)

    rim_bc_spec = pl.BlockSpec((RIM, 256), lambda i: (0, channels // 256))
    local_spec = whole((3, heads, rows))

    def stack(count):
        return pl.BlockSpec((count, BLK, rows), lambda i: (0, i, 0))

    wide_spec = channel_rows(128)

    def one(shape):
        return pl.BlockSpec(shape, lambda i: (0,) * len(shape))

    pay, head_rows, bctok = pl.pallas_call(
        state_kernel,
        grid=(steps,),
        in_specs=[
            columns(rows), columns(RIM), columns(rows), columns(4),
            one((rows, 256)), rim_bc_spec, one((4, 256)),
            one(segment_rows := (segment.shape[0] // 128, 128)), one((1, heads)), one((1, heads)),
            one((1, heads)), one((heads, rows)),
        ],
        out_specs=[
            pl.BlockSpec((8, 72, NS), lambda i: (i, 0, 0)), row_spec, whole((rows, 256)),
        ],
        out_shape=[
            shaped((peers, 72, NS), BF16),
            stored((8, heads, rows), F32), stored((rows, 256), BF16),
        ],
        compiler_params=params,
        cost_estimate=cost(7),
        name="states",
    )(
        *from_hbm(x_raw), rim, *from_hbm(grad_y, conv_x, bc_raw), rim,
        *from_hbm(
            conv_bc, segment.reshape(segment_rows), a_log[None], dt_bias[None],
            skip_weight[None], dt_raw.T,
        ),
    )

    got = lax.all_to_all(pay, "ctx", 0, 0, tiled=True)

    low, slope, scaled, sides_in, bclow, bcslope, bcsides = pl.pallas_call(
        slope_kernel,
        grid=(steps,),
        in_specs=[
            columns(rows), columns(RIM), columns(rows), columns(4), whole((rows, 256)),
            rim_bc_spec, whole((4, 256)), row_spec,
        ],
        out_specs=[
            stack(3), by_channel, stack(2), wide_spec, whole((2, 256, rows)), square,
            whole((256, 128)),
        ],
        out_shape=[
            stored((3, channels, rows), BF16), chan(F32), stored((2, channels, rows), BF16),
            stored((channels, 128), F32), stored((2, 256, rows), BF16), stored((256, rows), F32),
            stored((256, 128), F32),
        ],
        compiler_params=params,
        cost_estimate=cost(6),
        name="slopes",
    )(*from_hbm(x_raw, rim, grad_y, conv_x, bc_raw, rim, conv_bc, head_rows))
    got, low = lax.optimization_barrier((got, low))

    carried = pl.pallas_call(
        scan_kernel,
        in_specs=[pl.BlockSpec(memory_space=pltpu.VMEM)],
        out_specs=pl.BlockSpec(memory_space=pltpu.VMEM),
        out_shape=shaped((peers, 64, NS), BF16),
        compiler_params=params,
        cost_estimate=cost(1),
        name="state_scan",
    )(got)
    states = lax.all_to_all(carried, "ctx", 0, 0, tiled=True)

    high, red_loc, dbc = pl.pallas_call(
        block_kernel,
        grid=(steps,),
        in_specs=[
            stack(2), columns(rows), row_spec, whole((rows, 256)), whole((2, 256, rows)),
            by_channel,
        ],
        out_specs=[stack(3), local_spec, square],
        out_shape=[
            stored((3, channels, rows), F32), stored((3, heads, rows), F32),
            stored((256, rows), F32),
        ],
        scratch_shapes=[
            pltpu.VMEM((rows, rows), F32), pltpu.VMEM((rows, rows), F32),
            pltpu.VMEM((steps, rows, PER), F32), pltpu.VMEM((rows, rows), F32),
            pltpu.VMEM((HD, rows), F32), pltpu.VMEM((HD, rows), F32),
        ],
        compiler_params=params,
        cost_estimate=cost(8),
        name="in_block",
    )(*from_hbm(low, grad_y, head_rows, bctok, bclow, slope))

    state_spec = pl.BlockSpec((8, 64, NS), lambda i: (i, 0, 0))
    pay_bc = pl.pallas_call(
        bc_kernel,
        grid=(1,),
        in_specs=[
            one((peers, 64, NS)), one((2, channels, rows)), square, square,
            whole((2, 256, rows)), whole((256, 128)), row_spec,
        ],
        out_specs=whole((shares, share + 16, 256)),
        out_shape=shaped((shares, share + 16, 256), BF16),
        compiler_params=params,
        cost_estimate=cost(4),
        name="bc_part",
    )(states, *from_hbm(scaled, dbc, bcslope, bclow, bcsides, head_rows))
    got_bc = lax.all_to_all(pay_bc, "head", 0, 0, tiled=True)

    side_rows = 8 + 2 * RIM
    ssd_out, gx, sides, grad_dt, gh = pl.pallas_call(
        x_kernel,
        grid=(steps,),
        in_specs=[
            state_spec, stack(3), stack(3), wide_spec, row_spec, whole((rows, 256)), local_spec,
        ],
        out_specs=[
            columns(rows), columns(rows), columns(side_rows), whole((heads, rows)),
            whole((8, 128)),
        ],
        out_shape=[
            stored((rows, channels), BF16), stored((rows, channels), BF16),
            stored((side_rows, channels), F32), stored((heads, rows), F32),
            stored((8, 128), F32),
        ],
        scratch_shapes=[pltpu.VMEM((2, heads, rows), F32)],
        compiler_params=params,
        cost_estimate=cost(10),
        name="x_part",
    )(states, *from_hbm(low, high, sides_in, head_rows, bctok, red_loc))

    vmem = pl.BlockSpec(memory_space=pltpu.VMEM)
    width = channels + 256 + 128
    sums, own_bc, spills = pl.pallas_call(
        pack_kernel,
        in_specs=[vmem] * 3,
        out_specs=[vmem] * 3,
        out_shape=[
            shaped((8, width), F32), shaped((share, 256), F32),
            shaped((RIM, channels + 256), F32),
        ],
        compiler_params=params,
        cost_estimate=cost(1),
        name="pack_sums",
    )(got_bc, *from_hbm(sides, gh))
    parts = summed_over_ctx(sums)
    spills = passed_along(spills, -1)
    grad_x, grad_bc = pl.pallas_call(
        patch_kernel,
        grid=(1,),
        in_specs=[
            pl.BlockSpec(memory_space=pl.ANY), whole((side_rows, channels)), whole((share, 256)),
            whole((RIM, channels + 256)),
        ],
        out_specs=[
            pl.BlockSpec((RIM, channels), lambda i: (rows // RIM - 1, 0)), whole((share, 256)),
        ],
        out_shape=[stored((rows, channels), BF16), stored((share, 256), F32)],
        input_output_aliases={0: 0},
        compiler_params=params,
        cost_estimate=cost(1),
        name="last_rows",
    )(*from_hbm(gx, sides), own_bc, spills)
    grad_wx, grad_wbc, grad_heads = pl.pallas_call(
        finish_kernel,
        in_specs=[vmem] * 4,
        out_specs=[vmem] * 3,
        out_shape=[stored((4, channels), F32), stored((4, 256), F32), stored((3, heads), F32)],
        compiler_params=params,
        cost_estimate=cost(1),
        name="finish_sums",
    )(*parts)
    return ssd_out, grad_x, grad_bc, grad_dt.T, grad_wx, grad_wbc, grad_heads


def solution(mesh):
    in_specs = (
        P("ctx", "head"), P("ctx", None), P("ctx", "head"), P(None, "head"), P(),
        P("head"), P("head"), P("head"), P(), P("ctx", "head"),
    )
    out_specs = (
        P("ctx", "head"), P("ctx", "head"), P(("ctx", "head"), None), P("ctx", "head"),
        P(None, "head"), P(), P(None, "head"),
    )
    return jax.shard_map(local, mesh=mesh, in_specs=in_specs, out_specs=out_specs, check_vma=False)
```

```python
import jax
import jax.numpy as jnp
from jax import lax
from jax.experimental import pallas as pl
from jax.experimental.pallas import tpu as pltpu
from jax.sharding import PartitionSpec as P

F32 = jnp.float32
BF16 = jnp.bfloat16

BLK = 256
HD = 64
NS = 128
RIM = 16
PER = BLK // HD
VMEM = 24 * 1024 * 1024

DT, CUMUL, CARRY, END, SIG, SKIP, RATE, MASK = range(8)


def mm(a, b):
    return lax.dot_general(a, b, (((1,), (0,)), ((), ())), preferred_element_type=F32)


def mm_nt(a, b):
    return lax.dot_general(a, b, (((1,), (1,)), ((), ())), preferred_element_type=F32)


def split(value, count):
    parts = []
    for _ in range(count):
        part = value.astype(BF16)
        parts.append(part)
        value = value - part.astype(F32)
    return parts


def pick_nt(pick, value, count):
    return sum(mm_nt(pick, part) for part in split(value, count))


def pick_right(value, pick, count):
    return sum(mm(part, pick) for part in split(value, count))


def iota(shape, dim):
    return lax.broadcasted_iota(jnp.int32, shape, dim)


def eye(n, dtype):
    return (iota((n, n), 0) == iota((n, n), 1)).astype(dtype)


def conv_own(raw, taps, masks):
    lane = iota((raw.shape[0], 128), 1)
    total = taps[:, 3:4] * raw
    for j in range(1, 4):
        rolled = pltpu.roll(raw, j, 1)
        shifted = jnp.concatenate(
            [jnp.where(lane < j, 0.0, rolled[:, :128]), rolled[:, 128:]], axis=1
        )
        total = total + shifted * (taps[:, 3 - j : 4 - j] * masks[3 - j])
    return total


def conv_rim(rim, taps, masks):
    lane = iota(rim.shape, 1)
    total = jnp.zeros(rim.shape, F32)
    for j in range(1, 4):
        before = jnp.where(lane < j, pltpu.roll(rim, j, 1), 0.0)
        total = total + before * (taps[:, 3 - j : 4 - j] * masks[3 - j][:, :128])
    return total


def conv_back(g, raw, rim, taps, masks):
    lane = iota((g.shape[0], 128), 1)
    grad = taps[:, 3:4] * g
    spill = jnp.zeros((g.shape[0], 128), F32)
    product = g * raw
    products = [None, None, None, product[:, :128] + product[:, 128:]]
    for j in range(1, 4):
        masked = g * masks[3 - j]
        rolled = pltpu.roll(masked, g.shape[1] - j, 1)
        wrapped = lane >= 128 - j
        first = rolled[:, :128]
        second = jnp.where(wrapped, 0.0, rolled[:, 128:])
        outer = jnp.where(wrapped, rolled[:, 128:], 0.0)
        tap = taps[:, 3 - j : 4 - j]
        grad = grad + tap * jnp.concatenate([first, second], axis=1)
        spill = spill + tap * outer
        products[3 - j] = first * raw[:, :128] + second * raw[:, 128:] + outer * rim
    chosen = (iota((512, 128), 0) // 128 == iota((512, 128), 1)).astype(BF16)
    sums = pick_right(jnp.concatenate(products, axis=1), chosen, 2)
    moved = pltpu.roll(spill, 128 - RIM, 1)
    sides = jnp.where(lane >= 128 - RIM, grad[:, 128:], jnp.where(lane >= 96, moved, sums))
    return grad, sides


def wide_rim(rim):
    return jnp.concatenate([jnp.zeros((128 - RIM, rim.shape[1]), BF16), rim], axis=0)


def masks_of(rows_ref):
    return [rows_ref[MASK, k : k + 1, :] for k in range(4)]


def head_row(rows_ref, plane, head):
    return rows_ref[plane, pl.ds(head, 1), :]


def taps_of(w):
    padded = jnp.concatenate([w, jnp.zeros((124, BLK), F32)], axis=0)
    return jnp.transpose(padded)


def conv_all(raw_ref, rim_ref, taps, masks):
    ident = eye(BLK, BF16)
    raw = mm_nt(ident, raw_ref[...])
    rim = mm_nt(ident, wide_rim(rim_ref[...]))
    pre = conv_own(raw, taps, masks)
    pre = jnp.concatenate([pre[:, :128] + conv_rim(rim, taps, masks), pre[:, 128:]], axis=1)
    return raw, rim, pre


def with_taps(rim, taps):
    return jnp.where(iota(rim.shape, 1) < 4, taps, rim)


def sigmoid(value):
    return 1.0 / (1.0 + jnp.exp(-value))


def rim_kernel(x_ref, bc_ref, out_ref, sems):
    rows, width = x_ref.shape
    copies = [
        pltpu.make_async_copy(
            x_ref.at[pl.ds(rows - RIM, RIM), :], out_ref.at[:, pl.ds(0, width)], sems.at[0]
        ),
        pltpu.make_async_copy(
            bc_ref.at[pl.ds(rows - RIM, RIM), :],
            out_ref.at[:, pl.ds(width, bc_ref.shape[1])],
            sems.at[1],
        ),
    ]
    for copy in copies:
        copy.start()
    for copy in copies:
        copy.wait()


def head_rows_of(rows_ref, seg_ref, rate_ref, bias_ref, skip_ref, dt_ref):
    here = lax.axis_index("ctx")
    own = [seg_ref[pl.ds(2 * here + half, 1), :] for half in range(2)]
    target = jnp.concatenate(own, axis=1).astype(F32)
    before = seg_ref[pl.ds(jnp.maximum(2 * here - 1, 0), 1), :].astype(F32)
    before = jnp.where(here == 0, -1.0, before)
    lane = iota((1, 128), 1)
    masks = []
    for j in (3, 2, 1):
        rolled = pltpu.roll(target, j, 1)
        first = jnp.where(lane < j, pltpu.roll(before, j, 1), rolled[:, :128])
        shifted = jnp.concatenate([first, rolled[:, 128:]], axis=1)
        masks.append((shifted == target).astype(F32))
    rows_ref[MASK] = jnp.concatenate(
        masks + [jnp.ones((1, BLK), F32), target, jnp.zeros((11, BLK), F32)], axis=0
    )
    heads = dt_ref.shape[0]
    values = jnp.concatenate(
        [rate_ref[...], bias_ref[...], skip_ref[...], jnp.zeros((5, heads), F32)], axis=0
    )
    per_head = pick_nt(eye(heads, BF16), values, 3)
    rate = jnp.exp(per_head[:, 0:1])
    pre = dt_ref[...] + per_head[:, 1:2]
    dt = jnp.maximum(pre, 0.0) + jnp.log1p(jnp.exp(-jnp.abs(pre)))
    upto = (iota((BLK, BLK), 0) <= iota((BLK, BLK), 1)).astype(BF16)
    cumul = pick_right(-rate * dt, upto, 3)
    keep = (target == before[:, 127:]).astype(F32)
    same_end = target == target[:, BLK - 1 :]
    rows_ref[DT] = dt
    rows_ref[CUMUL] = cumul
    rows_ref[CARRY] = keep * jnp.exp(cumul)
    rows_ref[END] = jnp.exp(jnp.where(same_end, cumul[:, BLK - 1 :] - cumul, -jnp.inf))
    rows_ref[SIG] = sigmoid(pre)
    rows_ref[SKIP] = jnp.broadcast_to(per_head[:, 2:3], (heads, BLK))
    rows_ref[RATE] = jnp.broadcast_to(rate, (heads, BLK))


def state_kernel(
    x_ref, rim_ref, gy_ref, wx_ref, bc_ref, rimbc_ref, wbc_ref, seg_ref, rate_ref, bias_ref,
    skip_ref, dt_ref,
    pay_ref, rows_ref, bctok_ref,
):
    step = pl.program_id(0)
    ident = eye(BLK, BF16)

    @pl.when(step == 0)
    def _():
        head_rows_of(rows_ref, seg_ref, rate_ref, bias_ref, skip_ref, dt_ref)
        _, _, pre = conv_all(bc_ref, rimbc_ref, taps_of(wbc_ref[...]), masks_of(rows_ref))
        bctok_ref[...] = mm_nt(ident, (pre * sigmoid(pre)).astype(BF16)).astype(BF16)

    _, _, pre = conv_all(x_ref, rim_ref, taps_of(wx_ref[...]), masks_of(rows_ref))
    act = (pre * sigmoid(pre)).astype(BF16).astype(F32)
    dy = mm_nt(ident, gy_ref[...])
    ends, carries = [], []
    for k in range(PER):
        head = step * PER + k
        lo, hi = k * HD, (k + 1) * HD
        carry = head_row(rows_ref, CARRY, head)
        weight = head_row(rows_ref, END, head) * head_row(rows_ref, DT, head)
        ends.append((weight * act[lo:hi]).astype(BF16))
        carries.append((carry * dy[lo:hi]).astype(BF16))
        parts = split(carry[:, BLK - 1 :], 3)
        which = iota((8, NS), 0)
        through = jnp.where(
            which == 0, parts[0].astype(F32),
            jnp.where(which == 1, parts[1].astype(F32), parts[2].astype(F32)),
        ).astype(BF16)
        pay_ref[2 * k, 64:72, :] = through
        pay_ref[2 * k + 1, 64:72, :] = through
    state = mm(jnp.concatenate(ends, axis=0), bctok_ref[:, :NS]).astype(BF16)
    back = mm(jnp.concatenate(carries, axis=0), bctok_ref[:, NS:]).astype(BF16)
    for j in range(2 * PER):
        pay_ref[j, 0:32, :] = state[j * 32 : j * 32 + 32]
        pay_ref[j, 32:64, :] = back[j * 32 : j * 32 + 32]


def slope_kernel(
    x_ref, rim_ref, gy_ref, wx_ref, bc_ref, rimbc_ref, wbc_ref, rows_ref,
    low_ref, slope_ref, scaled_ref, sides_ref, bclow_ref, bcslope_ref, bcsides_ref,
):
    step = pl.program_id(0)
    masks = masks_of(rows_ref)

    @pl.when(step == 0)
    def _():
        taps = taps_of(wbc_ref[...])
        raw, rim, pre = conv_all(bc_ref, rimbc_ref, taps, masks)
        bcsides_ref[...] = with_taps(rim, taps)
        sig = sigmoid(pre)
        bclow_ref[0] = raw.astype(BF16)
        bclow_ref[1] = (pre * sig).astype(BF16)
        bcslope_ref[...] = sig * (1.0 + pre * (1.0 - sig))

    taps = taps_of(wx_ref[...])
    raw, rim, pre = conv_all(x_ref, rim_ref, taps, masks)
    sides_ref[...] = with_taps(rim, taps)
    sig = sigmoid(pre)
    slope_ref[...] = sig * (1.0 + pre * (1.0 - sig))
    low = (pre * sig).astype(BF16)
    dy = mm_nt(eye(BLK, BF16), gy_ref[...])
    low_ref[0] = low
    low_ref[1] = dy.astype(BF16)
    low_ref[2] = raw.astype(BF16)
    act = low.astype(F32)
    for k in range(PER):
        head = step * PER + k
        lo, hi = k * HD, (k + 1) * HD
        weight = head_row(rows_ref, END, head) * head_row(rows_ref, DT, head)
        scaled_ref[0, lo:hi, :] = (weight * act[lo:hi]).astype(BF16)
        scaled_ref[1, lo:hi, :] = (head_row(rows_ref, CARRY, head) * dy[lo:hi]).astype(BF16)


def block_kernel(
    low_ref, gy_ref, rows_ref, bctok_ref, bclow_ref, slope_ref,
    high_ref, red_ref, dbc_ref,
    scores_ref, link_ref, acol_ref, dg_ref, yt_ref, du_ref,
):
    step = pl.program_id(0)

    @pl.when(step == 0)
    def _():
        ident = eye(BLK, BF16)
        scores_ref[...] = mm_nt(bctok_ref[:, NS:], bctok_ref[:, :NS])
        seg_row = rows_ref[MASK, 4:5, :]
        seg_col = mm_nt(ident, rows_ref[MASK].astype(BF16))[:, 4:5]
        later = iota((BLK, BLK), 0) >= iota((BLK, BLK), 1)
        linked = jnp.logical_and(later, seg_col == seg_row)
        link_ref[...] = jnp.where(linked, 0.0, -jnp.inf)
        dg_ref[...] = jnp.zeros_like(dg_ref)
        cumul = pick_nt(ident, rows_ref[CUMUL], 3)
        for at in range(acol_ref.shape[0]):
            acol_ref[at] = cumul[:, at * PER : (at + 1) * PER]

    acols = acol_ref[step]
    for k in range(PER):
        head = step * PER + k
        lo, hi = k * HD, (k + 1) * HD
        arow = head_row(rows_ref, CUMUL, head)
        dt = head_row(rows_ref, DT, head)
        skip = head_row(rows_ref, SKIP, head)
        u_low = (dt * low_ref[0, lo:hi, :].astype(F32)).astype(BF16)
        du_first = None
        for tb in range(2):
            t0, t1 = tb * 128, tb * 128 + 128
            decay = jnp.exp(acols[t0:t1, k : k + 1] - arow[:, :t1] + link_ref[t0:t1, :t1])
            mixed = (decay * scores_ref[t0:t1, :t1]).astype(BF16)
            yt_ref[:, t0:t1] = mm_nt(u_low[:, :t1], mixed)
            du = mm(low_ref[1, lo:hi, t0:t1], mixed)
            if tb == 0:
                du_first = du
            else:
                du_ref[:, :128] = du_first + du[:, :128]
                du_ref[:, 128:] = du[:, 128:]
            dmix = mm(gy_ref[t0:t1, lo:hi], u_low[:, :t1])
            dg_ref[t0:t1, :t1] += decay * dmix
        x_h = low_ref[0, lo:hi, :].astype(F32)
        dy_h = low_ref[1, lo:hi, :].astype(F32)
        y_h = yt_ref[...]
        du_h = du_ref[...]
        slope = slope_ref[lo:hi, :]
        high_ref[0, lo:hi, :] = y_h + skip * x_h
        high_ref[1, lo:hi, :] = slope * (dt * du_h + skip * dy_h)
        high_ref[2, lo:hi, :] = slope * (dt * head_row(rows_ref, END, head))
        ga = jnp.sum(dy_h * y_h - u_low.astype(F32) * du_h, axis=0, keepdims=True)
        red_ref[0, pl.ds(head, 1), :] = ga
        red_ref[1, pl.ds(head, 1), :] = jnp.sum(x_h * du_h, axis=0, keepdims=True)
        red_ref[2, pl.ds(head, 1), :] = jnp.sum(x_h * dy_h, axis=0, keepdims=True)

    @pl.when(step == pl.num_programs(0) - 1)
    def _():
        dg = dg_ref[...].astype(BF16)
        dbc_ref[:NS, :] = mm(bclow_ref[1, NS:, :], dg)
        dbc_ref[NS:, :] = mm_nt(bclow_ref[1, :NS, :], dg)


def scan_kernel(in_ref, out_ref):
    peers = in_ref.shape[0]
    ahead = jnp.zeros((32, NS), F32)
    behind = jnp.zeros((32, NS), F32)

    def through(at):
        parts = in_ref[at, 64:72, :].astype(F32)
        return parts[0:1] + parts[1:2] + parts[2:3]

    for i in range(peers):
        out_ref[i, 0:32, :] = ahead.astype(BF16)
        ahead = through(i) * ahead + in_ref[i, 0:32, :].astype(F32)
        at = peers - 1 - i
        out_ref[at, 32:64, :] = behind.astype(BF16)
        behind = through(at) * behind + in_ref[at, 32:64, :].astype(F32)


def bc_kernel(
    state_ref, scaled_ref, dbc_ref, bcslope_ref, bclow_ref, bcsides_ref, rows_ref, pay_ref
):
    small = eye(NS, BF16)
    channels = scaled_ref.shape[1]
    state_in = state_ref[:, 0:32, :].reshape(channels, NS)
    state_back = state_ref[:, 32:64, :].reshape(channels, NS)
    grad_b = mm(mm_nt(small, state_back).astype(BF16), scaled_ref[0])
    grad_c = mm(mm_nt(small, state_in).astype(BF16), scaled_ref[1])
    grad_act = dbc_ref[...] + jnp.concatenate([grad_b, grad_c], axis=0)
    grad, sides = conv_back(
        grad_act * bcslope_ref[...], bclow_ref[0].astype(F32), bcsides_ref[...],
        bcsides_ref[...], masks_of(rows_ref),
    )
    token = mm_nt(eye(BLK, BF16), grad.astype(BF16)).astype(BF16)
    row = iota((8, 128), 0)
    pick = (jnp.where(row < 4, row, row + 104) == iota((8, 128), 1)).astype(BF16)
    rest = mm_nt(pick, sides.astype(BF16)).astype(BF16)
    shares = pay_ref.shape[0]
    share = BLK // shares
    for j in range(shares):
        pay_ref[j, 0:share, :] = token[j * share : (j + 1) * share]
        pay_ref[j, share : share + 8, :] = rest


def x_kernel(
    state_ref, low_ref, high_ref, taps_ref, rows_ref, bctok_ref, local_ref,
    out_ref, gx_ref, sides_ref, gdt_ref, gh_ref,
    red_ref,
):
    step = pl.program_id(0)
    ident = eye(BLK, BF16)
    masks = masks_of(rows_ref)
    state_in = state_ref[:, 0:32, :].reshape(BLK, NS)
    state_back = state_ref[:, 32:64, :].reshape(BLK, NS)
    carried = mm_nt(state_in, bctok_ref[:, NS:])
    from_end = mm_nt(state_back, bctok_ref[:, :NS])
    both = state_in.astype(F32) * state_back.astype(F32)
    last_lane = iota((1, BLK), 1) == BLK - 1
    y_parts = []
    for k in range(PER):
        head = step * PER + k
        lo, hi = k * HD, (k + 1) * HD
        dt = head_row(rows_ref, DT, head)
        carry = head_row(rows_ref, CARRY, head)
        end = head_row(rows_ref, END, head)
        x_h = low_ref[0, lo:hi, :].astype(F32)
        add = carry * carried[lo:hi]
        fed = end * jnp.sum(x_h * from_end[lo:hi], axis=0, keepdims=True)
        from_step = dt * fed
        at_end = jnp.sum(from_step, axis=1, keepdims=True)
        joint = jnp.sum(jnp.sum(both[lo:hi], axis=0, keepdims=True), axis=1, keepdims=True)
        at_end = at_end + carry[:, BLK - 1 :] * joint
        ga = jnp.sum(low_ref[1, lo:hi, :].astype(F32) * add, axis=0, keepdims=True) - from_step
        red_ref[0, pl.ds(head, 1), :] = ga + jnp.where(last_lane, at_end, 0.0)
        red_ref[1, pl.ds(head, 1), :] = fed
        y_parts.append((high_ref[0, lo:hi, :] + add).astype(BF16))
    out_ref[...] = mm_nt(ident, jnp.concatenate(y_parts, axis=0)).astype(BF16)
    grad, sides = conv_back(
        high_ref[1] + high_ref[2] * from_end, low_ref[2].astype(F32),
        taps_ref[...], taps_ref[...], masks,
    )
    gx_ref[...] = mm_nt(ident, grad.astype(BF16)).astype(BF16)
    row = iota((8 + 2 * RIM, 128), 0)
    pick = (jnp.where(row < 8, row, row + 88) == iota((8 + 2 * RIM, 128), 1)).astype(BF16)
    sides_ref[...] = pick_nt(pick, sides, 2)

    @pl.when(step == pl.num_programs(0) - 1)
    def _():
        later = (iota((BLK, BLK), 0) >= iota((BLK, BLK), 1)).astype(BF16)
        grad_log = pick_right(local_ref[0] + red_ref[0], later, 3)
        rate = rows_ref[RATE]
        grad_step = (local_ref[1] + red_ref[1] - rate * grad_log) * rows_ref[SIG]
        gdt_ref[...] = grad_step
        which = iota((8, BLK), 0)
        terms = (-rate * rows_ref[DT] * grad_log, grad_step, local_ref[2])
        gh_ref[...] = jnp.zeros_like(gh_ref)
        gh_ref[:, : rate.shape[0]] = sum(
            pick_nt((which == k).astype(BF16), term, 3) for k, term in enumerate(terms)
        )


def patch_kernel(gx_ref, sides_ref, own_ref, spill_ref, out_ref, bc_ref):
    del gx_ref
    width = sides_ref.shape[1]
    spill = jnp.concatenate([jnp.zeros((RIM - 8, width), F32), spill_ref[:, :width]], axis=0)
    out_ref[...] = (sides_ref[8 + RIM :, :] + spill).astype(BF16)
    share = own_ref.shape[0]
    bc_ref[: share - 8, :] = own_ref[: share - 8, :]
    is_last = lax.axis_index("head") == lax.axis_size("head") - 1
    came = spill_ref[:, width:]
    bc_ref[share - 8 :, :] = own_ref[share - 8 :, :] + jnp.where(is_last, came, 0.0)


def pack_kernel(got_ref, sides_ref, gh_ref, sums_ref, own_ref, out_ref):
    share = own_ref.shape[0]
    total = jnp.sum(got_ref[...].astype(F32), axis=0)
    own_ref[...] = total[:share]
    width = sides_ref.shape[1]
    rest = total[share:]
    out_ref[:, :width] = sides_ref[RIM : 8 + RIM, :]
    out_ref[:, width:] = jnp.where(iota(rest.shape, 0) < 4, 0.0, rest)
    sums_ref[:, :width] = sides_ref[:4, :]
    sums_ref[:, width : width + 256] = rest[:4]
    sums_ref[:, width + 256 :] = gh_ref[:4, :]


def finish_kernel(a_ref, b_ref, c_ref, d_ref, wx_ref, wbc_ref, heads_ref):
    total = (a_ref[...] + b_ref[...]) + (c_ref[...] + d_ref[...])
    width = wx_ref.shape[1]
    wx_ref[...] = total[:4, :width]
    wbc_ref[...] = total[:4, width : width + 256]
    heads_ref[...] = total[:3, width + 256 : width + 256 + heads_ref.shape[1]]


def whole(shape):
    zeros = (0,) * len(shape)
    return pl.BlockSpec(shape, lambda *_: zeros)


def columns(rows):
    return pl.BlockSpec((rows, BLK), lambda i: (0, i))


def channel_rows(width):
    return pl.BlockSpec((BLK, width), lambda i: (i, 0))


def shaped(shape, dtype):
    return jax.ShapeDtypeStruct(shape, dtype)


def stored(shape, dtype):
    return pltpu.HBM(shape, dtype)


def from_hbm(*values):
    return [pltpu.with_memory_space_constraint(value, pltpu.HBM) for value in values]


def passed_along(value, by):
    peers = lax.axis_size("ctx")
    return lax.ppermute(value, "ctx", [(i, (i + by) % peers) for i in range(peers)])


def summed_over_ctx(value):
    peers = lax.axis_size("ctx")

    def moved(value, to):
        return lax.ppermute(value, "ctx", [(i, to(i)) for i in range(peers)])

    def turned(i, stride, by):
        at = i // stride % 4
        return i + ((at + by) % 4 - at) * stride

    def swap(i):
        return i ^ 1

    value = value + moved(value, swap)
    one, two, three = [moved(value, lambda i, by=by: turned(i, 2, by)) for by in (1, 2, 3)]
    value = (value + one) + (two + three)
    near = moved(value, lambda i: turned(i, 8, 1 if i % 2 else 3))
    far = moved(value, lambda i: turned(i, 8, 2))
    return value, far, near, moved(near, swap)


def cost(micros):
    return pl.CostEstimate(
        flops=int(micros * 1e8), bytes_accessed=int(micros * 3e6), transcendentals=0
    )


def local(x_raw, bc_raw, dt_raw, conv_x, conv_bc, a_log, dt_bias, skip_weight, segment, grad_y):
    rows, channels = x_raw.shape
    heads = dt_raw.shape[1]
    steps = channels // BLK
    peers = lax.axis_size("ctx")
    shares = lax.axis_size("head")
    share = rows // shares
    params = pltpu.CompilerParams(vmem_limit_bytes=VMEM)
    last_inputs = pl.pallas_call(
        rim_kernel,
        in_specs=[pl.BlockSpec(memory_space=pl.ANY)] * 2,
        out_specs=pl.BlockSpec(memory_space=pltpu.VMEM),
        out_shape=shaped((RIM, channels + 256), BF16),
        scratch_shapes=[pltpu.SemaphoreType.DMA((2,))],
        compiler_params=params,
        name="rim_rows",
    )(*from_hbm(x_raw, bc_raw))
    rim = passed_along(last_inputs, 1)
    row_spec = whole((8, heads, rows))
    square = whole((256, rows))
    by_channel = channel_rows(rows)

    def chan(dtype):
        return stored((channels, rows), dtype)

    rim_bc_spec = pl.BlockSpec((RIM, 256), lambda i: (0, channels // 256))
    local_spec = whole((3, heads, rows))

    def stack(count):
        return pl.BlockSpec((count, BLK, rows), lambda i: (0, i, 0))

    wide_spec = channel_rows(128)

    def one(shape):
        return pl.BlockSpec(shape, lambda i: (0,) * len(shape))

    pay, head_rows, bctok = pl.pallas_call(
        state_kernel,
        grid=(steps,),
        in_specs=[
            columns(rows), columns(RIM), columns(rows), columns(4),
            one((rows, 256)), rim_bc_spec, one((4, 256)),
            one(segment_rows := (segment.shape[0] // 128, 128)), one((1, heads)), one((1, heads)),
            one((1, heads)), one((heads, rows)),
        ],
        out_specs=[
            pl.BlockSpec((8, 72, NS), lambda i: (i, 0, 0)), row_spec, whole((rows, 256)),
        ],
        out_shape=[
            shaped((peers, 72, NS), BF16),
            stored((8, heads, rows), F32), stored((rows, 256), BF16),
        ],
        compiler_params=params,
        cost_estimate=cost(7),
        name="states",
    )(
        *from_hbm(x_raw), rim, *from_hbm(grad_y, conv_x, bc_raw), rim,
        *from_hbm(
            conv_bc, segment.reshape(segment_rows), a_log[None], dt_bias[None],
            skip_weight[None], dt_raw.T,
        ),
    )

    got = lax.all_to_all(pay, "ctx", 0, 0, tiled=True)

    low, slope, scaled, sides_in, bclow, bcslope, bcsides = pl.pallas_call(
        slope_kernel,
        grid=(steps,),
        in_specs=[
            columns(rows), columns(RIM), columns(rows), columns(4), whole((rows, 256)),
            rim_bc_spec, whole((4, 256)), row_spec,
        ],
        out_specs=[
            stack(3), by_channel, stack(2), wide_spec, whole((2, 256, rows)), square,
            whole((256, 128)),
        ],
        out_shape=[
            stored((3, channels, rows), BF16), chan(F32), stored((2, channels, rows), BF16),
            stored((channels, 128), F32), stored((2, 256, rows), BF16), stored((256, rows), F32),
            stored((256, 128), F32),
        ],
        compiler_params=params,
        cost_estimate=cost(6),
        name="slopes",
    )(*from_hbm(x_raw, rim, grad_y, conv_x, bc_raw, rim, conv_bc, head_rows))
    got, low = lax.optimization_barrier((got, low))

    carried = pl.pallas_call(
        scan_kernel,
        in_specs=[pl.BlockSpec(memory_space=pltpu.VMEM)],
        out_specs=pl.BlockSpec(memory_space=pltpu.VMEM),
        out_shape=shaped((peers, 64, NS), BF16),
        compiler_params=params,
        cost_estimate=cost(1),
        name="state_scan",
    )(got)
    states = lax.all_to_all(carried, "ctx", 0, 0, tiled=True)

    high, red_loc, dbc = pl.pallas_call(
        block_kernel,
        grid=(steps,),
        in_specs=[
            stack(2), columns(rows), row_spec, whole((rows, 256)), whole((2, 256, rows)),
            by_channel,
        ],
        out_specs=[stack(3), local_spec, square],
        out_shape=[
            stored((3, channels, rows), F32), stored((3, heads, rows), F32),
            stored((256, rows), F32),
        ],
        scratch_shapes=[
            pltpu.VMEM((rows, rows), F32), pltpu.VMEM((rows, rows), F32),
            pltpu.VMEM((steps, rows, PER), F32), pltpu.VMEM((rows, rows), F32),
            pltpu.VMEM((HD, rows), F32), pltpu.VMEM((HD, rows), F32),
        ],
        compiler_params=params,
        cost_estimate=cost(8),
        name="in_block",
    )(*from_hbm(low, grad_y, head_rows, bctok, bclow, slope))

    state_spec = pl.BlockSpec((8, 64, NS), lambda i: (i, 0, 0))
    pay_bc = pl.pallas_call(
        bc_kernel,
        grid=(1,),
        in_specs=[
            one((peers, 64, NS)), one((2, channels, rows)), square, square,
            whole((2, 256, rows)), whole((256, 128)), row_spec,
        ],
        out_specs=whole((shares, share + 8, 256)),
        out_shape=shaped((shares, share + 8, 256), BF16),
        compiler_params=params,
        cost_estimate=cost(4),
        name="bc_part",
    )(states, *from_hbm(scaled, dbc, bcslope, bclow, bcsides, head_rows))
    got_bc = lax.all_to_all(pay_bc, "head", 0, 0, tiled=True)

    side_rows = 8 + 2 * RIM
    ssd_out, gx, sides, grad_dt, gh = pl.pallas_call(
        x_kernel,
        grid=(steps,),
        in_specs=[
            state_spec, stack(3), stack(3), wide_spec, row_spec, whole((rows, 256)), local_spec,
        ],
        out_specs=[
            columns(rows), columns(rows), columns(side_rows), whole((heads, rows)),
            whole((8, 128)),
        ],
        out_shape=[
            stored((rows, channels), BF16), stored((rows, channels), BF16),
            stored((side_rows, channels), F32), stored((heads, rows), F32),
            stored((8, 128), F32),
        ],
        scratch_shapes=[pltpu.VMEM((2, heads, rows), F32)],
        compiler_params=params,
        cost_estimate=cost(10),
        name="x_part",
    )(states, *from_hbm(low, high, sides_in, head_rows, bctok, red_loc))

    vmem = pl.BlockSpec(memory_space=pltpu.VMEM)
    width = channels + 256 + 128
    sums, own_bc, spills = pl.pallas_call(
        pack_kernel,
        in_specs=[vmem] * 3,
        out_specs=[vmem] * 3,
        out_shape=[
            shaped((4, width), F32), shaped((share, 256), F32),
            shaped((8, channels + 256), F32),
        ],
        compiler_params=params,
        cost_estimate=cost(1),
        name="pack_sums",
    )(got_bc, *from_hbm(sides, gh))
    parts = summed_over_ctx(sums)
    spills = passed_along(spills, -1)
    grad_x, grad_bc = pl.pallas_call(
        patch_kernel,
        grid=(1,),
        in_specs=[
            pl.BlockSpec(memory_space=pl.ANY), whole((side_rows, channels)), whole((share, 256)),
            whole((8, channels + 256)),
        ],
        out_specs=[
            pl.BlockSpec((RIM, channels), lambda i: (rows // RIM - 1, 0)), whole((share, 256)),
        ],
        out_shape=[stored((rows, channels), BF16), stored((share, 256), F32)],
        input_output_aliases={0: 0},
        compiler_params=params,
        cost_estimate=cost(1),
        name="last_rows",
    )(*from_hbm(gx, sides), own_bc, spills)
    grad_wx, grad_wbc, grad_heads = pl.pallas_call(
        finish_kernel,
        in_specs=[vmem] * 4,
        out_specs=[vmem] * 3,
        out_shape=[stored((4, channels), F32), stored((4, 256), F32), stored((3, heads), F32)],
        compiler_params=params,
        cost_estimate=cost(1),
        name="finish_sums",
    )(*parts)
    return ssd_out, grad_x, grad_bc, grad_dt.T, grad_wx, grad_wbc, grad_heads


def solution(mesh):
    in_specs = (
        P("ctx", "head"), P("ctx", None), P("ctx", "head"), P(None, "head"), P(),
        P("head"), P("head"), P("head"), P(), P("ctx", "head"),
    )
    out_specs = (
        P("ctx", "head"), P("ctx", "head"), P(("ctx", "head"), None), P("ctx", "head"),
        P(None, "head"), P(), P(None, "head"),
    )
    return jax.shard_map(local, mesh=mesh, in_specs=in_specs, out_specs=out_specs, check_vma=False)
```

```python
import jax
import jax.numpy as jnp
from jax import lax
from jax.experimental import pallas as pl
from jax.experimental.pallas import tpu as pltpu
from jax.sharding import PartitionSpec as P

F32 = jnp.float32
BF16 = jnp.bfloat16

BLK = 256
HD = 64
NS = 128
RIM = 16
PER = BLK // HD
VMEM = 24 * 1024 * 1024

DT, CUMUL, CARRY, END, SIG, SKIP, RATE, MASK = range(8)


def mm(a, b):
    return lax.dot_general(a, b, (((1,), (0,)), ((), ())), preferred_element_type=F32)


def mm_nt(a, b):
    return lax.dot_general(a, b, (((1,), (1,)), ((), ())), preferred_element_type=F32)


def split(value, count):
    parts = []
    for _ in range(count):
        part = value.astype(BF16)
        parts.append(part)
        value = value - part.astype(F32)
    return parts


def pick_nt(pick, value, count):
    return sum(mm_nt(pick, part) for part in split(value, count))


def pick_right(value, pick, count):
    return sum(mm(part, pick) for part in split(value, count))


def iota(shape, dim):
    return lax.broadcasted_iota(jnp.int32, shape, dim)


def eye(n, dtype):
    return (iota((n, n), 0) == iota((n, n), 1)).astype(dtype)


def conv_own(raw, taps, masks):
    lane = iota((raw.shape[0], 128), 1)
    total = taps[:, 3:4] * raw
    for j in range(1, 4):
        rolled = pltpu.roll(raw, j, 1)
        shifted = jnp.concatenate(
            [jnp.where(lane < j, 0.0, rolled[:, :128]), rolled[:, 128:]], axis=1
        )
        total = total + shifted * (taps[:, 3 - j : 4 - j] * masks[3 - j])
    return total


def conv_rim(rim, taps, masks):
    lane = iota(rim.shape, 1)
    total = jnp.zeros(rim.shape, F32)
    for j in range(1, 4):
        before = jnp.where(lane < j, pltpu.roll(rim, j, 1), 0.0)
        total = total + before * (taps[:, 3 - j : 4 - j] * masks[3 - j][:, :128])
    return total


def conv_back(g, raw, rim, taps, masks):
    lane = iota((g.shape[0], 128), 1)
    grad = taps[:, 3:4] * g
    spill = jnp.zeros((g.shape[0], 128), F32)
    product = g * raw
    products = [None, None, None, product[:, :128] + product[:, 128:]]
    for j in range(1, 4):
        masked = g * masks[3 - j]
        rolled = pltpu.roll(masked, g.shape[1] - j, 1)
        wrapped = lane >= 128 - j
        first = rolled[:, :128]
        second = jnp.where(wrapped, 0.0, rolled[:, 128:])
        outer = jnp.where(wrapped, rolled[:, 128:], 0.0)
        tap = taps[:, 3 - j : 4 - j]
        grad = grad + tap * jnp.concatenate([first, second], axis=1)
        spill = spill + tap * outer
        products[3 - j] = first * raw[:, :128] + second * raw[:, 128:] + outer * rim
    chosen = (iota((512, 128), 0) // 128 == iota((512, 128), 1)).astype(BF16)
    sums = pick_right(jnp.concatenate(products, axis=1), chosen, 2)
    moved = pltpu.roll(spill, 128 - RIM, 1)
    sides = jnp.where(lane >= 128 - RIM, grad[:, 128:], jnp.where(lane >= 96, moved, sums))
    return grad, sides


def wide_rim(rim):
    return jnp.concatenate([jnp.zeros((128 - RIM, rim.shape[1]), BF16), rim], axis=0)


def masks_of(rows_ref):
    return [rows_ref[MASK, k : k + 1, :] for k in range(4)]


def head_row(rows_ref, plane, head):
    return rows_ref[plane, pl.ds(head, 1), :]


def taps_of(w):
    padded = jnp.concatenate([w, jnp.zeros((124, BLK), F32)], axis=0)
    return jnp.transpose(padded)


def conv_all(raw_ref, rim_ref, taps, masks):
    ident = eye(BLK, BF16)
    raw = mm_nt(ident, raw_ref[...])
    rim = mm_nt(ident, wide_rim(rim_ref[...]))
    pre = conv_own(raw, taps, masks)
    pre = jnp.concatenate([pre[:, :128] + conv_rim(rim, taps, masks), pre[:, 128:]], axis=1)
    return raw, rim, pre


def with_taps(rim, taps):
    return jnp.where(iota(rim.shape, 1) < 4, taps, rim)


def sigmoid(value):
    return 1.0 / (1.0 + jnp.exp(-value))


def rim_kernel(x_ref, bc_ref, out_ref, sems):
    rows, width = x_ref.shape
    copies = [
        pltpu.make_async_copy(
            x_ref.at[pl.ds(rows - RIM, RIM), :], out_ref.at[:, pl.ds(0, width)], sems.at[0]
        ),
        pltpu.make_async_copy(
            bc_ref.at[pl.ds(rows - RIM, RIM), :],
            out_ref.at[:, pl.ds(width, bc_ref.shape[1])],
            sems.at[1],
        ),
    ]
    for copy in copies:
        copy.start()
    for copy in copies:
        copy.wait()


def head_rows_of(rows_ref, seg_ref, rate_ref, bias_ref, skip_ref, dt_ref):
    here = lax.axis_index("ctx")
    own = [seg_ref[pl.ds(2 * here + half, 1), :] for half in range(2)]
    target = jnp.concatenate(own, axis=1).astype(F32)
    before = seg_ref[pl.ds(jnp.maximum(2 * here - 1, 0), 1), :].astype(F32)
    before = jnp.where(here == 0, -1.0, before)
    lane = iota((1, 128), 1)
    masks = []
    for j in (3, 2, 1):
        rolled = pltpu.roll(target, j, 1)
        first = jnp.where(lane < j, pltpu.roll(before, j, 1), rolled[:, :128])
        shifted = jnp.concatenate([first, rolled[:, 128:]], axis=1)
        masks.append((shifted == target).astype(F32))
    rows_ref[MASK] = jnp.concatenate(
        masks + [jnp.ones((1, BLK), F32), target, jnp.zeros((11, BLK), F32)], axis=0
    )
    heads = dt_ref.shape[0]
    values = jnp.concatenate(
        [rate_ref[...], bias_ref[...], skip_ref[...], jnp.zeros((5, heads), F32)], axis=0
    )
    per_head = pick_nt(eye(heads, BF16), values, 3)
    rate = jnp.exp(per_head[:, 0:1])
    pre = dt_ref[...] + per_head[:, 1:2]
    dt = jnp.maximum(pre, 0.0) + jnp.log1p(jnp.exp(-jnp.abs(pre)))
    upto = (iota((BLK, BLK), 0) <= iota((BLK, BLK), 1)).astype(BF16)
    cumul = pick_right(-rate * dt, upto, 3)
    keep = (target == before[:, 127:]).astype(F32)
    same_end = target == target[:, BLK - 1 :]
    rows_ref[DT] = dt
    rows_ref[CUMUL] = cumul
    rows_ref[CARRY] = keep * jnp.exp(cumul)
    rows_ref[END] = jnp.exp(jnp.where(same_end, cumul[:, BLK - 1 :] - cumul, -jnp.inf))
    rows_ref[SIG] = sigmoid(pre)
    rows_ref[SKIP] = jnp.broadcast_to(per_head[:, 2:3], (heads, BLK))
    rows_ref[RATE] = jnp.broadcast_to(rate, (heads, BLK))


def state_kernel(
    x_ref, rim_ref, gy_ref, wx_ref, bc_ref, rimbc_ref, wbc_ref, seg_ref, rate_ref, bias_ref,
    skip_ref, dt_ref,
    pay_ref, rows_ref, bctok_ref,
):
    step = pl.program_id(0)
    ident = eye(BLK, BF16)

    @pl.when(step == 0)
    def _():
        head_rows_of(rows_ref, seg_ref, rate_ref, bias_ref, skip_ref, dt_ref)
        _, _, pre = conv_all(bc_ref, rimbc_ref, taps_of(wbc_ref[...]), masks_of(rows_ref))
        bctok_ref[...] = mm_nt(ident, (pre * sigmoid(pre)).astype(BF16)).astype(BF16)

    _, _, pre = conv_all(x_ref, rim_ref, taps_of(wx_ref[...]), masks_of(rows_ref))
    act = (pre * sigmoid(pre)).astype(BF16).astype(F32)
    dy = mm_nt(ident, gy_ref[...])
    ends, carries = [], []
    for k in range(PER):
        head = step * PER + k
        lo, hi = k * HD, (k + 1) * HD
        carry = head_row(rows_ref, CARRY, head)
        weight = head_row(rows_ref, END, head) * head_row(rows_ref, DT, head)
        ends.append((weight * act[lo:hi]).astype(BF16))
        carries.append((carry * dy[lo:hi]).astype(BF16))
        parts = split(carry[:, BLK - 1 :], 3)
        which = iota((8, NS), 0)
        through = jnp.where(
            which == 0, parts[0].astype(F32),
            jnp.where(which == 1, parts[1].astype(F32), parts[2].astype(F32)),
        ).astype(BF16)
        pay_ref[2 * k, 64:72, :] = through
        pay_ref[2 * k + 1, 64:72, :] = through
    state = mm(jnp.concatenate(ends, axis=0), bctok_ref[:, :NS]).astype(BF16)
    back = mm(jnp.concatenate(carries, axis=0), bctok_ref[:, NS:]).astype(BF16)
    for j in range(2 * PER):
        pay_ref[j, 0:32, :] = state[j * 32 : j * 32 + 32]
        pay_ref[j, 32:64, :] = back[j * 32 : j * 32 + 32]


def slope_kernel(
    x_ref, rim_ref, gy_ref, wx_ref, bc_ref, rimbc_ref, wbc_ref, rows_ref,
    low_ref, slope_ref, scaled_ref, sides_ref, bclow_ref, bcslope_ref, bcsides_ref,
):
    step = pl.program_id(0)
    masks = masks_of(rows_ref)

    @pl.when(step == 0)
    def _():
        taps = taps_of(wbc_ref[...])
        raw, rim, pre = conv_all(bc_ref, rimbc_ref, taps, masks)
        bcsides_ref[...] = with_taps(rim, taps)
        sig = sigmoid(pre)
        bclow_ref[0] = raw.astype(BF16)
        bclow_ref[1] = (pre * sig).astype(BF16)
        bcslope_ref[...] = sig * (1.0 + pre * (1.0 - sig))

    taps = taps_of(wx_ref[...])
    raw, rim, pre = conv_all(x_ref, rim_ref, taps, masks)
    sides_ref[...] = with_taps(rim, taps)
    sig = sigmoid(pre)
    slope_ref[...] = sig * (1.0 + pre * (1.0 - sig))
    low = (pre * sig).astype(BF16)
    dy = mm_nt(eye(BLK, BF16), gy_ref[...])
    low_ref[0] = low
    low_ref[1] = dy.astype(BF16)
    low_ref[2] = raw.astype(BF16)
    act = low.astype(F32)
    for k in range(PER):
        head = step * PER + k
        lo, hi = k * HD, (k + 1) * HD
        weight = head_row(rows_ref, END, head) * head_row(rows_ref, DT, head)
        scaled_ref[0, lo:hi, :] = (weight * act[lo:hi]).astype(BF16)
        scaled_ref[1, lo:hi, :] = (head_row(rows_ref, CARRY, head) * dy[lo:hi]).astype(BF16)


def block_kernel(
    low_ref, gy_ref, rows_ref, bctok_ref, bclow_ref, slope_ref,
    high_ref, red_ref, dbc_ref,
    scores_ref, link_ref, acol_ref, dg_ref, yt_ref, du_ref,
):
    step = pl.program_id(0)

    @pl.when(step == 0)
    def _():
        ident = eye(BLK, BF16)
        scores_ref[...] = mm_nt(bctok_ref[:, NS:], bctok_ref[:, :NS])
        seg_row = rows_ref[MASK, 4:5, :]
        seg_col = mm_nt(ident, rows_ref[MASK].astype(BF16))[:, 4:5]
        later = iota((BLK, BLK), 0) >= iota((BLK, BLK), 1)
        linked = jnp.logical_and(later, seg_col == seg_row)
        link_ref[...] = jnp.where(linked, 0.0, -jnp.inf)
        dg_ref[...] = jnp.zeros_like(dg_ref)
        cumul = pick_nt(ident, rows_ref[CUMUL], 3)
        for at in range(acol_ref.shape[0]):
            acol_ref[at] = cumul[:, at * PER : (at + 1) * PER]

    acols = acol_ref[step]
    for k in range(PER):
        head = step * PER + k
        lo, hi = k * HD, (k + 1) * HD
        arow = head_row(rows_ref, CUMUL, head)
        dt = head_row(rows_ref, DT, head)
        skip = head_row(rows_ref, SKIP, head)
        u_low = (dt * low_ref[0, lo:hi, :].astype(F32)).astype(BF16)
        du_first = None
        for tb in range(2):
            t0, t1 = tb * 128, tb * 128 + 128
            decay = jnp.exp(acols[t0:t1, k : k + 1] - arow[:, :t1] + link_ref[t0:t1, :t1])
            mixed = (decay * scores_ref[t0:t1, :t1]).astype(BF16)
            yt_ref[:, t0:t1] = mm_nt(u_low[:, :t1], mixed)
            du = mm(low_ref[1, lo:hi, t0:t1], mixed)
            if tb == 0:
                du_first = du
            else:
                du_ref[:, :128] = du_first + du[:, :128]
                du_ref[:, 128:] = du[:, 128:]
            dmix = mm(gy_ref[t0:t1, lo:hi], u_low[:, :t1])
            dg_ref[t0:t1, :t1] += decay * dmix
        x_h = low_ref[0, lo:hi, :].astype(F32)
        dy_h = low_ref[1, lo:hi, :].astype(F32)
        y_h = yt_ref[...]
        du_h = du_ref[...]
        slope = slope_ref[lo:hi, :]
        high_ref[0, lo:hi, :] = y_h + skip * x_h
        high_ref[1, lo:hi, :] = slope * (dt * du_h + skip * dy_h)
        high_ref[2, lo:hi, :] = slope * (dt * head_row(rows_ref, END, head))
        ga = jnp.sum(dy_h * y_h - u_low.astype(F32) * du_h, axis=0, keepdims=True)
        red_ref[0, pl.ds(head, 1), :] = ga
        red_ref[1, pl.ds(head, 1), :] = jnp.sum(x_h * du_h, axis=0, keepdims=True)
        red_ref[2, pl.ds(head, 1), :] = jnp.sum(x_h * dy_h, axis=0, keepdims=True)

    @pl.when(step == pl.num_programs(0) - 1)
    def _():
        dg = dg_ref[...].astype(BF16)
        dbc_ref[:NS, :] = mm(bclow_ref[1, NS:, :], dg)
        dbc_ref[NS:, :] = mm_nt(bclow_ref[1, :NS, :], dg)


def scan_kernel(in_ref, out_ref):
    peers = in_ref.shape[0]
    ahead = jnp.zeros((32, NS), F32)
    behind = jnp.zeros((32, NS), F32)

    def through(at):
        parts = in_ref[at, 64:72, :].astype(F32)
        return parts[0:1] + parts[1:2] + parts[2:3]

    for i in range(peers):
        out_ref[i, 0:32, :] = ahead.astype(BF16)
        ahead = through(i) * ahead + in_ref[i, 0:32, :].astype(F32)
        at = peers - 1 - i
        out_ref[at, 32:64, :] = behind.astype(BF16)
        behind = through(at) * behind + in_ref[at, 32:64, :].astype(F32)


def bc_kernel(
    state_ref, scaled_ref, dbc_ref, bcslope_ref, bclow_ref, bcsides_ref, rows_ref, pay_ref
):
    small = eye(NS, BF16)
    channels = scaled_ref.shape[1]
    state_in = state_ref[:, 0:32, :].reshape(channels, NS)
    state_back = state_ref[:, 32:64, :].reshape(channels, NS)
    grad_b = mm(mm_nt(small, state_back).astype(BF16), scaled_ref[0])
    grad_c = mm(mm_nt(small, state_in).astype(BF16), scaled_ref[1])
    grad_act = dbc_ref[...] + jnp.concatenate([grad_b, grad_c], axis=0)
    grad, sides = conv_back(
        grad_act * bcslope_ref[...], bclow_ref[0].astype(F32), bcsides_ref[...],
        bcsides_ref[...], masks_of(rows_ref),
    )
    token = mm_nt(eye(BLK, BF16), grad.astype(BF16)).astype(BF16)
    row = iota((8, 128), 0)
    pick = (jnp.where(row < 4, row, row + 104) == iota((8, 128), 1)).astype(BF16)
    rest = mm_nt(pick, sides.astype(BF16)).astype(BF16)
    shares = pay_ref.shape[0]
    share = BLK // shares
    for j in range(shares):
        pay_ref[j, 0:share, :] = token[j * share : (j + 1) * share]
        pay_ref[j, share : share + 8, :] = rest


def x_kernel(
    state_ref, low_ref, high_ref, taps_ref, rows_ref, bctok_ref, local_ref,
    out_ref, gx_ref, sides_ref, gdt_ref, gh_ref,
    red_ref,
):
    step = pl.program_id(0)
    ident = eye(BLK, BF16)
    masks = masks_of(rows_ref)
    state_in = state_ref[:, 0:32, :].reshape(BLK, NS)
    state_back = state_ref[:, 32:64, :].reshape(BLK, NS)
    carried = mm_nt(state_in, bctok_ref[:, NS:])
    from_end = mm_nt(state_back, bctok_ref[:, :NS])
    both = state_in.astype(F32) * state_back.astype(F32)
    last_lane = iota((1, BLK), 1) == BLK - 1
    y_parts = []
    for k in range(PER):
        head = step * PER + k
        lo, hi = k * HD, (k + 1) * HD
        dt = head_row(rows_ref, DT, head)
        carry = head_row(rows_ref, CARRY, head)
        end = head_row(rows_ref, END, head)
        x_h = low_ref[0, lo:hi, :].astype(F32)
        add = carry * carried[lo:hi]
        fed = end * jnp.sum(x_h * from_end[lo:hi], axis=0, keepdims=True)
        from_step = dt * fed
        at_end = jnp.sum(from_step, axis=1, keepdims=True)
        joint = jnp.sum(jnp.sum(both[lo:hi], axis=0, keepdims=True), axis=1, keepdims=True)
        at_end = at_end + carry[:, BLK - 1 :] * joint
        ga = jnp.sum(low_ref[1, lo:hi, :].astype(F32) * add, axis=0, keepdims=True) - from_step
        red_ref[0, pl.ds(head, 1), :] = ga + jnp.where(last_lane, at_end, 0.0)
        red_ref[1, pl.ds(head, 1), :] = fed
        y_parts.append((high_ref[0, lo:hi, :] + add).astype(BF16))
    out_ref[...] = mm_nt(ident, jnp.concatenate(y_parts, axis=0)).astype(BF16)
    grad, sides = conv_back(
        high_ref[1] + high_ref[2] * from_end, low_ref[2].astype(F32),
        taps_ref[...], taps_ref[...], masks,
    )
    gx_ref[...] = mm_nt(ident, grad.astype(BF16)).astype(BF16)
    row = iota((8 + 2 * RIM, 128), 0)
    pick = (jnp.where(row < 8, row, row + 88) == iota((8 + 2 * RIM, 128), 1)).astype(BF16)
    sides_ref[...] = pick_nt(pick, sides, 2)

    @pl.when(step == pl.num_programs(0) - 1)
    def _():
        later = (iota((BLK, BLK), 0) >= iota((BLK, BLK), 1)).astype(BF16)
        grad_log = pick_right(local_ref[0] + red_ref[0], later, 3)
        rate = rows_ref[RATE]
        grad_step = (local_ref[1] + red_ref[1] - rate * grad_log) * rows_ref[SIG]
        gdt_ref[...] = grad_step
        which = iota((8, BLK), 0)
        terms = (-rate * rows_ref[DT] * grad_log, grad_step, local_ref[2])
        gh_ref[...] = jnp.zeros_like(gh_ref)
        gh_ref[:, : rate.shape[0]] = sum(
            pick_nt((which == k).astype(BF16), term, 3) for k, term in enumerate(terms)
        )


def patch_kernel(gx_ref, sides_ref, own_ref, spill_ref, out_ref, bc_ref):
    del gx_ref
    width = sides_ref.shape[1]
    spill = jnp.concatenate([jnp.zeros((RIM - 8, width), F32), spill_ref[:, :width]], axis=0)
    out_ref[...] = (sides_ref[8 + RIM :, :] + spill).astype(BF16)
    share = own_ref.shape[0]
    bc_ref[: share - 8, :] = own_ref[: share - 8, :]
    is_last = lax.axis_index("head") == lax.axis_size("head") - 1
    came = spill_ref[:, width:]
    bc_ref[share - 8 :, :] = own_ref[share - 8 :, :] + jnp.where(is_last, came, 0.0)


def pack_kernel(got_ref, sides_ref, gh_ref, sums_ref, own_ref, out_ref):
    share = own_ref.shape[0]
    total = jnp.sum(got_ref[...].astype(F32), axis=0)
    own_ref[...] = total[:share]
    width = sides_ref.shape[1]
    rest = total[share:]
    out_ref[:, :width] = sides_ref[RIM : 8 + RIM, :]
    out_ref[:, width:] = jnp.where(iota(rest.shape, 0) < 4, 0.0, rest)
    sums_ref[:, :width] = sides_ref[:4, :]
    sums_ref[:, width : width + 256] = rest[:4]
    sums_ref[:, width + 256 :] = gh_ref[:4, :]


def finish_kernel(a_ref, b_ref, c_ref, d_ref, wx_ref, wbc_ref, heads_ref):
    total = (a_ref[...] + b_ref[...]) + (c_ref[...] + d_ref[...])
    width = wx_ref.shape[1]
    wx_ref[...] = total[:4, :width]
    wbc_ref[...] = total[:4, width : width + 256]
    heads_ref[...] = total[:3, width + 256 : width + 256 + heads_ref.shape[1]]


def whole(shape):
    zeros = (0,) * len(shape)
    return pl.BlockSpec(shape, lambda *_: zeros)


def columns(rows):
    return pl.BlockSpec((rows, BLK), lambda i: (0, i))


def channel_rows(width):
    return pl.BlockSpec((BLK, width), lambda i: (i, 0))


def shaped(shape, dtype):
    return jax.ShapeDtypeStruct(shape, dtype)


def stored(shape, dtype):
    return pltpu.HBM(shape, dtype)


def from_hbm(*values):
    return [pltpu.with_memory_space_constraint(value, pltpu.HBM) for value in values]


def passed_along(value, by):
    peers = lax.axis_size("ctx")
    return lax.ppermute(value, "ctx", [(i, (i + by) % peers) for i in range(peers)])


def summed_over_ctx(value):
    peers = lax.axis_size("ctx")

    def moved(value, to):
        return lax.ppermute(value, "ctx", [(i, to(i)) for i in range(peers)])

    def turned(i, stride, by):
        at = i // stride % 4
        return i + ((at + by) % 4 - at) * stride

    def swap(i):
        return i ^ 1

    def terms(value, stride):
        near = moved(value, lambda i: turned(i, stride, 1 if i % 2 else 3))
        far = moved(value, lambda i: turned(i, stride, 2))
        return value, far, near, moved(near, swap)

    value = value + moved(value, swap)
    own, far, near, other = terms(value, 2)
    return terms((own + far) + (near + other), 8)


def cost(micros):
    return pl.CostEstimate(
        flops=int(micros * 1e8), bytes_accessed=int(micros * 3e6), transcendentals=0
    )


def local(x_raw, bc_raw, dt_raw, conv_x, conv_bc, a_log, dt_bias, skip_weight, segment, grad_y):
    rows, channels = x_raw.shape
    heads = dt_raw.shape[1]
    steps = channels // BLK
    peers = lax.axis_size("ctx")
    shares = lax.axis_size("head")
    share = rows // shares
    params = pltpu.CompilerParams(vmem_limit_bytes=VMEM)
    last_inputs = pl.pallas_call(
        rim_kernel,
        in_specs=[pl.BlockSpec(memory_space=pl.ANY)] * 2,
        out_specs=pl.BlockSpec(memory_space=pltpu.VMEM),
        out_shape=shaped((RIM, channels + 256), BF16),
        scratch_shapes=[pltpu.SemaphoreType.DMA((2,))],
        compiler_params=params,
        name="rim_rows",
    )(*from_hbm(x_raw, bc_raw))
    rim = passed_along(last_inputs, 1)
    row_spec = whole((8, heads, rows))
    square = whole((256, rows))
    by_channel = channel_rows(rows)

    def chan(dtype):
        return stored((channels, rows), dtype)

    rim_bc_spec = pl.BlockSpec((RIM, 256), lambda i: (0, channels // 256))
    local_spec = whole((3, heads, rows))

    def stack(count):
        return pl.BlockSpec((count, BLK, rows), lambda i: (0, i, 0))

    wide_spec = channel_rows(128)

    def one(shape):
        return pl.BlockSpec(shape, lambda i: (0,) * len(shape))

    pay, head_rows, bctok = pl.pallas_call(
        state_kernel,
        grid=(steps,),
        in_specs=[
            columns(rows), columns(RIM), columns(rows), columns(4),
            one((rows, 256)), rim_bc_spec, one((4, 256)),
            one(segment_rows := (segment.shape[0] // 128, 128)), one((1, heads)), one((1, heads)),
            one((1, heads)), one((heads, rows)),
        ],
        out_specs=[
            pl.BlockSpec((8, 72, NS), lambda i: (i, 0, 0)), row_spec, whole((rows, 256)),
        ],
        out_shape=[
            shaped((peers, 72, NS), BF16),
            stored((8, heads, rows), F32), stored((rows, 256), BF16),
        ],
        compiler_params=params,
        cost_estimate=cost(7),
        name="states",
    )(
        *from_hbm(x_raw), rim, *from_hbm(grad_y, conv_x, bc_raw), rim,
        *from_hbm(
            conv_bc, segment.reshape(segment_rows), a_log[None], dt_bias[None],
            skip_weight[None], dt_raw.T,
        ),
    )

    got = lax.all_to_all(pay, "ctx", 0, 0, tiled=True)

    low, slope, scaled, sides_in, bclow, bcslope, bcsides = pl.pallas_call(
        slope_kernel,
        grid=(steps,),
        in_specs=[
            columns(rows), columns(RIM), columns(rows), columns(4), whole((rows, 256)),
            rim_bc_spec, whole((4, 256)), row_spec,
        ],
        out_specs=[
            stack(3), by_channel, stack(2), wide_spec, whole((2, 256, rows)), square,
            whole((256, 128)),
        ],
        out_shape=[
            stored((3, channels, rows), BF16), chan(F32), stored((2, channels, rows), BF16),
            stored((channels, 128), F32), stored((2, 256, rows), BF16), stored((256, rows), F32),
            stored((256, 128), F32),
        ],
        compiler_params=params,
        cost_estimate=cost(6),
        name="slopes",
    )(*from_hbm(x_raw, rim, grad_y, conv_x, bc_raw, rim, conv_bc, head_rows))
    got, low = lax.optimization_barrier((got, low))

    carried = pl.pallas_call(
        scan_kernel,
        in_specs=[pl.BlockSpec(memory_space=pltpu.VMEM)],
        out_specs=pl.BlockSpec(memory_space=pltpu.VMEM),
        out_shape=shaped((peers, 64, NS), BF16),
        compiler_params=params,
        cost_estimate=cost(1),
        name="state_scan",
    )(got)
    states = lax.all_to_all(carried, "ctx", 0, 0, tiled=True)

    high, red_loc, dbc = pl.pallas_call(
        block_kernel,
        grid=(steps,),
        in_specs=[
            stack(2), columns(rows), row_spec, whole((rows, 256)), whole((2, 256, rows)),
            by_channel,
        ],
        out_specs=[stack(3), local_spec, square],
        out_shape=[
            stored((3, channels, rows), F32), stored((3, heads, rows), F32),
            stored((256, rows), F32),
        ],
        scratch_shapes=[
            pltpu.VMEM((rows, rows), F32), pltpu.VMEM((rows, rows), F32),
            pltpu.VMEM((steps, rows, PER), F32), pltpu.VMEM((rows, rows), F32),
            pltpu.VMEM((HD, rows), F32), pltpu.VMEM((HD, rows), F32),
        ],
        compiler_params=params,
        cost_estimate=cost(8),
        name="in_block",
    )(*from_hbm(low, grad_y, head_rows, bctok, bclow, slope))

    state_spec = pl.BlockSpec((8, 64, NS), lambda i: (i, 0, 0))
    pay_bc = pl.pallas_call(
        bc_kernel,
        grid=(1,),
        in_specs=[
            one((peers, 64, NS)), one((2, channels, rows)), square, square,
            whole((2, 256, rows)), whole((256, 128)), row_spec,
        ],
        out_specs=whole((shares, share + 8, 256)),
        out_shape=shaped((shares, share + 8, 256), BF16),
        compiler_params=params,
        cost_estimate=cost(4),
        name="bc_part",
    )(states, *from_hbm(scaled, dbc, bcslope, bclow, bcsides, head_rows))
    got_bc = lax.all_to_all(pay_bc, "head", 0, 0, tiled=True)

    side_rows = 8 + 2 * RIM
    ssd_out, gx, sides, grad_dt, gh = pl.pallas_call(
        x_kernel,
        grid=(steps,),
        in_specs=[
            state_spec, stack(3), stack(3), wide_spec, row_spec, whole((rows, 256)), local_spec,
        ],
        out_specs=[
            columns(rows), columns(rows), columns(side_rows), whole((heads, rows)),
            whole((8, 128)),
        ],
        out_shape=[
            stored((rows, channels), BF16), stored((rows, channels), BF16),
            stored((side_rows, channels), F32), stored((heads, rows), F32),
            stored((8, 128), F32),
        ],
        scratch_shapes=[pltpu.VMEM((2, heads, rows), F32)],
        compiler_params=params,
        cost_estimate=cost(10),
        name="x_part",
    )(states, *from_hbm(low, high, sides_in, head_rows, bctok, red_loc))

    vmem = pl.BlockSpec(memory_space=pltpu.VMEM)
    width = channels + 256 + 128
    sums, own_bc, spills = pl.pallas_call(
        pack_kernel,
        in_specs=[vmem] * 3,
        out_specs=[vmem] * 3,
        out_shape=[
            shaped((4, width), F32), shaped((share, 256), F32),
            shaped((8, channels + 256), F32),
        ],
        compiler_params=params,
        cost_estimate=cost(1),
        name="pack_sums",
    )(got_bc, *from_hbm(sides, gh))
    parts = summed_over_ctx(sums)
    spills = passed_along(spills, -1)
    grad_x, grad_bc = pl.pallas_call(
        patch_kernel,
        grid=(1,),
        in_specs=[
            pl.BlockSpec(memory_space=pl.ANY), whole((side_rows, channels)), whole((share, 256)),
            whole((8, channels + 256)),
        ],
        out_specs=[
            pl.BlockSpec((RIM, channels), lambda i: (rows // RIM - 1, 0)), whole((share, 256)),
        ],
        out_shape=[stored((rows, channels), BF16), stored((share, 256), F32)],
        input_output_aliases={0: 0},
        compiler_params=params,
        cost_estimate=cost(1),
        name="last_rows",
    )(*from_hbm(gx, sides), own_bc, spills)
    grad_wx, grad_wbc, grad_heads = pl.pallas_call(
        finish_kernel,
        in_specs=[vmem] * 4,
        out_specs=[vmem] * 3,
        out_shape=[stored((4, channels), F32), stored((4, 256), F32), stored((3, heads), F32)],
        compiler_params=params,
        cost_estimate=cost(1),
        name="finish_sums",
    )(*parts)
    return ssd_out, grad_x, grad_bc, grad_dt.T, grad_wx, grad_wbc, grad_heads


def solution(mesh):
    in_specs = (
        P("ctx", "head"), P("ctx", None), P("ctx", "head"), P(None, "head"), P(),
        P("head"), P("head"), P("head"), P(), P("ctx", "head"),
    )
    out_specs = (
        P("ctx", "head"), P("ctx", "head"), P(("ctx", "head"), None), P("ctx", "head"),
        P(None, "head"), P(), P(None, "head"),
    )
    return jax.shard_map(local, mesh=mesh, in_specs=in_specs, out_specs=out_specs, check_vma=False)
```

```python
import jax
import jax.numpy as jnp
from jax import lax
from jax.experimental import pallas as pl
from jax.experimental.pallas import tpu as pltpu
from jax.sharding import PartitionSpec as P

F32 = jnp.float32
BF16 = jnp.bfloat16

BLK = 256
HD = 64
NS = 128
RIM = 16
PER = BLK // HD
VMEM = 24 * 1024 * 1024

DT, CUMUL, CARRY, END, SIG, SKIP, RATE, MASK = range(8)


def mm(a, b):
    return lax.dot_general(a, b, (((1,), (0,)), ((), ())), preferred_element_type=F32)


def mm_nt(a, b):
    return lax.dot_general(a, b, (((1,), (1,)), ((), ())), preferred_element_type=F32)


def split(value, count):
    parts = []
    for _ in range(count):
        part = value.astype(BF16)
        parts.append(part)
        value = value - part.astype(F32)
    return parts


def pick_nt(pick, value, count):
    return sum(mm_nt(pick, part) for part in split(value, count))


def pick_right(value, pick, count):
    return sum(mm(part, pick) for part in split(value, count))


def iota(shape, dim):
    return lax.broadcasted_iota(jnp.int32, shape, dim)


def eye(n, dtype):
    return (iota((n, n), 0) == iota((n, n), 1)).astype(dtype)


def conv_own(raw, taps, masks):
    lane = iota((raw.shape[0], 128), 1)
    total = taps[:, 3:4] * raw
    for j in range(1, 4):
        rolled = pltpu.roll(raw, j, 1)
        shifted = jnp.concatenate(
            [jnp.where(lane < j, 0.0, rolled[:, :128]), rolled[:, 128:]], axis=1
        )
        total = total + shifted * (taps[:, 3 - j : 4 - j] * masks[3 - j])
    return total


def conv_rim(rim, taps, masks):
    lane = iota(rim.shape, 1)
    total = jnp.zeros(rim.shape, F32)
    for j in range(1, 4):
        before = jnp.where(lane < j, pltpu.roll(rim, j, 1), 0.0)
        total = total + before * (taps[:, 3 - j : 4 - j] * masks[3 - j][:, :128])
    return total


def conv_back(g, raw, rim, taps, masks):
    lane = iota((g.shape[0], 128), 1)
    grad = taps[:, 3:4] * g
    spill = jnp.zeros((g.shape[0], 128), F32)
    product = g * raw
    products = [None, None, None, product[:, :128] + product[:, 128:]]
    for j in range(1, 4):
        masked = g * masks[3 - j]
        rolled = pltpu.roll(masked, g.shape[1] - j, 1)
        wrapped = lane >= 128 - j
        first = rolled[:, :128]
        second = jnp.where(wrapped, 0.0, rolled[:, 128:])
        outer = jnp.where(wrapped, rolled[:, 128:], 0.0)
        tap = taps[:, 3 - j : 4 - j]
        grad = grad + tap * jnp.concatenate([first, second], axis=1)
        spill = spill + tap * outer
        products[3 - j] = first * raw[:, :128] + second * raw[:, 128:] + outer * rim
    chosen = (iota((512, 128), 0) // 128 == iota((512, 128), 1)).astype(BF16)
    sums = pick_right(jnp.concatenate(products, axis=1), chosen, 2)
    moved = pltpu.roll(spill, 128 - RIM, 1)
    sides = jnp.where(lane >= 128 - RIM, grad[:, 128:], jnp.where(lane >= 96, moved, sums))
    return grad, sides


def wide_rim(rim):
    return jnp.concatenate([jnp.zeros((128 - RIM, rim.shape[1]), BF16), rim], axis=0)


def masks_of(rows_ref):
    return [rows_ref[MASK, k : k + 1, :] for k in range(4)]


def head_row(rows_ref, plane, head):
    return rows_ref[plane, pl.ds(head, 1), :]


def taps_of(w):
    padded = jnp.concatenate([w, jnp.zeros((124, BLK), F32)], axis=0)
    return jnp.transpose(padded)


def conv_all(raw_ref, rim_ref, taps, masks):
    ident = eye(BLK, BF16)
    raw = mm_nt(ident, raw_ref[...])
    rim = mm_nt(ident, wide_rim(rim_ref[...]))
    pre = conv_own(raw, taps, masks)
    pre = jnp.concatenate([pre[:, :128] + conv_rim(rim, taps, masks), pre[:, 128:]], axis=1)
    return raw, rim, pre


def with_taps(rim, taps):
    return jnp.where(iota(rim.shape, 1) < 4, taps, rim)


def sigmoid(value):
    return 1.0 / (1.0 + jnp.exp(-value))


def rim_kernel(x_ref, bc_ref, out_ref, sems):
    rows, width = x_ref.shape
    copies = [
        pltpu.make_async_copy(
            x_ref.at[pl.ds(rows - RIM, RIM), :], out_ref.at[:, pl.ds(0, width)], sems.at[0]
        ),
        pltpu.make_async_copy(
            bc_ref.at[pl.ds(rows - RIM, RIM), :],
            out_ref.at[:, pl.ds(width, bc_ref.shape[1])],
            sems.at[1],
        ),
    ]
    for copy in copies:
        copy.start()
    for copy in copies:
        copy.wait()


def head_rows_of(rows_ref, seg_ref, rate_ref, bias_ref, skip_ref, dt_ref):
    here = lax.axis_index("ctx")
    own = [seg_ref[pl.ds(2 * here + half, 1), :] for half in range(2)]
    target = jnp.concatenate(own, axis=1).astype(F32)
    before = seg_ref[pl.ds(jnp.maximum(2 * here - 1, 0), 1), :].astype(F32)
    before = jnp.where(here == 0, -1.0, before)
    lane = iota((1, 128), 1)
    masks = []
    for j in (3, 2, 1):
        rolled = pltpu.roll(target, j, 1)
        first = jnp.where(lane < j, pltpu.roll(before, j, 1), rolled[:, :128])
        shifted = jnp.concatenate([first, rolled[:, 128:]], axis=1)
        masks.append((shifted == target).astype(F32))
    rows_ref[MASK] = jnp.concatenate(
        masks + [jnp.ones((1, BLK), F32), target, jnp.zeros((11, BLK), F32)], axis=0
    )
    heads = dt_ref.shape[0]
    values = jnp.concatenate(
        [rate_ref[...], bias_ref[...], skip_ref[...], jnp.zeros((5, heads), F32)], axis=0
    )
    per_head = pick_nt(eye(heads, BF16), values, 3)
    rate = jnp.exp(per_head[:, 0:1])
    pre = dt_ref[...] + per_head[:, 1:2]
    dt = jnp.maximum(pre, 0.0) + jnp.log1p(jnp.exp(-jnp.abs(pre)))
    upto = (iota((BLK, BLK), 0) <= iota((BLK, BLK), 1)).astype(BF16)
    cumul = pick_right(-rate * dt, upto, 3)
    keep = (target == before[:, 127:]).astype(F32)
    same_end = target == target[:, BLK - 1 :]
    rows_ref[DT] = dt
    rows_ref[CUMUL] = cumul
    rows_ref[CARRY] = keep * jnp.exp(cumul)
    rows_ref[END] = jnp.exp(jnp.where(same_end, cumul[:, BLK - 1 :] - cumul, -jnp.inf))
    rows_ref[SIG] = sigmoid(pre)
    rows_ref[SKIP] = jnp.broadcast_to(per_head[:, 2:3], (heads, BLK))
    rows_ref[RATE] = jnp.broadcast_to(rate, (heads, BLK))


def state_kernel(
    x_ref, rim_ref, gy_ref, wx_ref, bc_ref, rimbc_ref, wbc_ref, seg_ref, rate_ref, bias_ref,
    skip_ref, dt_ref,
    pay_ref, rows_ref, bctok_ref,
):
    step = pl.program_id(0)
    ident = eye(BLK, BF16)

    @pl.when(step == 0)
    def _():
        head_rows_of(rows_ref, seg_ref, rate_ref, bias_ref, skip_ref, dt_ref)
        _, _, pre = conv_all(bc_ref, rimbc_ref, taps_of(wbc_ref[...]), masks_of(rows_ref))
        bctok_ref[...] = mm_nt(ident, (pre * sigmoid(pre)).astype(BF16)).astype(BF16)

    _, _, pre = conv_all(x_ref, rim_ref, taps_of(wx_ref[...]), masks_of(rows_ref))
    act = (pre * sigmoid(pre)).astype(BF16).astype(F32)
    dy = mm_nt(ident, gy_ref[...])
    ends, carries = [], []
    for k in range(PER):
        head = step * PER + k
        lo, hi = k * HD, (k + 1) * HD
        carry = head_row(rows_ref, CARRY, head)
        weight = head_row(rows_ref, END, head) * head_row(rows_ref, DT, head)
        ends.append((weight * act[lo:hi]).astype(BF16))
        carries.append((carry * dy[lo:hi]).astype(BF16))
        parts = split(carry[:, BLK - 1 :], 3)
        which = iota((8, NS), 0)
        through = jnp.where(
            which == 0, parts[0].astype(F32),
            jnp.where(which == 1, parts[1].astype(F32), parts[2].astype(F32)),
        ).astype(BF16)
        pay_ref[2 * k, 64:72, :] = through
        pay_ref[2 * k + 1, 64:72, :] = through
    state = mm(jnp.concatenate(ends, axis=0), bctok_ref[:, :NS]).astype(BF16)
    back = mm(jnp.concatenate(carries, axis=0), bctok_ref[:, NS:]).astype(BF16)
    for j in range(2 * PER):
        pay_ref[j, 0:32, :] = state[j * 32 : j * 32 + 32]
        pay_ref[j, 32:64, :] = back[j * 32 : j * 32 + 32]


def slope_kernel(
    x_ref, rim_ref, gy_ref, wx_ref, bc_ref, rimbc_ref, wbc_ref, rows_ref,
    low_ref, slope_ref, scaled_ref, sides_ref, bclow_ref, bcslope_ref, bcsides_ref,
):
    step = pl.program_id(0)
    masks = masks_of(rows_ref)

    @pl.when(step == 0)
    def _():
        taps = taps_of(wbc_ref[...])
        raw, rim, pre = conv_all(bc_ref, rimbc_ref, taps, masks)
        bcsides_ref[...] = with_taps(rim, taps)
        sig = sigmoid(pre)
        bclow_ref[0] = raw.astype(BF16)
        bclow_ref[1] = (pre * sig).astype(BF16)
        bcslope_ref[...] = sig * (1.0 + pre * (1.0 - sig))

    taps = taps_of(wx_ref[...])
    raw, rim, pre = conv_all(x_ref, rim_ref, taps, masks)
    sides_ref[...] = with_taps(rim, taps)
    sig = sigmoid(pre)
    slope_ref[...] = sig * (1.0 + pre * (1.0 - sig))
    low = (pre * sig).astype(BF16)
    dy = mm_nt(eye(BLK, BF16), gy_ref[...])
    low_ref[0] = low
    low_ref[1] = dy.astype(BF16)
    low_ref[2] = raw.astype(BF16)
    act = low.astype(F32)
    for k in range(PER):
        head = step * PER + k
        lo, hi = k * HD, (k + 1) * HD
        weight = head_row(rows_ref, END, head) * head_row(rows_ref, DT, head)
        scaled_ref[0, lo:hi, :] = (weight * act[lo:hi]).astype(BF16)
        scaled_ref[1, lo:hi, :] = (head_row(rows_ref, CARRY, head) * dy[lo:hi]).astype(BF16)


def block_kernel(
    low_ref, gy_ref, rows_ref, bctok_ref, bclow_ref, slope_ref,
    high_ref, red_ref, dbc_ref,
    scores_ref, link_ref, acol_ref, dg_ref, yt_ref, du_ref,
):
    step = pl.program_id(0)

    @pl.when(step == 0)
    def _():
        ident = eye(BLK, BF16)
        scores_ref[...] = mm_nt(bctok_ref[:, NS:], bctok_ref[:, :NS])
        seg_row = rows_ref[MASK, 4:5, :]
        seg_col = mm_nt(ident, rows_ref[MASK].astype(BF16))[:, 4:5]
        later = iota((BLK, BLK), 0) >= iota((BLK, BLK), 1)
        linked = jnp.logical_and(later, seg_col == seg_row)
        link_ref[...] = jnp.where(linked, 0.0, -jnp.inf)
        dg_ref[...] = jnp.zeros_like(dg_ref)
        cumul = pick_nt(ident, rows_ref[CUMUL], 3)
        for at in range(acol_ref.shape[0]):
            acol_ref[at] = cumul[:, at * PER : (at + 1) * PER]

    acols = acol_ref[step]
    for k in range(PER):
        head = step * PER + k
        lo, hi = k * HD, (k + 1) * HD
        arow = head_row(rows_ref, CUMUL, head)
        dt = head_row(rows_ref, DT, head)
        skip = head_row(rows_ref, SKIP, head)
        u_low = (dt * low_ref[0, lo:hi, :].astype(F32)).astype(BF16)
        du_first = None
        for tb in range(2):
            t0, t1 = tb * 128, tb * 128 + 128
            decay = jnp.exp(acols[t0:t1, k : k + 1] - arow[:, :t1] + link_ref[t0:t1, :t1])
            mixed = (decay * scores_ref[t0:t1, :t1]).astype(BF16)
            yt_ref[:, t0:t1] = mm_nt(u_low[:, :t1], mixed)
            du = mm(low_ref[1, lo:hi, t0:t1], mixed)
            if tb == 0:
                du_first = du
            else:
                du_ref[:, :128] = du_first + du[:, :128]
                du_ref[:, 128:] = du[:, 128:]
            dmix = mm(gy_ref[t0:t1, lo:hi], u_low[:, :t1])
            dg_ref[t0:t1, :t1] += decay * dmix
        x_h = low_ref[0, lo:hi, :].astype(F32)
        dy_h = low_ref[1, lo:hi, :].astype(F32)
        y_h = yt_ref[...]
        du_h = du_ref[...]
        slope = slope_ref[lo:hi, :]
        high_ref[0, lo:hi, :] = y_h + skip * x_h
        high_ref[1, lo:hi, :] = slope * (dt * du_h + skip * dy_h)
        high_ref[2, lo:hi, :] = slope * (dt * head_row(rows_ref, END, head))
        ga = jnp.sum(dy_h * y_h - u_low.astype(F32) * du_h, axis=0, keepdims=True)
        red_ref[0, pl.ds(head, 1), :] = ga
        red_ref[1, pl.ds(head, 1), :] = jnp.sum(x_h * du_h, axis=0, keepdims=True)
        red_ref[2, pl.ds(head, 1), :] = jnp.sum(x_h * dy_h, axis=0, keepdims=True)

    @pl.when(step == pl.num_programs(0) - 1)
    def _():
        dg = dg_ref[...].astype(BF16)
        dbc_ref[:NS, :] = mm(bclow_ref[1, NS:, :], dg)
        dbc_ref[NS:, :] = mm_nt(bclow_ref[1, :NS, :], dg)


def scan_kernel(in_ref, out_ref):
    peers = in_ref.shape[0]
    ahead = jnp.zeros((32, NS), F32)
    behind = jnp.zeros((32, NS), F32)

    def through(at):
        parts = in_ref[at, 64:72, :].astype(F32)
        return parts[0:1] + parts[1:2] + parts[2:3]

    for i in range(peers):
        out_ref[i, 0:32, :] = ahead.astype(BF16)
        ahead = through(i) * ahead + in_ref[i, 0:32, :].astype(F32)
        at = peers - 1 - i
        out_ref[at, 32:64, :] = behind.astype(BF16)
        behind = through(at) * behind + in_ref[at, 32:64, :].astype(F32)


def bc_kernel(
    state_ref, scaled_ref, dbc_ref, bcslope_ref, bclow_ref, bcsides_ref, rows_ref, pay_ref
):
    small = eye(NS, BF16)
    channels = scaled_ref.shape[1]
    state_in = state_ref[:, 0:32, :].reshape(channels, NS)
    state_back = state_ref[:, 32:64, :].reshape(channels, NS)
    grad_b = mm(mm_nt(small, state_back).astype(BF16), scaled_ref[0])
    grad_c = mm(mm_nt(small, state_in).astype(BF16), scaled_ref[1])
    grad_act = dbc_ref[...] + jnp.concatenate([grad_b, grad_c], axis=0)
    grad, sides = conv_back(
        grad_act * bcslope_ref[...], bclow_ref[0].astype(F32), bcsides_ref[...],
        bcsides_ref[...], [rows_ref[0, k : k + 1, :] for k in range(4)],
    )
    token = mm_nt(eye(BLK, BF16), grad.astype(BF16)).astype(BF16)
    row = iota((8, 128), 0)
    pick = (jnp.where(row < 4, row, row + 104) == iota((8, 128), 1)).astype(BF16)
    rest = mm_nt(pick, sides.astype(BF16)).astype(BF16)
    shares = pay_ref.shape[0]
    share = BLK // shares
    for j in range(shares):
        pay_ref[j, 0:share, :] = token[j * share : (j + 1) * share]
        pay_ref[j, share : share + 8, :] = rest


def x_kernel(
    state_ref, low_ref, high_ref, taps_ref, rows_ref, bctok_ref, local_ref,
    out_ref, gx_ref, sides_ref, gdt_ref, gh_ref,
    red_ref,
):
    step = pl.program_id(0)
    ident = eye(BLK, BF16)
    masks = masks_of(rows_ref)
    state_in = state_ref[:, 0:32, :].reshape(BLK, NS)
    state_back = state_ref[:, 32:64, :].reshape(BLK, NS)
    carried = mm_nt(state_in, bctok_ref[:, NS:])
    from_end = mm_nt(state_back, bctok_ref[:, :NS])
    both = state_in.astype(F32) * state_back.astype(F32)
    last_lane = iota((1, BLK), 1) == BLK - 1
    y_parts = []
    for k in range(PER):
        head = step * PER + k
        lo, hi = k * HD, (k + 1) * HD
        dt = head_row(rows_ref, DT, head)
        carry = head_row(rows_ref, CARRY, head)
        end = head_row(rows_ref, END, head)
        x_h = low_ref[0, lo:hi, :].astype(F32)
        add = carry * carried[lo:hi]
        fed = end * jnp.sum(x_h * from_end[lo:hi], axis=0, keepdims=True)
        from_step = dt * fed
        at_end = jnp.sum(from_step, axis=1, keepdims=True)
        joint = jnp.sum(jnp.sum(both[lo:hi], axis=0, keepdims=True), axis=1, keepdims=True)
        at_end = at_end + carry[:, BLK - 1 :] * joint
        ga = jnp.sum(low_ref[1, lo:hi, :].astype(F32) * add, axis=0, keepdims=True) - from_step
        red_ref[0, pl.ds(head, 1), :] = ga + jnp.where(last_lane, at_end, 0.0)
        red_ref[1, pl.ds(head, 1), :] = fed
        y_parts.append((high_ref[0, lo:hi, :] + add).astype(BF16))
    out_ref[...] = mm_nt(ident, jnp.concatenate(y_parts, axis=0)).astype(BF16)
    grad, sides = conv_back(
        high_ref[1] + high_ref[2] * from_end, low_ref[2].astype(F32),
        taps_ref[...], taps_ref[...], masks,
    )
    gx_ref[...] = mm_nt(ident, grad.astype(BF16)).astype(BF16)
    row = iota((8 + 2 * RIM, 128), 0)
    pick = (jnp.where(row < 8, row, row + 88) == iota((8 + 2 * RIM, 128), 1)).astype(BF16)
    sides_ref[...] = pick_nt(pick, sides, 2)

    @pl.when(step == pl.num_programs(0) - 1)
    def _():
        later = (iota((BLK, BLK), 0) >= iota((BLK, BLK), 1)).astype(BF16)
        grad_log = pick_right(local_ref[0] + red_ref[0], later, 3)
        rate = rows_ref[RATE]
        grad_step = (local_ref[1] + red_ref[1] - rate * grad_log) * rows_ref[SIG]
        gdt_ref[...] = grad_step
        which = iota((8, BLK), 0)
        terms = (-rate * rows_ref[DT] * grad_log, grad_step, local_ref[2])
        gh_ref[...] = jnp.zeros_like(gh_ref)
        gh_ref[:, : rate.shape[0]] = sum(
            pick_nt((which == k).astype(BF16), term, 3) for k, term in enumerate(terms)
        )


def patch_kernel(gx_ref, sides_ref, own_ref, spill_ref, out_ref, bc_ref):
    del gx_ref
    width = sides_ref.shape[1]
    spill = jnp.concatenate([jnp.zeros((RIM - 8, width), F32), spill_ref[:, :width]], axis=0)
    out_ref[...] = (sides_ref[8 + RIM :, :] + spill).astype(BF16)
    share = own_ref.shape[0]
    bc_ref[: share - 8, :] = own_ref[: share - 8, :]
    is_last = lax.axis_index("head") == lax.axis_size("head") - 1
    came = spill_ref[:, width:]
    bc_ref[share - 8 :, :] = own_ref[share - 8 :, :] + jnp.where(is_last, came, 0.0)


def pack_kernel(got_ref, sides_ref, gh_ref, sums_ref, own_ref, out_ref):
    share = own_ref.shape[0]
    total = jnp.sum(got_ref[...].astype(F32), axis=0)
    own_ref[...] = total[:share]
    width = sides_ref.shape[1]
    rest = total[share:]
    out_ref[:, :width] = sides_ref[RIM : 8 + RIM, :]
    out_ref[:, width:] = jnp.where(iota(rest.shape, 0) < 4, 0.0, rest)
    sums_ref[:, :width] = sides_ref[:4, :]
    sums_ref[:, width : width + 256] = rest[:4]
    sums_ref[:, width + 256 :] = gh_ref[:4, :]


def finish_kernel(a_ref, b_ref, c_ref, d_ref, wx_ref, wbc_ref, heads_ref):
    total = (a_ref[...] + b_ref[...]) + (c_ref[...] + d_ref[...])
    width = wx_ref.shape[1]
    wx_ref[...] = total[:4, :width]
    wbc_ref[...] = total[:4, width : width + 256]
    heads_ref[...] = total[:3, width + 256 : width + 256 + heads_ref.shape[1]]


def whole(shape):
    zeros = (0,) * len(shape)
    return pl.BlockSpec(shape, lambda *_: zeros)


def columns(rows):
    return pl.BlockSpec((rows, BLK), lambda i: (0, i))


def channel_rows(width):
    return pl.BlockSpec((BLK, width), lambda i: (i, 0))


def shaped(shape, dtype):
    return jax.ShapeDtypeStruct(shape, dtype)


def stored(shape, dtype):
    return pltpu.HBM(shape, dtype)


def from_hbm(*values):
    return [pltpu.with_memory_space_constraint(value, pltpu.HBM) for value in values]


def passed_along(value, by):
    peers = lax.axis_size("ctx")
    return lax.ppermute(value, "ctx", [(i, (i + by) % peers) for i in range(peers)])


def summed_over_ctx(value):
    peers = lax.axis_size("ctx")

    def moved(value, to):
        return lax.ppermute(value, "ctx", [(i, to(i)) for i in range(peers)])

    def turned(i, stride, by):
        at = i // stride % 4
        return i + ((at + by) % 4 - at) * stride

    def swap(i):
        return i ^ 1

    def terms(value, stride):
        near = moved(value, lambda i: turned(i, stride, 1 if i % 2 else 3))
        far = moved(value, lambda i: turned(i, stride, 2))
        return value, far, near, moved(near, swap)

    value = value + moved(value, swap)
    own, far, near, other = terms(value, 2)
    return terms((own + far) + (near + other), 8)


def cost(micros):
    return pl.CostEstimate(
        flops=int(micros * 1e8), bytes_accessed=int(micros * 3e6), transcendentals=0
    )


def local(x_raw, bc_raw, dt_raw, conv_x, conv_bc, a_log, dt_bias, skip_weight, segment, grad_y):
    rows, channels = x_raw.shape
    heads = dt_raw.shape[1]
    steps = channels // BLK
    peers = lax.axis_size("ctx")
    shares = lax.axis_size("head")
    share = rows // shares
    params = pltpu.CompilerParams(vmem_limit_bytes=VMEM)
    last_inputs = pl.pallas_call(
        rim_kernel,
        in_specs=[pl.BlockSpec(memory_space=pl.ANY)] * 2,
        out_specs=pl.BlockSpec(memory_space=pltpu.VMEM),
        out_shape=shaped((RIM, channels + 256), BF16),
        scratch_shapes=[pltpu.SemaphoreType.DMA((2,))],
        compiler_params=params,
        name="rim_rows",
    )(*from_hbm(x_raw, bc_raw))
    rim = passed_along(last_inputs, 1)
    row_spec = whole((8, heads, rows))
    square = whole((256, rows))
    by_channel = channel_rows(rows)

    def chan(dtype):
        return stored((channels, rows), dtype)

    rim_bc_spec = pl.BlockSpec((RIM, 256), lambda i: (0, channels // 256))
    local_spec = whole((3, heads, rows))

    def stack(count):
        return pl.BlockSpec((count, BLK, rows), lambda i: (0, i, 0))

    wide_spec = channel_rows(128)

    def one(shape):
        return pl.BlockSpec(shape, lambda i: (0,) * len(shape))

    pay, head_rows, bctok = pl.pallas_call(
        state_kernel,
        grid=(steps,),
        in_specs=[
            columns(rows), columns(RIM), columns(rows), columns(4),
            one((rows, 256)), rim_bc_spec, one((4, 256)),
            one(segment_rows := (segment.shape[0] // 128, 128)), one((1, heads)), one((1, heads)),
            one((1, heads)), one((heads, rows)),
        ],
        out_specs=[
            pl.BlockSpec((8, 72, NS), lambda i: (i, 0, 0)), row_spec, whole((rows, 256)),
        ],
        out_shape=[
            shaped((peers, 72, NS), BF16),
            stored((8, heads, rows), F32), stored((rows, 256), BF16),
        ],
        compiler_params=params,
        cost_estimate=cost(7),
        name="states",
    )(
        *from_hbm(x_raw), rim, *from_hbm(grad_y, conv_x, bc_raw), rim,
        *from_hbm(
            conv_bc, segment.reshape(segment_rows), a_log[None], dt_bias[None],
            skip_weight[None], dt_raw.T,
        ),
    )

    got = lax.all_to_all(pay, "ctx", 0, 0, tiled=True)

    low, slope, scaled, sides_in, bclow, bcslope, bcsides = pl.pallas_call(
        slope_kernel,
        grid=(steps,),
        in_specs=[
            columns(rows), columns(RIM), columns(rows), columns(4), whole((rows, 256)),
            rim_bc_spec, whole((4, 256)), row_spec,
        ],
        out_specs=[
            stack(3), by_channel, stack(2), wide_spec, whole((2, 256, rows)), square,
            whole((256, 128)),
        ],
        out_shape=[
            stored((3, channels, rows), BF16), chan(F32), stored((2, channels, rows), BF16),
            stored((channels, 128), F32), stored((2, 256, rows), BF16), stored((256, rows), F32),
            stored((256, 128), F32),
        ],
        compiler_params=params,
        cost_estimate=cost(6),
        name="slopes",
    )(*from_hbm(x_raw, rim, grad_y, conv_x, bc_raw, rim, conv_bc, head_rows))
    got, low = lax.optimization_barrier((got, low))

    carried = pl.pallas_call(
        scan_kernel,
        in_specs=[pl.BlockSpec(memory_space=pltpu.VMEM)],
        out_specs=pl.BlockSpec(memory_space=pltpu.VMEM),
        out_shape=shaped((peers, 64, NS), BF16),
        compiler_params=params,
        cost_estimate=cost(1),
        name="state_scan",
    )(got)
    states = lax.all_to_all(carried, "ctx", 0, 0, tiled=True)

    high, red_loc, dbc = pl.pallas_call(
        block_kernel,
        grid=(steps,),
        in_specs=[
            stack(2), columns(rows), row_spec, whole((rows, 256)), whole((2, 256, rows)),
            by_channel,
        ],
        out_specs=[stack(3), local_spec, square],
        out_shape=[
            stored((3, channels, rows), F32), stored((3, heads, rows), F32),
            stored((256, rows), F32),
        ],
        scratch_shapes=[
            pltpu.VMEM((rows, rows), F32), pltpu.VMEM((rows, rows), F32),
            pltpu.VMEM((steps, rows, PER), F32), pltpu.VMEM((rows, rows), F32),
            pltpu.VMEM((HD, rows), F32), pltpu.VMEM((HD, rows), F32),
        ],
        compiler_params=params,
        cost_estimate=cost(8),
        name="in_block",
    )(*from_hbm(low, grad_y, head_rows, bctok, bclow, slope))

    state_spec = pl.BlockSpec((8, 64, NS), lambda i: (i, 0, 0))
    pay_bc = pl.pallas_call(
        bc_kernel,
        grid=(1,),
        in_specs=[
            one((peers, 64, NS)), one((2, channels, rows)), square, square,
            one((1, 256, rows)), whole((256, 128)),
            pl.BlockSpec((1, heads, rows), lambda i: (MASK, 0, 0)),
        ],
        out_specs=whole((shares, share + 8, 256)),
        out_shape=shaped((shares, share + 8, 256), BF16),
        compiler_params=params,
        cost_estimate=cost(4),
        name="bc_part",
    )(states, *from_hbm(scaled, dbc, bcslope, bclow, bcsides, head_rows))
    got_bc = lax.all_to_all(pay_bc, "head", 0, 0, tiled=True)

    side_rows = 8 + 2 * RIM
    ssd_out, gx, sides, grad_dt, gh = pl.pallas_call(
        x_kernel,
        grid=(steps,),
        in_specs=[
            state_spec, stack(3), stack(3), wide_spec, row_spec, whole((rows, 256)), local_spec,
        ],
        out_specs=[
            columns(rows), columns(rows), columns(side_rows), whole((heads, rows)),
            whole((8, 128)),
        ],
        out_shape=[
            stored((rows, channels), BF16), stored((rows, channels), BF16),
            stored((side_rows, channels), F32), stored((heads, rows), F32),
            stored((8, 128), F32),
        ],
        scratch_shapes=[pltpu.VMEM((2, heads, rows), F32)],
        compiler_params=params,
        cost_estimate=cost(10),
        name="x_part",
    )(states, *from_hbm(low, high, sides_in, head_rows, bctok, red_loc))

    vmem = pl.BlockSpec(memory_space=pltpu.VMEM)
    width = channels + 256 + 128
    sums, own_bc, spills = pl.pallas_call(
        pack_kernel,
        in_specs=[vmem] * 3,
        out_specs=[vmem] * 3,
        out_shape=[
            shaped((4, width), F32), shaped((share, 256), F32),
            shaped((8, channels + 256), F32),
        ],
        compiler_params=params,
        cost_estimate=cost(1),
        name="pack_sums",
    )(got_bc, *from_hbm(sides, gh))
    parts = summed_over_ctx(sums)
    spills = passed_along(spills, -1)
    grad_x, grad_bc = pl.pallas_call(
        patch_kernel,
        grid=(1,),
        in_specs=[
            pl.BlockSpec(memory_space=pl.ANY), whole((side_rows, channels)), whole((share, 256)),
            whole((8, channels + 256)),
        ],
        out_specs=[
            pl.BlockSpec((RIM, channels), lambda i: (rows // RIM - 1, 0)), whole((share, 256)),
        ],
        out_shape=[stored((rows, channels), BF16), stored((share, 256), F32)],
        input_output_aliases={0: 0},
        compiler_params=params,
        cost_estimate=cost(1),
        name="last_rows",
    )(*from_hbm(gx, sides), own_bc, spills)
    grad_wx, grad_wbc, grad_heads = pl.pallas_call(
        finish_kernel,
        in_specs=[vmem] * 4,
        out_specs=[vmem] * 3,
        out_shape=[stored((4, channels), F32), stored((4, 256), F32), stored((3, heads), F32)],
        compiler_params=params,
        cost_estimate=cost(1),
        name="finish_sums",
    )(*parts)
    return ssd_out, grad_x, grad_bc, grad_dt.T, grad_wx, grad_wbc, grad_heads


def solution(mesh):
    in_specs = (
        P("ctx", "head"), P("ctx", None), P("ctx", "head"), P(None, "head"), P(),
        P("head"), P("head"), P("head"), P(), P("ctx", "head"),
    )
    out_specs = (
        P("ctx", "head"), P("ctx", "head"), P(("ctx", "head"), None), P("ctx", "head"),
        P(None, "head"), P(), P(None, "head"),
    )
    return jax.shard_map(local, mesh=mesh, in_specs=in_specs, out_specs=out_specs, check_vma=False)
```
